128 devices in a mesh: mem: 32 (over z_lo, y, x), gx: 2 (over core), gy: 2 (over z_hi).
Axes of the slice: x: 4, y: 4, z: 4 (z_hi: 2, z_lo: 2; z = z_hi * 2 + z_lo), core: 2. Of those that a mesh axis runs over, the one named last changes fastest.
Arguments:
- fields: float32 [128, 3, 256, 256], P('mem', None, 'gx', 'gy'), may hold values from -3 to 3
- noise: float32 [64, 256, 256], P('mem', 'gx', 'gy'), may hold values from -6 to 6
- ancestors: int32 [2, 2, 64], P('gx', 'gy'), may hold values from 0 to 63
- obs_cells: int32 [2, 2, 256], P('gx', 'gy'), may hold values from 0 to 16383
- obs_values: float32 [2, 2, 256], P('gx', 'gy'), may hold values from -3 to 12
Outputs:
- resampled: float32 [128, 3, 256, 256], P('mem', None, 'gx', 'gy')
- log_weights: float32 [2, 2, 128], P('gx', 'gy', 'mem')
The draws below stay inside these ranges and needn't reach their ends.
All inputs are finite; a program needn't handle non-finite values.
Results may differ from the reference program's by a relative error of at most 0.00012.
Values sent between devices are 32-bit elements; how exact they have to be, the bound alone decides.
No kernel may reach another device: no remote copies, remote signals or barrier semaphores. Data moves between devices by JAX's collectives and lax.ppermute only.
A program may use at most 128 MiB of HBM per device.

```python
import math
import jax
import jax.numpy as jnp
import numpy as np

CX = 128
CY = 128
OBS = 256
MEMBERS = 128
PAIRS = 64
NX = 256
NY = 256
N_GX = 2
N_GY = 2


def draw_fields(key, part):
    key_vals = jax.random.fold_in(key, 21)
    key_order = jax.random.fold_in(key, 22)
    tiles = N_GX * N_GY
    base = jax.random.normal(key_vals, (MEMBERS, 3, NX, NY), jnp.float32)
    table = jnp.array([0.25, 0.5, 0.8, 1.2], jnp.float32)
    order = jax.random.permutation(key_order, jnp.arange(tiles, dtype=jnp.int32) % 4)
    tile_scale = jnp.take(table, order).reshape(N_GX, N_GY)
    cell_scale = jnp.repeat(jnp.repeat(tile_scale, CX, axis=0), CY, axis=1)
    return jnp.clip(base * cell_scale[None, None, :, :], -3.0, 3.0).astype(jnp.float32)


def draw_obs_values(key, part):
    key_base = jax.random.fold_in(key, 11)
    key_order = jax.random.fold_in(key, 12)
    tiles = N_GX * N_GY
    base = jnp.clip(0.3 * jax.random.normal(key_base, (N_GX, N_GY, OBS), jnp.float32), -1.2, 1.2)
    table = jnp.array([0.0, 300.0, 600.0, 1200.0], jnp.float32)
    order = jax.random.permutation(key_order, jnp.arange(tiles, dtype=jnp.int32) % 4)
    strength = jnp.take(table, order).reshape(N_GX, N_GY, 1)
    offset = jnp.sqrt(strength / (2.0 * OBS))
    return (base + offset).astype(jnp.float32)


def plant(values, stream_key, low, top_value):
    longest = values.shape.index(max(values.shape))
    spots = []
    for shift in (0, 1):
        where = [jax.random.randint(jax.random.fold_in(stream_key, axis), (), 0, length) for axis, length in enumerate(values.shape)]
        where[longest] = (where[longest] + shift) % values.shape[longest]
        spots.append(tuple(where))
    return values.at[spots[0]].set(low).at[spots[1]].set(top_value)


def steps_of(stream_key, dims, cuts, low, top_value):
    factor_of = 1.0
    for dim, parts in cuts:
        draws = jax.random.uniform(jax.random.fold_in(jax.random.fold_in(stream_key, 6), dim), (parts,), jnp.float32, low / len(cuts), top_value / len(cuts))
        factor_of = factor_of * jnp.repeat(jnp.exp(draws), dims[dim] // parts).reshape((-1,) + (1,) * (len(dims) - 1 - dim))
    return factor_of


def rank_bounds(count, slope):
    weights = [(1 << 20) // math.isqrt(standing ** slope) + 1 for standing in range(1, count + 1)]
    scale = 1 + sum(weights) // (1 << 30)
    return np.cumsum(np.array([max(1, weight // scale) for weight in weights]))


def ranked_ids(rng, shape, count, skew):
    table = rank_bounds(count, skew)
    lot = jax.random.randint(jax.random.fold_in(rng, 1), shape, 0, int(table[count - 1]))
    standing = jnp.searchsorted(jnp.asarray(table, jnp.int32), lot, side="right")
    return jax.random.permutation(jax.random.fold_in(rng, 2), count)[standing].astype(jnp.int32)


def gaussian(stream_key, dims, width, limit, split=(), held_as=jnp.bfloat16):
    drawn = jax.random.normal(stream_key, dims, jnp.float32) * width
    if len(split) > 0:
        drawn = steps_of(stream_key, dims, split, -0.22, 0.18) * drawn
    return jnp.clip(drawn, min=-limit, max=limit).astype(held_as)


def setup_inputs(seed: int = 0) -> dict:
    keys = jax.random.split(jax.random.key(seed), 6)
    return {
        "fields": draw_fields(jax.random.fold_in(keys[5], 71), 0),
        "noise": gaussian(keys[1], (PAIRS, NX, NY), 1.0, 6.0, ((0, 32), (1, 2), (2, 2)), jnp.float32),
        "ancestors": plant(ranked_ids(keys[2], (N_GX, N_GY, PAIRS), PAIRS, 2), jax.random.fold_in(keys[2], 3), 0, PAIRS - 1).astype(jnp.int32),
        "obs_cells": plant(jax.random.randint(keys[3], (N_GX, N_GY, OBS), 0, CX * CY), jax.random.fold_in(keys[3], 1), 0, (CX * CY) - 1).astype(jnp.int32),
        "obs_values": draw_obs_values(jax.random.fold_in(keys[5], 71), 0),
    }


COURANT = 0.3
DIFFUSE = 0.05
HYPER = 0.005
NOISE_AMP = 0.1
OBS_VAR = 0.25


def xdiff(a):
    return (jnp.roll(a, -1, -2) - jnp.roll(a, 1, -2)) * 0.5


def ydiff(a):
    return (jnp.roll(a, -1, -1) - jnp.roll(a, 1, -1)) * 0.5


def laplace(a):
    return jnp.roll(a, -1, -2) + jnp.roll(a, 1, -2) + jnp.roll(a, -1, -1) + jnp.roll(a, 1, -1) - 4.0 * a


def smooth(a):
    return DIFFUSE * laplace(a) - HYPER * laplace(laplace(a))


def advance(eta, speed_x, speed_y, force, coriolis):
    depth = 1.0 + eta
    tend_h = xdiff(depth * speed_x) + ydiff(depth * speed_y)
    tend_u = speed_x * xdiff(speed_x) + speed_y * ydiff(speed_x) + xdiff(eta) - coriolis * speed_y
    tend_v = speed_x * xdiff(speed_y) + speed_y * ydiff(speed_y) + ydiff(eta) + coriolis * speed_x
    new_eta = eta - COURANT * tend_h + smooth(eta) + NOISE_AMP * force
    new_u = speed_x - COURANT * tend_u + smooth(speed_x)
    new_v = speed_y - COURANT * tend_v + smooth(speed_y)
    return new_eta, new_u, new_v


def reference(fields, noise, ancestors, obs_cells, obs_values):
    rows_y = jnp.arange(NY, dtype=jnp.int32).astype(jnp.float32)
    coriolis = 0.1 + 0.2 * ((rows_y + 0.5) / NY - 0.5)
    force = jnp.repeat(noise, 2, axis=0)
    eta, speed_x, speed_y = fields[:, 0], fields[:, 1], fields[:, 2]
    for step in range(2):
        eta, speed_x, speed_y = advance(eta, speed_x, speed_y, force, coriolis)
    state = jnp.stack([eta, speed_x, speed_y], axis=1)
    tiles = eta.reshape(MEMBERS, N_GX, CX, N_GY, CY).transpose(1, 3, 0, 2, 4).reshape(N_GX, N_GY, MEMBERS, CX * CY)
    values = jnp.take_along_axis(tiles, obs_cells[:, :, None, :].astype(jnp.int32), axis=3)
    misfit = values - obs_values[:, :, None, :]
    logw = -0.5 * jnp.sum(misfit * misfit, axis=3) / OBS_VAR
    peak = jnp.max(logw, axis=2, keepdims=True)
    expo = jnp.exp(logw - peak)
    log_weights = logw - peak - jnp.log(jnp.sum(expo, axis=2, keepdims=True))
    blocks = state.reshape(MEMBERS, 3, N_GX, CX, N_GY, CY).transpose(2, 4, 0, 1, 3, 5)
    slots = jnp.arange(MEMBERS, dtype=jnp.int32)
    source = 2 * jnp.take(ancestors, slots // 2, axis=2) + slots % 2
    picked = jnp.take_along_axis(blocks, source[:, :, :, None, None, None].astype(jnp.int32), axis=2)
    resampled = picked.transpose(2, 3, 0, 4, 1, 5).reshape(MEMBERS, 3, NX, NY)
    return resampled, log_weights
```

```python
import functools

import jax
import jax.numpy as jnp
from jax import lax
from jax.experimental import pallas as pl
from jax.experimental.pallas import tpu as pltpu
from jax.sharding import PartitionSpec as P

COURANT = 0.3
NOISE_AMP = 0.1
OBS_VAR = 0.25
T = 128
F32 = jnp.float32
CHUNK = 16


def lanes(shape):
    return lax.broadcasted_iota(jnp.int32, shape, len(shape) - 1)


def subl(shape):
    return lax.broadcasted_iota(jnp.int32, shape, len(shape) - 2)


def lroll(a, shift):
    return pltpu.roll(a, shift % T, 1)


def rows_at(ref, lead, start, off, count, total):
    first = start + off
    if first < 0:
        return pltpu.roll(ref[(*lead, pl.ds(0, count))], -first, 0)
    if first + count > total:
        over = first + count - total
        return pltpu.roll(ref[(*lead, pl.ds(total - count, count))], count - over, 0)
    return ref[(*lead, pl.ds(first, count))]


def one_step(ref, lead, start, count, total, force, cor):
    get = lambda f, off: rows_at(ref, (*lead, f), start, off, count, total)
    cen, low, high = [], [], []
    dx, dy, loc, q = [], [], [], []
    for f in range(3):
        a, am, ap = get(f, 0), get(f, -1), get(f, 1)
        far = get(f, -2) + get(f, 2)
        cross = am + ap
        yp, ym = lroll(a, -1), lroll(a, 1)
        cen.append(a)
        low.append(am)
        high.append(ap)
        dx.append(ap - am)
        dy.append(yp - ym)
        loc.append(0.71 * a + (0.09 * cross - 0.005 * far))
        q.append(0.09 * a - (0.01 * cross + 0.005 * (yp + ym)))
    eta, u, v = cen
    half = 0.5 * COURANT
    hv = half * ((1.0 + eta) * v)
    hu = (1.0 + high[0]) * high[1] - (1.0 + low[0]) * low[1]
    new_eta = loc[0] + lroll(q[0] - hv, -1) + lroll(q[0] + hv, 1) - half * hu + NOISE_AMP * force
    tend_u = u * dx[1] + v * dy[1] + dx[0]
    tend_v = u * dx[2] + v * dy[2] + dy[0]
    new_u = loc[1] + (lroll(q[1], -1) + lroll(q[1], 1)) - half * tend_u + (COURANT * cor) * v
    new_v = loc[2] + (lroll(q[2], -1) + lroll(q[2], 1)) - half * tend_v - (COURANT * cor) * u
    return new_eta, new_u, new_v


def coriolis(cols, total_y):
    y = lax.rem(lax.axis_index("gy") * T + cols + total_y, total_y)
    return 0.1 + 0.2 * ((y.astype(F32) + 0.5) / total_y - 0.5)


def pack_kernel(fields, noise, rowpack, colpack, cornpack):
    members = fields.shape[0]
    top = subl((8, T)) < 4
    for m in range(members):
        for f in range(3):
            rowpack[3 * m + f] = jnp.where(top, fields[m, f, 0:8], fields[m, f, T - 8 : T])
    for p in range(members // 2):
        rowpack[3 * members + p] = jnp.where(top, noise[p, 0:8], noise[p, T - 8 : T])
    for t in range(0, T, CHUNK):
        ln = lanes((CHUNK, T)) // 8
        acc = jnp.zeros((CHUNK, T), F32)
        for m in range(members):
            for f in range(4):
                src = fields[m, f, t : t + CHUNK] if f < 3 else noise[m // 2, t : t + CHUNK]
                acc = jnp.where(ln == 4 * m + f, lroll(src, 32 * m + 8 * f + 4), acc)
        colpack[t : t + CHUNK] = acc
    cornpack[...] = jnp.where(top, colpack[0:8], colpack[T - 8 : T])


def own_columns(tiles):
    shape = tiles[0].shape
    ln = lanes(shape) // 8
    acc = jnp.zeros(shape, F32)
    for m, a in enumerate(tiles):
        acc = jnp.where(ln == 4 * m, lroll(a, 32 * m + 8), acc)
        acc = jnp.where(ln == 4 * m + 3, lroll(a, 32 * m + 24), acc)
    return acc


def interior_kernel(total_y, fields, noise, inner, ownrow, owncol, tmp):
    members = fields.shape[0]
    cor = coriolis(lanes((1, T)), total_y)

    def body(m, carry):
        for r in range(0, T, CHUNK):
            new = one_step(fields, (m,), r, CHUNK, T, noise[m // 2, pl.ds(r, CHUNK)], cor)
            for f in range(3):
                tmp[f, pl.ds(r, CHUNK)] = new[f]
        for r in range(0, T, CHUNK):
            new = one_step(tmp, (), r, CHUNK, T, noise[m // 2, pl.ds(r, CHUNK)], cor)
            for f in range(3):
                inner[m, f, pl.ds(r, CHUNK)] = new[f]
        return carry

    lax.fori_loop(0, members, body, 0)
    for m in range(members):
        for f in range(4):
            src = fields.at[m, f] if f < 3 else noise.at[m // 2]
            ownrow[f, 2 * m] = src[0:8]
            ownrow[f, 2 * m + 1] = src[T - 8 : T]
    for f in range(4):
        for t in range(0, T, CHUNK):
            tiles = []
            for m in range(members):
                src = fields.at[m, f] if f < 3 else noise.at[m // 2]
                tiles.append(src[t : t + CHUNK])
            owncol[f, t : t + CHUNK] = own_columns(tiles)


def merge_kernel(total_y, inner, ownrow, owncol, rowrecv, colrecv, cornrecv, cells, values,
                 out, logw, rs, rs1, cs, cs1, eta_s):
    members = inner.shape[0]
    tall = T + 16
    l32 = lax.rem(lanes((1, T)), 32)
    cor_row = coriolis(lanes((1, T)), total_y)
    cor_col = coriolis(jnp.where(l32 < 16, l32 + 120, l32 - 24), total_y)
    is_low = (l32 >= 20) & (l32 < 24)
    is_high = (l32 >= 8) & (l32 < 12)

    for f in range(4):
        for m in range(members):
            halo = rowrecv[3 * m + f] if f < 3 else rowrecv[3 * members + m // 2]
            rs[f, 32 * m : 32 * m + 8] = halo
            rs[f, 32 * m + 8 : 32 * m + 16] = ownrow[f, 2 * m]
            rs[f, 32 * m + 16 : 32 * m + 24] = ownrow[f, 2 * m + 1]
            rs[f, 32 * m + 24 : 32 * m + 32] = halo
        with_halo = lambda own, recv: jnp.where(
            is_low, lroll(recv, 20 - 8 * f), jnp.where(is_high, lroll(recv, 4 - 8 * f), own)
        )
        tiles = [rowrecv[3 * m + f] if f < 3 else rowrecv[3 * members + m // 2] for m in range(members)]
        ends = with_halo(own_columns(tiles), cornrecv[...])
        cs[f, 0:8] = ends
        cs[f, T + 8 : T + 16] = ends
        for t in range(0, T, CHUNK):
            cs[f, t + 8 : t + 8 + CHUNK] = with_halo(owncol[f, t : t + CHUNK], colrecv[t : t + CHUNK])

    def twice(a, a1, total, cor):
        for src, dst in ((a, a1), (a1, a)):
            for r in range(0, total, CHUNK):
                new = one_step(src, (), r, CHUNK, total, a[3, r : r + CHUNK], cor)
                for f in range(3):
                    dst[f, r : r + CHUNK] = new[f]

    twice(rs, rs1, T, cor_row)
    twice(cs, cs1, tall, cor_col)

    top = subl((8, T)) < 4
    left = lanes((8, T)) < 4
    right = lanes((8, T)) >= T - 4
    for m in range(members):
        p, mm = m // 2, m % 2
        for f in range(3):
            for t in range(T // 8):
                a = inner[m, f, 8 * t : 8 * t + 8]
                if t == 0:
                    a = jnp.where(top, rs[f, 32 * m + 8 : 32 * m + 16], a)
                if t == T // 8 - 1:
                    a = jnp.where(top, a, rs[f, 32 * m + 16 : 32 * m + 24])
                col = cs[f, 8 * t + 8 : 8 * t + 16]
                a = jnp.where(left, lroll(col, 104 - 32 * m), a)
                a = jnp.where(right, lroll(col, 120 - 32 * m), a)
                k = mm * 48 + f * 16 + t
                per = 96 // out.shape[0]
                out[k // per, p, 8 * (k % per) : 8 * (k % per) + 8] = a
                if f == 0:
                    eta_s[m * T + 8 * t : m * T + 8 * t + 8] = a

    count = cells.shape[1]
    cell = cells[...]
    pick_y = (lax.broadcasted_iota(jnp.int32, (T, count), 0) == lax.rem(cell, T)).astype(F32)
    pick_x = lax.broadcasted_iota(jnp.int32, (T, count), 0) == cell // T
    for m in range(members):
        seen = jnp.dot(eta_s[m * T : (m + 1) * T], pick_y, precision=lax.Precision.HIGHEST,
                       preferred_element_type=F32)
        seen = jnp.sum(jnp.where(pick_x, seen, 0.0), axis=0, keepdims=True)
        miss = seen - values[...]
        total = jnp.sum(miss * miss, axis=1, keepdims=True)
        logw[m : m + 1] = jnp.broadcast_to(-0.5 * total / OBS_VAR, (1, T))


def select_kernel(lineage, recv, out):
    def body(k, carry):
        out[k] = recv[lineage[k]]
        return carry

    lax.fori_loop(0, recv.shape[0], body, 0, unroll=8)


VM = pl.BlockSpec(memory_space=pltpu.VMEM)
SM = pl.BlockSpec(memory_space=pltpu.SMEM)
PARAMS = pltpu.CompilerParams(vmem_limit_bytes=24 << 20)


def sds(*shape):
    return jax.ShapeDtypeStruct(shape, F32)


def shards(fields, noise, ancestors, obs_cells, obs_values):
    members = fields.shape[0]
    devices = lax.axis_size("mem")
    total_y = T * lax.axis_size("gy")
    rowpack, colpack, cornpack = pl.pallas_call(
        pack_kernel,
        out_shape=(sds(3 * members + members // 2, 8, T), sds(T, T), sds(8, T)),
        in_specs=[VM] * 2,
        out_specs=[VM] * 3,
        compiler_params=PARAMS,
        name="pack",
    )(fields, noise)
    swap = [(0, 1), (1, 0)]
    colrecv = lax.ppermute(colpack, "gy", swap)
    cornrecv = lax.ppermute(cornpack, ("gx", "gy"), [(0, 3), (1, 2), (2, 1), (3, 0)])
    rowrecv = lax.ppermute(rowpack, "gx", swap)
    inner, ownrow, owncol = pl.pallas_call(
        functools.partial(interior_kernel, total_y),
        out_shape=(sds(members, 3, T, T), sds(4, 2 * members, 8, T), sds(4, T, T)),
        in_specs=[VM] * 2,
        out_specs=[VM] * 3,
        scratch_shapes=[pltpu.VMEM((3, T, T), F32)],
        compiler_params=PARAMS,
        cost_estimate=pl.CostEstimate(flops=50_000_000, bytes_accessed=2_500_000, transcendentals=0),
        name="interior",
    )(fields, noise)
    rows = members // 2 * 96 // devices * 4
    pieces, logw = pl.pallas_call(
        functools.partial(merge_kernel, total_y),
        out_shape=(sds(devices, members // 2, 768 // devices, T), sds(members, T)),
        in_specs=[VM] * 8,
        out_specs=[VM] * 2,
        scratch_shapes=[
            pltpu.VMEM((4, T, T), F32),
            pltpu.VMEM((3, T, T), F32),
            pltpu.VMEM((4, T + 16, T), F32),
            pltpu.VMEM((3, T + 16, T), F32),
            pltpu.VMEM((members * T, T), F32),
        ],
        compiler_params=PARAMS,
        name="merge",
    )(inner, ownrow, owncol, rowrecv, colrecv, cornrecv, obs_cells.reshape(1, -1), obs_values.reshape(1, -1))
    held = lax.all_to_all(pieces, "mem", 0, 0)
    logw = logw[:, 0]
    logw_all = lax.all_gather(logw, "mem")
    picked = pl.pallas_call(
        select_kernel,
        out_shape=sds(devices * members // 2, 768 // devices, T),
        in_specs=[SM, VM],
        out_specs=VM,
        compiler_params=PARAMS,
        name="select",
    )(ancestors.reshape(-1), held.reshape(devices * members // 2, 768 // devices, T))
    back = lax.all_to_all(picked.reshape(held.shape), "mem", 0, 0)
    resampled = back.transpose(1, 0, 2, 3).reshape(fields.shape)
    peak = jnp.max(logw_all)
    total = jnp.sum(jnp.exp(logw_all - peak))
    log_weights = (logw - peak - jnp.log(total)).reshape(1, 1, members)
    return (resampled, log_weights)


def solution(mesh):
    return jax.shard_map(
        shards,
        mesh=mesh,
        in_specs=(
            P("mem", None, "gx", "gy"),
            P("mem", "gx", "gy"),
            P("gx", "gy", None),
            P("gx", "gy", None),
            P("gx", "gy", None),
        ),
        out_specs=(P("mem", None, "gx", "gy"), P("gx", "gy", "mem")),
        check_vma=False,
    )
```

```python
import functools

import jax
import jax.numpy as jnp
from jax import lax
from jax.experimental import pallas as pl
from jax.experimental.pallas import tpu as pltpu
from jax.sharding import PartitionSpec as P

COURANT = 0.3
NOISE_AMP = 0.1
OBS_VAR = 0.25
T = 128
F32 = jnp.float32
CHUNK = 16


def lanes(shape):
    return lax.broadcasted_iota(jnp.int32, shape, len(shape) - 1)


def subl(shape):
    return lax.broadcasted_iota(jnp.int32, shape, len(shape) - 2)


def lroll(a, shift):
    return pltpu.roll(a, shift % T, 1)


def rows_at(ref, lead, start, off, count, total):
    first = start + off
    if first < 0:
        return pltpu.roll(ref[(*lead, pl.ds(0, count))], -first, 0)
    if first + count > total:
        over = first + count - total
        return pltpu.roll(ref[(*lead, pl.ds(total - count, count))], count - over, 0)
    return ref[(*lead, pl.ds(first, count))]


def one_step(ref, lead, start, count, total, force, cor):
    get = lambda f, off: rows_at(ref, (*lead, f), start, off, count, total)
    cen, low, high = [], [], []
    dx, dy, loc, q = [], [], [], []
    for f in range(3):
        a, am, ap = get(f, 0), get(f, -1), get(f, 1)
        far = get(f, -2) + get(f, 2)
        cross = am + ap
        yp, ym = lroll(a, -1), lroll(a, 1)
        cen.append(a)
        low.append(am)
        high.append(ap)
        dx.append(ap - am)
        dy.append(yp - ym)
        loc.append(0.71 * a + (0.09 * cross - 0.005 * far))
        q.append(0.09 * a - (0.01 * cross + 0.005 * (yp + ym)))
    eta, u, v = cen
    half = 0.5 * COURANT
    hv = half * ((1.0 + eta) * v)
    hu = (1.0 + high[0]) * high[1] - (1.0 + low[0]) * low[1]
    new_eta = loc[0] + lroll(q[0] - hv, -1) + lroll(q[0] + hv, 1) - half * hu + NOISE_AMP * force
    tend_u = u * dx[1] + v * dy[1] + dx[0]
    tend_v = u * dx[2] + v * dy[2] + dy[0]
    new_u = loc[1] + (lroll(q[1], -1) + lroll(q[1], 1)) - half * tend_u + (COURANT * cor) * v
    new_v = loc[2] + (lroll(q[2], -1) + lroll(q[2], 1)) - half * tend_v - (COURANT * cor) * u
    return new_eta, new_u, new_v


def coriolis(cols, total_y):
    y = lax.rem(lax.axis_index("gy") * T + cols + total_y, total_y)
    return 0.1 + 0.2 * ((y.astype(F32) + 0.5) / total_y - 0.5)


def pack_kernel(fields, noise, rowpack, colpack, cornpack):
    members = fields.shape[0]
    top = subl((8, T)) < 4
    for m in range(members):
        for f in range(3):
            rowpack[3 * m + f] = jnp.where(top, fields[m, f, 0:8], fields[m, f, T - 8 : T])
    for p in range(members // 2):
        rowpack[3 * members + p] = jnp.where(top, noise[p, 0:8], noise[p, T - 8 : T])
    for t in range(0, T, CHUNK):
        ln = lanes((CHUNK, T)) // 8
        acc = jnp.zeros((CHUNK, T), F32)
        for m in range(members):
            for f in range(4):
                src = fields[m, f, t : t + CHUNK] if f < 3 else noise[m // 2, t : t + CHUNK]
                acc = jnp.where(ln == 4 * m + f, lroll(src, 32 * m + 8 * f + 4), acc)
        colpack[t : t + CHUNK] = acc
    cornpack[...] = jnp.where(top, colpack[0:8], colpack[T - 8 : T])


def own_columns(tiles):
    shape = tiles[0].shape
    ln = lanes(shape) // 8
    acc = jnp.zeros(shape, F32)
    for m, a in enumerate(tiles):
        acc = jnp.where(ln == 4 * m, lroll(a, 32 * m + 8), acc)
        acc = jnp.where(ln == 4 * m + 3, lroll(a, 32 * m + 24), acc)
    return acc


def interior_kernel(total_y, fields, noise, inner, ownrow, owncol, tmp):
    members = fields.shape[0]
    cor = coriolis(lanes((1, T)), total_y)

    def body(m, carry):
        for r in range(0, T, CHUNK):
            new = one_step(fields, (m,), r, CHUNK, T, noise[m // 2, pl.ds(r, CHUNK)], cor)
            for f in range(3):
                tmp[f, pl.ds(r, CHUNK)] = new[f]
        for r in range(0, T, CHUNK):
            new = one_step(tmp, (), r, CHUNK, T, noise[m // 2, pl.ds(r, CHUNK)], cor)
            for f in range(3):
                inner[m, f, pl.ds(r, CHUNK)] = new[f]
        return carry

    lax.fori_loop(0, members, body, 0)
    for m in range(members):
        for f in range(4):
            src = fields.at[m, f] if f < 3 else noise.at[m // 2]
            ownrow[f, 2 * m] = src[0:8]
            ownrow[f, 2 * m + 1] = src[T - 8 : T]
    for f in range(4):
        for t in range(0, T, CHUNK):
            tiles = []
            for m in range(members):
                src = fields.at[m, f] if f < 3 else noise.at[m // 2]
                tiles.append(src[t : t + CHUNK])
            owncol[f, t : t + CHUNK] = own_columns(tiles)


def merge_kernel(total_y, devices, inner, ownrow, owncol, rowrecv, colrecv, cornrecv, cells, values,
                 out, rs, rs1, cs, cs1, eta_s):
    members = inner.shape[0]
    tall = T + 16
    l32 = lax.rem(lanes((1, T)), 32)
    cor_row = coriolis(lanes((1, T)), total_y)
    cor_col = coriolis(jnp.where(l32 < 16, l32 + 120, l32 - 24), total_y)
    is_low = (l32 >= 20) & (l32 < 24)
    is_high = (l32 >= 8) & (l32 < 12)

    for f in range(4):
        for m in range(members):
            halo = rowrecv[3 * m + f] if f < 3 else rowrecv[3 * members + m // 2]
            rs[f, 32 * m : 32 * m + 8] = halo
            rs[f, 32 * m + 8 : 32 * m + 16] = ownrow[f, 2 * m]
            rs[f, 32 * m + 16 : 32 * m + 24] = ownrow[f, 2 * m + 1]
            rs[f, 32 * m + 24 : 32 * m + 32] = halo
        with_halo = lambda own, recv: jnp.where(
            is_low, lroll(recv, 20 - 8 * f), jnp.where(is_high, lroll(recv, 4 - 8 * f), own)
        )
        tiles = [rowrecv[3 * m + f] if f < 3 else rowrecv[3 * members + m // 2] for m in range(members)]
        ends = with_halo(own_columns(tiles), cornrecv[...])
        cs[f, 0:8] = ends
        cs[f, T + 8 : T + 16] = ends
        for t in range(0, T, CHUNK):
            cs[f, t + 8 : t + 8 + CHUNK] = with_halo(owncol[f, t : t + CHUNK], colrecv[t : t + CHUNK])

    def twice(a, a1, total, cor):
        for src, dst in ((a, a1), (a1, a)):
            for r in range(0, total, CHUNK):
                new = one_step(src, (), r, CHUNK, total, a[3, r : r + CHUNK], cor)
                for f in range(3):
                    dst[f, r : r + CHUNK] = new[f]

    twice(rs, rs1, T, cor_row)
    twice(cs, cs1, tall, cor_col)

    per = 96 // devices
    stride = members // 2 * 8 * per + 1
    top = subl((8, T)) < 4
    left = lanes((8, T)) < 4
    right = lanes((8, T)) >= T - 4
    for m in range(members):
        p, mm = m // 2, m % 2
        for f in range(3):
            for t in range(T // 8):
                a = inner[m, f, 8 * t : 8 * t + 8]
                if t == 0:
                    a = jnp.where(top, rs[f, 32 * m + 8 : 32 * m + 16], a)
                if t == T // 8 - 1:
                    a = jnp.where(top, a, rs[f, 32 * m + 16 : 32 * m + 24])
                col = cs[f, 8 * t + 8 : 8 * t + 16]
                a = jnp.where(left, lroll(col, 104 - 32 * m), a)
                a = jnp.where(right, lroll(col, 120 - 32 * m), a)
                k = mm * 48 + f * 16 + t
                first = (k // per) * stride + p * 8 * per + 8 * (k % per)
                out[first : first + 8] = a
                if f == 0:
                    eta_s[m * T + 8 * t : m * T + 8 * t + 8] = a

    count = cells.shape[1]
    cell = cells[...]
    pick_y = (lax.broadcasted_iota(jnp.int32, (T, count), 0) == lax.rem(cell, T)).astype(F32)
    pick_x = lax.broadcasted_iota(jnp.int32, (T, count), 0) == cell // T
    logw = jnp.zeros((1, T), F32)
    for m in range(members):
        seen = jnp.dot(eta_s[m * T : (m + 1) * T], pick_y, precision=lax.Precision.HIGHEST,
                       preferred_element_type=F32)
        seen = jnp.sum(jnp.where(pick_x, seen, 0.0), axis=0, keepdims=True)
        miss = seen - values[...]
        total = jnp.sum(miss * miss, axis=1, keepdims=True)
        logw = jnp.where(lanes((1, T)) == m, -0.5 * total / OBS_VAR, logw)
    for j in range(devices):
        out[(j + 1) * stride - 1 : (j + 1) * stride] = logw


def select_kernel(members, devices, lineage, recv, out, log_weights):
    pairs, rows = members // 2 * devices, out.shape[1]
    stride = members // 2 * rows + 1

    def body(k, carry):
        pair = lineage[k]
        first = lax.div(pair, members // 2) * stride + lax.rem(pair, members // 2) * rows
        out[k] = recv[pl.ds(first, rows)]
        return carry

    lax.fori_loop(0, pairs, body, 0, unroll=8)
    logw = recv[pl.ds(stride - 1, devices, stride)]
    logw = jnp.where(lanes(logw.shape) < members, logw, -jnp.inf)
    peak = jnp.max(jnp.max(logw, axis=1, keepdims=True), axis=0, keepdims=True)
    total = jnp.sum(jnp.sum(jnp.exp(logw - peak), axis=1, keepdims=True), axis=0, keepdims=True)
    own = recv[pl.ds(lax.axis_index("mem") * stride + stride - 1, 1)]
    log_weights[0] = (own - peak - jnp.log(total))[:, :members]


VM = pl.BlockSpec(memory_space=pltpu.VMEM)
SM = pl.BlockSpec(memory_space=pltpu.SMEM)
PARAMS = pltpu.CompilerParams(vmem_limit_bytes=24 << 20)


def sds(*shape):
    return jax.ShapeDtypeStruct(shape, F32)


def shards(fields, noise, ancestors, obs_cells, obs_values):
    members = fields.shape[0]
    devices = lax.axis_size("mem")
    total_y = T * lax.axis_size("gy")
    rowpack, colpack, cornpack = pl.pallas_call(
        pack_kernel,
        out_shape=(sds(3 * members + members // 2, 8, T), sds(T, T), sds(8, T)),
        in_specs=[VM] * 2,
        out_specs=[VM] * 3,
        compiler_params=PARAMS,
        name="pack",
    )(fields, noise)
    swap = [(0, 1), (1, 0)]
    colrecv = lax.ppermute(colpack, "gy", swap)
    cornrecv = lax.ppermute(cornpack, ("gx", "gy"), [(0, 3), (1, 2), (2, 1), (3, 0)])
    rowrecv = lax.ppermute(rowpack, "gx", swap)
    inner, ownrow, owncol = pl.pallas_call(
        functools.partial(interior_kernel, total_y),
        out_shape=(sds(members, 3, T, T), sds(4, 2 * members, 8, T), sds(4, T, T)),
        in_specs=[VM] * 2,
        out_specs=[VM] * 3,
        scratch_shapes=[pltpu.VMEM((3, T, T), F32)],
        compiler_params=PARAMS,
        cost_estimate=pl.CostEstimate(flops=50_000_000, bytes_accessed=2_500_000, transcendentals=0),
        name="interior",
    )(fields, noise)
    rows = 768 // devices
    stride = members // 2 * rows + 1
    pieces = pl.pallas_call(
        functools.partial(merge_kernel, total_y, devices),
        out_shape=sds(devices * stride, T),
        in_specs=[VM] * 8,
        out_specs=VM,
        scratch_shapes=[
            pltpu.VMEM((4, T, T), F32),
            pltpu.VMEM((3, T, T), F32),
            pltpu.VMEM((4, T + 16, T), F32),
            pltpu.VMEM((3, T + 16, T), F32),
            pltpu.VMEM((members * T, T), F32),
        ],
        compiler_params=PARAMS,
        name="merge",
    )(inner, ownrow, owncol, rowrecv, colrecv, cornrecv, obs_cells.reshape(1, -1), obs_values.reshape(1, -1))
    held = lax.all_to_all(pieces.reshape(devices, stride, 1, T), "mem", 0, 0).reshape(devices * stride, T)
    picked, log_weights = pl.pallas_call(
        functools.partial(select_kernel, members, devices),
        out_shape=(sds(devices * members // 2, rows, T), sds(1, 1, members)),
        in_specs=[SM, VM],
        out_specs=[VM] * 2,
        compiler_params=PARAMS,
        name="select",
    )(ancestors.reshape(-1), held)
    back = lax.all_to_all(picked.reshape(devices, members // 2, rows, T), "mem", 0, 0)
    resampled = back.transpose(1, 0, 2, 3).reshape(fields.shape)
    return (resampled, log_weights)


def solution(mesh):
    return jax.shard_map(
        shards,
        mesh=mesh,
        in_specs=(
            P("mem", None, "gx", "gy"),
            P("mem", "gx", "gy"),
            P("gx", "gy", None),
            P("gx", "gy", None),
            P("gx", "gy", None),
        ),
        out_specs=(P("mem", None, "gx", "gy"), P("gx", "gy", "mem")),
        check_vma=False,
    )
```

```python
import functools

import jax
import jax.numpy as jnp
from jax import lax
from jax.experimental import pallas as pl
from jax.experimental.pallas import tpu as pltpu
from jax.sharding import PartitionSpec as P

COURANT = 0.3
NOISE_AMP = 0.1
OBS_VAR = 0.25
T = 128
F32 = jnp.float32
CHUNK = 64


def lanes(shape):
    return lax.broadcasted_iota(jnp.int32, shape, len(shape) - 1)


def subl(shape):
    return lax.broadcasted_iota(jnp.int32, shape, len(shape) - 2)


def lroll(a, shift):
    return pltpu.roll(a, shift % T, 1)


def rows_at(ref, lead, start, off, count, total):
    first = start + off
    if first < 0:
        return pltpu.roll(ref[(*lead, pl.ds(0, count))], -first, 0)
    if first + count > total:
        over = first + count - total
        return pltpu.roll(ref[(*lead, pl.ds(total - count, count))], count - over, 0)
    return ref[(*lead, pl.ds(first, count))]


def one_step(ref, lead, start, count, total, force, cor):
    get = lambda f, off: rows_at(ref, (*lead, f), start, off, count, total)
    cen, low, high = [], [], []
    dx, dy, loc, q = [], [], [], []
    for f in range(3):
        a, am, ap = get(f, 0), get(f, -1), get(f, 1)
        far = get(f, -2) + get(f, 2)
        cross = am + ap
        yp, ym = lroll(a, -1), lroll(a, 1)
        cen.append(a)
        low.append(am)
        high.append(ap)
        dx.append(ap - am)
        dy.append(yp - ym)
        loc.append(0.71 * a + (0.09 * cross - 0.005 * far))
        q.append(0.09 * a - (0.01 * cross + 0.005 * (yp + ym)))
    eta, u, v = cen
    half = 0.5 * COURANT
    hv = half * ((1.0 + eta) * v)
    hu = (1.0 + high[0]) * high[1] - (1.0 + low[0]) * low[1]
    new_eta = loc[0] + lroll(q[0] - hv, -1) + lroll(q[0] + hv, 1) - half * hu + NOISE_AMP * force
    tend_u = u * dx[1] + v * dy[1] + dx[0]
    tend_v = u * dx[2] + v * dy[2] + dy[0]
    new_u = loc[1] + (lroll(q[1], -1) + lroll(q[1], 1)) - half * tend_u + (COURANT * cor) * v
    new_v = loc[2] + (lroll(q[2], -1) + lroll(q[2], 1)) - half * tend_v - (COURANT * cor) * u
    return new_eta, new_u, new_v


def coriolis(cols, total_y):
    y = lax.rem(lax.axis_index("gy") * T + cols + total_y, total_y)
    return 0.1 + 0.2 * ((y.astype(F32) + 0.5) / total_y - 0.5)


def pack_kernel(fields_hbm, noise_hbm, fields, noise, rowpack, colpack, cornpack, sems):
    members = fields.shape[0]
    copies = [pltpu.make_async_copy(noise_hbm, noise, sems.at[members])]
    for m in range(members):
        copies.append(pltpu.make_async_copy(fields_hbm.at[m], fields.at[m], sems.at[m]))
    for copy in copies:
        copy.start()
    copies[0].wait()
    top = subl((8, T)) < 4
    ln = lanes((T, T)) // 8
    for p in range(members // 2):
        rowpack[3 * members + p] = jnp.where(top, noise[p, 0:8], noise[p, T - 8 : T])
    acc = jnp.zeros((T, T), F32)
    for m in range(members):
        acc = jnp.where(ln == 4 * m + 3, lroll(noise[m // 2], 32 * m + 28), acc)
    for m in range(members):
        copies[1 + m].wait()
        for f in range(3):
            rowpack[3 * m + f] = jnp.where(top, fields[m, f, 0:8], fields[m, f, T - 8 : T])
            acc = jnp.where(ln == 4 * m + f, lroll(fields[m, f], 32 * m + 8 * f + 4), acc)
    colpack[...] = acc
    cornpack[...] = jnp.where(top, acc[0:8], acc[T - 8 : T])


def own_columns(tiles):
    shape = tiles[0].shape
    ln = lanes(shape) // 8
    acc = jnp.zeros(shape, F32)
    for m, a in enumerate(tiles):
        acc = jnp.where(ln == 4 * m, lroll(a, 32 * m + 8), acc)
        acc = jnp.where(ln == 4 * m + 3, lroll(a, 32 * m + 24), acc)
    return acc


def interior_kernel(total_y, fields, noise, cells_hbm, values_hbm, inner, ownrow, owncol, pick_y, cell_x,
                    values, tmp, cells, sems):
    members = fields.shape[0]
    copies = [
        pltpu.make_async_copy(cells_hbm, cells, sems.at[0]),
        pltpu.make_async_copy(values_hbm, values, sems.at[1]),
    ]
    for copy in copies:
        copy.start()
    cor = coriolis(lanes((1, T)), total_y)
    for src, dst in ((fields, tmp), (tmp, inner)):
        for m in range(members):
            for r in range(0, T, CHUNK):
                new = one_step(src, (m,), r, CHUNK, T, noise[m // 2, r : r + CHUNK], cor)
                for f in range(3):
                    dst[m, f, r : r + CHUNK] = new[f]
    for m in range(members):
        for f in range(4):
            src = fields.at[m, f] if f < 3 else noise.at[m // 2]
            ownrow[f, 2 * m] = src[0:8]
            ownrow[f, 2 * m + 1] = src[T - 8 : T]
    for f in range(4):
        tiles = []
        for m in range(members):
            src = fields.at[m, f] if f < 3 else noise.at[m // 2]
            tiles.append(src[...])
        owncol[f] = own_columns(tiles)
    for copy in copies:
        copy.wait()
    cell = cells[...]
    line_y = lax.broadcasted_iota(jnp.int32, pick_y.shape, 0)
    pick_y[...] = jnp.where(line_y == lax.rem(cell, T), 1.0, 0.0).astype(pick_y.dtype)
    cell_x[...] = cell // T


def merge_kernel(total_y, devices, inner, ownrow, owncol, rowrecv, colrecv, cornrecv, pick_y, cell_x,
                 values, out, rs, rs1, cs, cs1, eta_s):
    members = inner.shape[0]
    tall = T + 16
    l32 = lax.rem(lanes((1, T)), 32)
    cor_row = coriolis(lanes((1, T)), total_y)
    cor_col = coriolis(jnp.where(l32 < 16, l32 + 120, l32 - 24), total_y)
    is_low = (l32 >= 20) & (l32 < 24)
    is_high = (l32 >= 8) & (l32 < 12)

    for f in range(4):
        for m in range(members):
            halo = rowrecv[3 * m + f] if f < 3 else rowrecv[3 * members + m // 2]
            rs[f, 32 * m : 32 * m + 8] = halo
            rs[f, 32 * m + 8 : 32 * m + 16] = ownrow[f, 2 * m]
            rs[f, 32 * m + 16 : 32 * m + 24] = ownrow[f, 2 * m + 1]
            rs[f, 32 * m + 24 : 32 * m + 32] = halo
        with_halo = lambda own, recv: jnp.where(
            is_low, lroll(recv, 20 - 8 * f), jnp.where(is_high, lroll(recv, 4 - 8 * f), own)
        )
        tiles = [rowrecv[3 * m + f] if f < 3 else rowrecv[3 * members + m // 2] for m in range(members)]
        ends = with_halo(own_columns(tiles), cornrecv[...])
        cs[f, 0:8] = ends
        cs[f, T + 8 : T + 16] = ends
        cs[f, 8 : T + 8] = with_halo(owncol[f], colrecv[...])

    def twice(a, a1, total, cor):
        chunk = total // 2
        for src, dst in ((a, a1), (a1, a)):
            for r in range(0, total, chunk):
                new = one_step(src, (), r, chunk, total, a[3, r : r + chunk], cor)
                for f in range(3):
                    dst[f, r : r + chunk] = new[f]

    twice(rs, rs1, T, cor_row)
    twice(cs, cs1, tall, cor_col)

    per = 96 // devices
    stride = members // 2 * 8 * per + 1
    top = subl((8, T)) < 4
    left = lanes((8, T)) < 4
    right = lanes((8, T)) >= T - 4
    for m in range(members):
        p, mm = m // 2, m % 2
        for f in range(3):
            for t in range(T // 8):
                a = inner[m, f, 8 * t : 8 * t + 8]
                if t == 0:
                    a = jnp.where(top, rs[f, 32 * m + 8 : 32 * m + 16], a)
                if t == T // 8 - 1:
                    a = jnp.where(top, a, rs[f, 32 * m + 16 : 32 * m + 24])
                col = cs[f, 8 * t + 8 : 8 * t + 16]
                a = jnp.where(left, lroll(col, 104 - 32 * m), a)
                a = jnp.where(right, lroll(col, 120 - 32 * m), a)
                k = mm * 48 + f * 16 + t
                first = (k // per) * stride + p * 8 * per + 8 * (k % per)
                out[first : first + 8] = a
                if f == 0:
                    eta_s[m * T + 8 * t : m * T + 8 * t + 8] = a

    eta = eta_s[...]
    hi = eta.astype(jnp.bfloat16)
    rest = eta - hi.astype(F32)
    mid = rest.astype(jnp.bfloat16)
    low = (rest - mid.astype(F32)).astype(jnp.bfloat16)
    dot = lambda part: jnp.dot(part, pick_y[...], preferred_element_type=F32)
    seen = dot(hi) + (dot(mid) + dot(low))
    pick_x = lax.broadcasted_iota(jnp.int32, pick_y.shape, 0) == cell_x[...]
    logw = jnp.zeros((1, T), F32)
    for m in range(members):
        at = jnp.sum(jnp.where(pick_x, seen[m * T : (m + 1) * T], 0.0), axis=0, keepdims=True)
        miss = at - values[...]
        total = jnp.sum(miss * miss, axis=1, keepdims=True)
        logw = jnp.where(lanes((1, T)) == m, -0.5 * total / OBS_VAR, logw)
    for j in range(devices):
        out[(j + 1) * stride - 1 : (j + 1) * stride] = logw


def select_kernel(members, devices, lineage_hbm, recv, out, log_weights, lineage, sem):
    copy = pltpu.make_async_copy(lineage_hbm, lineage, sem)
    copy.start()
    pairs, rows = members // 2 * devices, out.shape[1]
    stride = members // 2 * rows + 1
    logw = recv[pl.ds(stride - 1, devices, stride)]
    logw = jnp.where(lanes(logw.shape) < members, logw, -jnp.inf)
    peak = jnp.max(jnp.max(logw, axis=1, keepdims=True), axis=0, keepdims=True)
    total = jnp.sum(jnp.sum(jnp.exp(logw - peak), axis=1, keepdims=True), axis=0, keepdims=True)
    own = recv[pl.ds(lax.axis_index("mem") * stride + stride - 1, 1)]
    log_weights[0] = (own - peak - jnp.log(total))[:, :members]
    copy.wait()

    def body(k, carry):
        pair = lineage[0, k]
        first = lax.div(pair, members // 2) * stride + lax.rem(pair, members // 2) * rows
        out[k] = recv[pl.ds(first, rows)]
        return carry

    lax.fori_loop(0, pairs, body, 0, unroll=8)


VM = pl.BlockSpec(memory_space=pltpu.VMEM)
HB = pl.BlockSpec(memory_space=pltpu.MemorySpace.HBM)
PARAMS = pltpu.CompilerParams(vmem_limit_bytes=24 << 20)


def in_hbm(a):
    return pltpu.with_memory_space_constraint(a, pltpu.MemorySpace.HBM)


def sds(*shape):
    return jax.ShapeDtypeStruct(shape, F32)


def shards(fields, noise, ancestors, obs_cells, obs_values):
    members = fields.shape[0]
    devices = lax.axis_size("mem")
    total_y = T * lax.axis_size("gy")
    fields_vm, noise_vm, rowpack, colpack, cornpack = pl.pallas_call(
        pack_kernel,
        out_shape=(
            sds(*fields.shape),
            sds(*noise.shape),
            sds(3 * members + members // 2, 8, T),
            sds(T, T),
            sds(8, T),
        ),
        in_specs=[HB] * 2,
        out_specs=[VM] * 5,
        scratch_shapes=[pltpu.SemaphoreType.DMA((members + 1,))],
        compiler_params=PARAMS,
        name="pack",
    )(in_hbm(fields), in_hbm(noise))
    swap = [(0, 1), (1, 0)]
    colrecv = lax.ppermute(colpack, "gy", swap)
    cornrecv = lax.ppermute(cornpack, ("gx", "gy"), [(0, 3), (1, 2), (2, 1), (3, 0)])
    rowrecv = lax.ppermute(rowpack, "gx", swap)
    count = obs_cells.shape[-1]
    inner, ownrow, owncol, pick_y, cell_x, values = pl.pallas_call(
        functools.partial(interior_kernel, total_y),
        out_shape=(
            sds(members, 3, T, T),
            sds(4, 2 * members, 8, T),
            sds(4, T, T),
            jax.ShapeDtypeStruct((T, count), jnp.bfloat16),
            jax.ShapeDtypeStruct((1, count), jnp.int32),
            sds(1, count),
        ),
        in_specs=[VM] * 2 + [HB] * 2,
        out_specs=[VM] * 6,
        scratch_shapes=[
            pltpu.VMEM((members, 3, T, T), F32),
            pltpu.VMEM((1, count), jnp.int32),
            pltpu.SemaphoreType.DMA((2,)),
        ],
        compiler_params=PARAMS,
        cost_estimate=pl.CostEstimate(flops=50_000_000, bytes_accessed=2_500_000, transcendentals=0),
        name="interior",
    )(fields_vm, noise_vm, in_hbm(obs_cells.reshape(1, -1)), in_hbm(obs_values.reshape(1, -1)))
    rows = 768 // devices
    stride = members // 2 * rows + 1
    pieces = pl.pallas_call(
        functools.partial(merge_kernel, total_y, devices),
        out_shape=sds(devices * stride, T),
        in_specs=[VM] * 9,
        out_specs=VM,
        scratch_shapes=[
            pltpu.VMEM((4, T, T), F32),
            pltpu.VMEM((3, T, T), F32),
            pltpu.VMEM((4, T + 16, T), F32),
            pltpu.VMEM((3, T + 16, T), F32),
            pltpu.VMEM((members * T, T), F32),
        ],
        compiler_params=PARAMS,
        name="merge",
    )(inner, ownrow, owncol, rowrecv, colrecv, cornrecv, pick_y, cell_x, values)
    held = lax.all_to_all(pieces.reshape(devices, stride, 1, T), "mem", 0, 0).reshape(devices * stride, T)
    picked, log_weights = pl.pallas_call(
        functools.partial(select_kernel, members, devices),
        out_shape=(sds(devices * members // 2, rows, T), sds(1, 1, members)),
        in_specs=[HB, VM],
        out_specs=[VM] * 2,
        scratch_shapes=[pltpu.SMEM((1, devices * members // 2), jnp.int32), pltpu.SemaphoreType.DMA],
        compiler_params=PARAMS,
        name="select",
    )(in_hbm(ancestors.reshape(1, -1)), held)
    back = lax.all_to_all(picked.reshape(devices, members // 2, rows, T), "mem", 0, 0)
    resampled = back.transpose(1, 0, 2, 3).reshape(fields.shape)
    return (resampled, log_weights)


def solution(mesh):
    return jax.shard_map(
        shards,
        mesh=mesh,
        in_specs=(
            P("mem", None, "gx", "gy"),
            P("mem", "gx", "gy"),
            P("gx", "gy", None),
            P("gx", "gy", None),
            P("gx", "gy", None),
        ),
        out_specs=(P("mem", None, "gx", "gy"), P("gx", "gy", "mem")),
        check_vma=False,
    )
```

```python
import functools

import jax
import jax.numpy as jnp
from jax import lax
from jax.experimental import pallas as pl
from jax.experimental.pallas import tpu as pltpu
from jax.sharding import PartitionSpec as P

COURANT = 0.3
NOISE_AMP = 0.1
OBS_VAR = 0.25
T = 128
F32 = jnp.float32
CHUNK = 64


def lanes(shape):
    return lax.broadcasted_iota(jnp.int32, shape, len(shape) - 1)


def subl(shape):
    return lax.broadcasted_iota(jnp.int32, shape, len(shape) - 2)


def lroll(a, shift):
    return pltpu.roll(a, shift % T, 1)


def rows_at(ref, lead, start, off, count, total):
    first = start + off
    if first < 0:
        return pltpu.roll(ref[(*lead, pl.ds(0, count))], -first, 0)
    if first + count > total:
        over = first + count - total
        return pltpu.roll(ref[(*lead, pl.ds(total - count, count))], count - over, 0)
    return ref[(*lead, pl.ds(first, count))]


def one_step(ref, lead, start, count, total, force, cor):
    get = lambda f, off: rows_at(ref, (*lead, f), start, off, count, total)
    cen, low, high = [], [], []
    dx, dy, loc, q = [], [], [], []
    for f in range(3):
        a, am, ap = get(f, 0), get(f, -1), get(f, 1)
        far = get(f, -2) + get(f, 2)
        cross = am + ap
        yp, ym = lroll(a, -1), lroll(a, 1)
        cen.append(a)
        low.append(am)
        high.append(ap)
        dx.append(ap - am)
        dy.append(yp - ym)
        loc.append(0.71 * a + (0.09 * cross - 0.005 * far))
        q.append(0.09 * a - (0.01 * cross + 0.005 * (yp + ym)))
    eta, u, v = cen
    half = 0.5 * COURANT
    hv = half * ((1.0 + eta) * v)
    hu = (1.0 + high[0]) * high[1] - (1.0 + low[0]) * low[1]
    new_eta = loc[0] + lroll(q[0] - hv, -1) + lroll(q[0] + hv, 1) - half * hu + NOISE_AMP * force
    tend_u = u * dx[1] + v * dy[1] + dx[0]
    tend_v = u * dx[2] + v * dy[2] + dy[0]
    new_u = loc[1] + (lroll(q[1], -1) + lroll(q[1], 1)) - half * tend_u + (COURANT * cor) * v
    new_v = loc[2] + (lroll(q[2], -1) + lroll(q[2], 1)) - half * tend_v - (COURANT * cor) * u
    return new_eta, new_u, new_v


def coriolis(cols, total_y):
    y = lax.rem(lax.axis_index("gy") * T + cols + total_y, total_y)
    return 0.1 + 0.2 * ((y.astype(F32) + 0.5) / total_y - 0.5)


def pack_kernel(fields_hbm, noise_hbm, fields, noise, rowpack, colpack, cornpack, allpack, sems):
    members = fields.shape[0]
    copies = [pltpu.make_async_copy(noise_hbm, noise, sems.at[members])]
    for m in range(members):
        copies.append(pltpu.make_async_copy(fields_hbm.at[m], fields.at[m], sems.at[m]))
    for copy in copies:
        copy.start()
    copies[0].wait()
    top = subl((8, T)) < 4
    ln = lanes((T, T)) // 8
    for p in range(members // 2):
        rowpack[3 * members + p] = jnp.where(top, noise[p, 0:8], noise[p, T - 8 : T])
    acc = jnp.zeros((T, T), F32)
    for m in range(members):
        acc = jnp.where(ln == 4 * m + 3, lroll(noise[m // 2], 32 * m + 28), acc)
    for m in range(members):
        copies[1 + m].wait()
        for f in range(3):
            rowpack[3 * m + f] = jnp.where(top, fields[m, f, 0:8], fields[m, f, T - 8 : T])
            acc = jnp.where(ln == 4 * m + f, lroll(fields[m, f], 32 * m + 8 * f + 4), acc)
    corn = jnp.where(top, acc[0:8], acc[T - 8 : T])
    colpack[...] = acc
    cornpack[...] = corn
    allpack[0:8] = corn
    allpack[8 : T + 8] = acc


def own_columns(tiles):
    shape = tiles[0].shape
    ln = lanes(shape) // 8
    acc = jnp.zeros(shape, F32)
    for m, a in enumerate(tiles):
        acc = jnp.where(ln == 4 * m, lroll(a, 32 * m + 8), acc)
        acc = jnp.where(ln == 4 * m + 3, lroll(a, 32 * m + 24), acc)
    return acc


def interior_kernel(total_y, fields, noise, cells_hbm, values_hbm, inner, ownrow, owncol, pick_y, cell_x,
                    values, tmp, cells, sems):
    members = fields.shape[0]
    copies = [
        pltpu.make_async_copy(cells_hbm, cells, sems.at[0]),
        pltpu.make_async_copy(values_hbm, values, sems.at[1]),
    ]
    for copy in copies:
        copy.start()
    cor = coriolis(lanes((1, T)), total_y)
    for src, dst in ((fields, tmp), (tmp, inner)):
        for m in range(members):
            for r in range(0, T, CHUNK):
                new = one_step(src, (m,), r, CHUNK, T, noise[m // 2, r : r + CHUNK], cor)
                for f in range(3):
                    dst[m, f, r : r + CHUNK] = new[f]
    for m in range(members):
        for f in range(4):
            src = fields.at[m, f] if f < 3 else noise.at[m // 2]
            ownrow[f, 2 * m] = src[0:8]
            ownrow[f, 2 * m + 1] = src[T - 8 : T]
    for f in range(4):
        tiles = []
        for m in range(members):
            src = fields.at[m, f] if f < 3 else noise.at[m // 2]
            tiles.append(src[...])
        owncol[f] = own_columns(tiles)
    for copy in copies:
        copy.wait()
    cell = cells[...]
    line_y = lax.broadcasted_iota(jnp.int32, pick_y.shape, 0)
    pick_y[...] = jnp.where(line_y == lax.rem(cell, T), 1.0, 0.0).astype(pick_y.dtype)
    cell_x[...] = cell // T


def merge_kernel(total_y, devices, inner, ownrow, owncol, rowrecv, col_down, col_up, corn_down, corn_up,
                 pick_y, cell_x, values, out, rs, rs1, cs, cs1, eta_s):
    members = inner.shape[0]
    tall = T + 16
    l32 = lax.rem(lanes((1, T)), 32)
    cor_row = coriolis(lanes((1, T)), total_y)
    cor_col = coriolis(jnp.where(l32 < 16, l32 + 120, l32 - 24), total_y)
    is_low = (l32 >= 20) & (l32 < 24)
    is_high = (l32 >= 8) & (l32 < 12)

    colrecv = col_down[8 : T + 8] + col_up[...]
    cornrecv = corn_down[0:8] + corn_up[...]
    for f in range(4):
        for m in range(members):
            halo = rowrecv[3 * m + f] if f < 3 else rowrecv[3 * members + m // 2]
            rs[f, 32 * m : 32 * m + 8] = halo
            rs[f, 32 * m + 8 : 32 * m + 16] = ownrow[f, 2 * m]
            rs[f, 32 * m + 16 : 32 * m + 24] = ownrow[f, 2 * m + 1]
            rs[f, 32 * m + 24 : 32 * m + 32] = halo
        with_halo = lambda own, recv: jnp.where(
            is_low, lroll(recv, 20 - 8 * f), jnp.where(is_high, lroll(recv, 4 - 8 * f), own)
        )
        tiles = [rowrecv[3 * m + f] if f < 3 else rowrecv[3 * members + m // 2] for m in range(members)]
        ends = with_halo(own_columns(tiles), cornrecv)
        cs[f, 0:8] = ends
        cs[f, T + 8 : T + 16] = ends
        cs[f, 8 : T + 8] = with_halo(owncol[f], colrecv)

    def twice(a, a1, total, cor):
        chunk = total // 2
        for src, dst in ((a, a1), (a1, a)):
            for r in range(0, total, chunk):
                new = one_step(src, (), r, chunk, total, a[3, r : r + chunk], cor)
                for f in range(3):
                    dst[f, r : r + chunk] = new[f]

    twice(rs, rs1, T, cor_row)
    twice(cs, cs1, tall, cor_col)

    per = 96 // devices
    stride = members // 2 * 8 * per + 1
    top = subl((8, T)) < 4
    left = lanes((8, T)) < 4
    right = lanes((8, T)) >= T - 4
    for m in range(members):
        p, mm = m // 2, m % 2
        for f in range(3):
            for t in range(T // 8):
                a = inner[m, f, 8 * t : 8 * t + 8]
                if t == 0:
                    a = jnp.where(top, rs[f, 32 * m + 8 : 32 * m + 16], a)
                if t == T // 8 - 1:
                    a = jnp.where(top, a, rs[f, 32 * m + 16 : 32 * m + 24])
                col = cs[f, 8 * t + 8 : 8 * t + 16]
                a = jnp.where(left, lroll(col, 104 - 32 * m), a)
                a = jnp.where(right, lroll(col, 120 - 32 * m), a)
                k = mm * 48 + f * 16 + t
                first = (k // per) * stride + p * 8 * per + 8 * (k % per)
                out[first : first + 8] = a
                if f == 0:
                    eta_s[m * T + 8 * t : m * T + 8 * t + 8] = a

    eta = eta_s[...]
    hi = eta.astype(jnp.bfloat16)
    rest = eta - hi.astype(F32)
    mid = rest.astype(jnp.bfloat16)
    low = (rest - mid.astype(F32)).astype(jnp.bfloat16)
    dot = lambda part: jnp.dot(part, pick_y[...], preferred_element_type=F32)
    seen = dot(hi) + (dot(mid) + dot(low))
    pick_x = lax.broadcasted_iota(jnp.int32, pick_y.shape, 0) == cell_x[...]
    logw = jnp.zeros((1, T), F32)
    for m in range(members):
        at = jnp.sum(jnp.where(pick_x, seen[m * T : (m + 1) * T], 0.0), axis=0, keepdims=True)
        miss = at - values[...]
        total = jnp.sum(miss * miss, axis=1, keepdims=True)
        logw = jnp.where(lanes((1, T)) == m, -0.5 * total / OBS_VAR, logw)
    for j in range(devices):
        out[(j + 1) * stride - 1 : (j + 1) * stride] = logw


def select_kernel(members, devices, lineage_hbm, recv, out, log_weights, lineage, sem):
    copy = pltpu.make_async_copy(lineage_hbm, lineage, sem)
    copy.start()
    pairs, rows = members // 2 * devices, out.shape[1]
    stride = members // 2 * rows + 1
    logw = recv[pl.ds(stride - 1, devices, stride)]
    logw = jnp.where(lanes(logw.shape) < members, logw, -jnp.inf)
    peak = jnp.max(jnp.max(logw, axis=1, keepdims=True), axis=0, keepdims=True)
    total = jnp.sum(jnp.sum(jnp.exp(logw - peak), axis=1, keepdims=True), axis=0, keepdims=True)
    own = recv[pl.ds(lax.axis_index("mem") * stride + stride - 1, 1)]
    log_weights[0] = (own - peak - jnp.log(total))[:, :members]
    copy.wait()

    def body(k, carry):
        pair = lineage[0, k]
        first = lax.div(pair, members // 2) * stride + lax.rem(pair, members // 2) * rows
        out[k] = recv[pl.ds(first, rows)]
        return carry

    lax.fori_loop(0, pairs, body, 0, unroll=8)


VM = pl.BlockSpec(memory_space=pltpu.VMEM)
HB = pl.BlockSpec(memory_space=pltpu.MemorySpace.HBM)
PARAMS = pltpu.CompilerParams(vmem_limit_bytes=24 << 20)


def in_hbm(a):
    return pltpu.with_memory_space_constraint(a, pltpu.MemorySpace.HBM)


def sds(*shape):
    return jax.ShapeDtypeStruct(shape, F32)


def shards(fields, noise, ancestors, obs_cells, obs_values):
    members = fields.shape[0]
    devices = lax.axis_size("mem")
    total_y = T * lax.axis_size("gy")
    fields_vm, noise_vm, rowpack, colpack, cornpack, allpack = pl.pallas_call(
        pack_kernel,
        out_shape=(
            sds(*fields.shape),
            sds(*noise.shape),
            sds(3 * members + members // 2, 8, T),
            sds(T, T),
            sds(8, T),
            sds(T + 8, T),
        ),
        in_specs=[HB] * 2,
        out_specs=[VM] * 6,
        scratch_shapes=[pltpu.SemaphoreType.DMA((members + 1,))],
        compiler_params=PARAMS,
        name="pack",
    )(in_hbm(fields), in_hbm(noise))
    grid = ("gx", "gy")
    col_down = lax.ppermute(allpack, "gy", [(1, 0)])
    corn_down = lax.ppermute(allpack, grid, [(1, 2), (3, 0)])
    rowrecv = lax.ppermute(rowpack, "gx", [(0, 1), (1, 0)])
    col_up = lax.ppermute(colpack, "gy", [(0, 1)])
    corn_up = lax.ppermute(cornpack, grid, [(2, 1), (0, 3)])
    count = obs_cells.shape[-1]
    inner, ownrow, owncol, pick_y, cell_x, values = pl.pallas_call(
        functools.partial(interior_kernel, total_y),
        out_shape=(
            sds(members, 3, T, T),
            sds(4, 2 * members, 8, T),
            sds(4, T, T),
            jax.ShapeDtypeStruct((T, count), jnp.bfloat16),
            jax.ShapeDtypeStruct((1, count), jnp.int32),
            sds(1, count),
        ),
        in_specs=[VM] * 2 + [HB] * 2,
        out_specs=[VM] * 6,
        scratch_shapes=[
            pltpu.VMEM((members, 3, T, T), F32),
            pltpu.VMEM((1, count), jnp.int32),
            pltpu.SemaphoreType.DMA((2,)),
        ],
        compiler_params=PARAMS,
        cost_estimate=pl.CostEstimate(flops=50_000_000, bytes_accessed=2_500_000, transcendentals=0),
        name="interior",
    )(fields_vm, noise_vm, in_hbm(obs_cells.reshape(1, -1)), in_hbm(obs_values.reshape(1, -1)))
    rows = 768 // devices
    stride = members // 2 * rows + 1
    pieces = pl.pallas_call(
        functools.partial(merge_kernel, total_y, devices),
        out_shape=sds(devices * stride, T),
        in_specs=[VM] * 11,
        out_specs=VM,
        scratch_shapes=[
            pltpu.VMEM((4, T, T), F32),
            pltpu.VMEM((3, T, T), F32),
            pltpu.VMEM((4, T + 16, T), F32),
            pltpu.VMEM((3, T + 16, T), F32),
            pltpu.VMEM((members * T, T), F32),
        ],
        compiler_params=PARAMS,
        name="merge",
    )(inner, ownrow, owncol, rowrecv, col_down, col_up, corn_down, corn_up, pick_y, cell_x, values)
    held = lax.all_to_all(pieces.reshape(devices, stride, 1, T), "mem", 0, 0).reshape(devices * stride, T)
    picked, log_weights = pl.pallas_call(
        functools.partial(select_kernel, members, devices),
        out_shape=(sds(devices * members // 2, rows, T), sds(1, 1, members)),
        in_specs=[HB, VM],
        out_specs=[VM] * 2,
        scratch_shapes=[pltpu.SMEM((1, devices * members // 2), jnp.int32), pltpu.SemaphoreType.DMA],
        compiler_params=PARAMS,
        name="select",
    )(in_hbm(ancestors.reshape(1, -1)), held)
    back = lax.all_to_all(picked.reshape(devices, members // 2, rows, T), "mem", 0, 0)
    resampled = back.transpose(1, 0, 2, 3).reshape(fields.shape)
    return (resampled, log_weights)


def solution(mesh):
    return jax.shard_map(
        shards,
        mesh=mesh,
        in_specs=(
            P("mem", None, "gx", "gy"),
            P("mem", "gx", "gy"),
            P("gx", "gy", None),
            P("gx", "gy", None),
            P("gx", "gy", None),
        ),
        out_specs=(P("mem", None, "gx", "gy"), P("gx", "gy", "mem")),
        check_vma=False,
    )
```

```python
import functools

import jax
import jax.numpy as jnp
from jax import lax
from jax.experimental import pallas as pl
from jax.experimental.pallas import tpu as pltpu
from jax.sharding import PartitionSpec as P

COURANT = 0.3
NOISE_AMP = 0.1
OBS_VAR = 0.25
T = 128
F32 = jnp.float32
CHUNK = 64


def lanes(shape):
    return lax.broadcasted_iota(jnp.int32, shape, len(shape) - 1)


def subl(shape):
    return lax.broadcasted_iota(jnp.int32, shape, len(shape) - 2)


def lroll(a, shift):
    return pltpu.roll(a, shift % T, 1)


def rows_at(ref, lead, start, off, count, total):
    first = start + off
    if first < 0:
        return pltpu.roll(ref[(*lead, pl.ds(0, count))], -first, 0)
    if first + count > total:
        over = first + count - total
        return pltpu.roll(ref[(*lead, pl.ds(total - count, count))], count - over, 0)
    return ref[(*lead, pl.ds(first, count))]


def one_step(ref, lead, start, count, total, force, cor):
    get = lambda f, off: rows_at(ref, (*lead, f), start, off, count, total)
    cen, low, high = [], [], []
    dx, dy, loc, q = [], [], [], []
    for f in range(3):
        a, am, ap = get(f, 0), get(f, -1), get(f, 1)
        far = get(f, -2) + get(f, 2)
        cross = am + ap
        yp, ym = lroll(a, -1), lroll(a, 1)
        cen.append(a)
        low.append(am)
        high.append(ap)
        dx.append(ap - am)
        dy.append(yp - ym)
        loc.append(0.71 * a + (0.09 * cross - 0.005 * far))
        q.append(0.09 * a - (0.01 * cross + 0.005 * (yp + ym)))
    eta, u, v = cen
    half = 0.5 * COURANT
    hv = half * ((1.0 + eta) * v)
    hu = (1.0 + high[0]) * high[1] - (1.0 + low[0]) * low[1]
    new_eta = loc[0] + lroll(q[0] - hv, -1) + lroll(q[0] + hv, 1) - half * hu + NOISE_AMP * force
    tend_u = u * dx[1] + v * dy[1] + dx[0]
    tend_v = u * dx[2] + v * dy[2] + dy[0]
    new_u = loc[1] + (lroll(q[1], -1) + lroll(q[1], 1)) - half * tend_u + (COURANT * cor) * v
    new_v = loc[2] + (lroll(q[2], -1) + lroll(q[2], 1)) - half * tend_v - (COURANT * cor) * u
    return new_eta, new_u, new_v


def coriolis(cols, total_y):
    y = lax.rem(lax.axis_index("gy") * T + cols + total_y, total_y)
    return 0.1 + 0.2 * ((y.astype(F32) + 0.5) / total_y - 0.5)


def pack_kernel(fields_hbm, noise_hbm, fields, noise, slots, sems):
    members = fields.shape[0]
    copies = [pltpu.make_async_copy(noise_hbm, noise, sems.at[members])]
    for m in range(members):
        copies.append(pltpu.make_async_copy(fields_hbm.at[m], fields.at[m], sems.at[m]))
    for copy in copies:
        copy.start()
    own = 2 * lax.axis_index("gx") + lax.axis_index("gy")
    own_y, own_x, own_xy = own ^ 1, own ^ 2, own ^ 3
    copies[0].wait()
    top = subl((8, T)) < 4
    ln = lanes((T, T)) // 8
    slots[own] = jnp.zeros((T, T), F32)
    for p in range(members // 2):
        k = 8 * (3 * members + p)
        slots[own_x, k : k + 8] = jnp.where(top, noise[p, 0:8], noise[p, T - 8 : T])
    acc = jnp.zeros((T, T), F32)
    for m in range(members):
        acc = jnp.where(ln == 4 * m + 3, lroll(noise[m // 2], 32 * m + 28), acc)
    for m in range(members):
        copies[1 + m].wait()
        for f in range(3):
            k = 8 * (3 * m + f)
            slots[own_x, k : k + 8] = jnp.where(top, fields[m, f, 0:8], fields[m, f, T - 8 : T])
            acc = jnp.where(ln == 4 * m + f, lroll(fields[m, f], 32 * m + 8 * f + 4), acc)
    slots[own_y] = acc
    slots[own_xy, 0:8] = jnp.where(top, acc[0:8], acc[T - 8 : T])


def own_columns(tiles):
    shape = tiles[0].shape
    ln = lanes(shape) // 8
    acc = jnp.zeros(shape, F32)
    for m, a in enumerate(tiles):
        acc = jnp.where(ln == 4 * m, lroll(a, 32 * m + 8), acc)
        acc = jnp.where(ln == 4 * m + 3, lroll(a, 32 * m + 24), acc)
    return acc


def interior_kernel(total_y, fields, noise, cells_hbm, values_hbm, inner, ownrow, owncol, pick_y, cell_x,
                    values, tmp, cells, sems):
    members = fields.shape[0]
    copies = [
        pltpu.make_async_copy(cells_hbm, cells, sems.at[0]),
        pltpu.make_async_copy(values_hbm, values, sems.at[1]),
    ]
    for copy in copies:
        copy.start()
    cor = coriolis(lanes((1, T)), total_y)
    for src, dst in ((fields, tmp), (tmp, inner)):
        for m in range(members):
            for r in range(0, T, CHUNK):
                new = one_step(src, (m,), r, CHUNK, T, noise[m // 2, r : r + CHUNK], cor)
                for f in range(3):
                    dst[m, f, r : r + CHUNK] = new[f]
    for m in range(members):
        for f in range(4):
            src = fields.at[m, f] if f < 3 else noise.at[m // 2]
            ownrow[f, 2 * m] = src[0:8]
            ownrow[f, 2 * m + 1] = src[T - 8 : T]
    for f in range(4):
        tiles = []
        for m in range(members):
            src = fields.at[m, f] if f < 3 else noise.at[m // 2]
            tiles.append(src[...])
        owncol[f] = own_columns(tiles)
    for copy in copies:
        copy.wait()
    cell = cells[...]
    line_y = lax.broadcasted_iota(jnp.int32, pick_y.shape, 0)
    pick_y[...] = jnp.where(line_y == lax.rem(cell, T), 1.0, 0.0).astype(pick_y.dtype)
    cell_x[...] = cell // T


def merge_kernel(total_y, devices, inner, ownrow, owncol, slots, pick_y, cell_x, values, out, rs, rs1, cs, cs1, eta_s):
    members = inner.shape[0]
    tall = T + 16
    l32 = lax.rem(lanes((1, T)), 32)
    cor_row = coriolis(lanes((1, T)), total_y)
    cor_col = coriolis(jnp.where(l32 < 16, l32 + 120, l32 - 24), total_y)
    is_low = (l32 >= 20) & (l32 < 24)
    is_high = (l32 >= 8) & (l32 < 12)

    own = 2 * lax.axis_index("gx") + lax.axis_index("gy")
    own_y, own_x, own_xy = own ^ 1, own ^ 2, own ^ 3
    row_of = lambda m, f: pl.ds(8 * (3 * m + f if f < 3 else 3 * members + m // 2), 8)
    for f in range(4):
        for m in range(members):
            halo = slots[own_x, row_of(m, f)]
            rs[f, 32 * m : 32 * m + 8] = halo
            rs[f, 32 * m + 8 : 32 * m + 16] = ownrow[f, 2 * m]
            rs[f, 32 * m + 16 : 32 * m + 24] = ownrow[f, 2 * m + 1]
            rs[f, 32 * m + 24 : 32 * m + 32] = halo
        with_halo = lambda own, recv: jnp.where(
            is_low, lroll(recv, 20 - 8 * f), jnp.where(is_high, lroll(recv, 4 - 8 * f), own)
        )
        tiles = [slots[own_x, row_of(m, f)] for m in range(members)]
        ends = with_halo(own_columns(tiles), slots[own_xy, 0:8])
        cs[f, 0:8] = ends
        cs[f, T + 8 : T + 16] = ends
        cs[f, 8 : T + 8] = with_halo(owncol[f], slots[own_y])

    def twice(a, a1, total, cor):
        chunk = total // 2
        for src, dst in ((a, a1), (a1, a)):
            for r in range(0, total, chunk):
                new = one_step(src, (), r, chunk, total, a[3, r : r + chunk], cor)
                for f in range(3):
                    dst[f, r : r + chunk] = new[f]

    twice(rs, rs1, T, cor_row)
    twice(cs, cs1, tall, cor_col)

    per = 96 // devices
    stride = members // 2 * 8 * per + 1
    top = subl((8, T)) < 4
    left = lanes((8, T)) < 4
    right = lanes((8, T)) >= T - 4
    for m in range(members):
        p, mm = m // 2, m % 2
        for f in range(3):
            for t in range(T // 8):
                a = inner[m, f, 8 * t : 8 * t + 8]
                if t == 0:
                    a = jnp.where(top, rs[f, 32 * m + 8 : 32 * m + 16], a)
                if t == T // 8 - 1:
                    a = jnp.where(top, a, rs[f, 32 * m + 16 : 32 * m + 24])
                col = cs[f, 8 * t + 8 : 8 * t + 16]
                a = jnp.where(left, lroll(col, 104 - 32 * m), a)
                a = jnp.where(right, lroll(col, 120 - 32 * m), a)
                k = mm * 48 + f * 16 + t
                first = (k // per) * stride + p * 8 * per + 8 * (k % per)
                out[first : first + 8] = a
                if f == 0:
                    eta_s[m * T + 8 * t : m * T + 8 * t + 8] = a

    eta = eta_s[...]
    hi = eta.astype(jnp.bfloat16)
    rest = eta - hi.astype(F32)
    mid = rest.astype(jnp.bfloat16)
    low = (rest - mid.astype(F32)).astype(jnp.bfloat16)
    dot = lambda part: jnp.dot(part, pick_y[...], preferred_element_type=F32)
    seen = dot(hi) + (dot(mid) + dot(low))
    pick_x = lax.broadcasted_iota(jnp.int32, pick_y.shape, 0) == cell_x[...]
    logw = jnp.zeros((1, T), F32)
    for m in range(members):
        at = jnp.sum(jnp.where(pick_x, seen[m * T : (m + 1) * T], 0.0), axis=0, keepdims=True)
        miss = at - values[...]
        total = jnp.sum(miss * miss, axis=1, keepdims=True)
        logw = jnp.where(lanes((1, T)) == m, -0.5 * total / OBS_VAR, logw)
    for j in range(devices):
        out[(j + 1) * stride - 1 : (j + 1) * stride] = logw


def select_kernel(members, devices, lineage_hbm, recv, out, log_weights, lineage, sem):
    copy = pltpu.make_async_copy(lineage_hbm, lineage, sem)
    copy.start()
    pairs, rows = members // 2 * devices, out.shape[1]
    stride = members // 2 * rows + 1
    logw = recv[pl.ds(stride - 1, devices, stride)]
    logw = jnp.where(lanes(logw.shape) < members, logw, -jnp.inf)
    peak = jnp.max(jnp.max(logw, axis=1, keepdims=True), axis=0, keepdims=True)
    total = jnp.sum(jnp.sum(jnp.exp(logw - peak), axis=1, keepdims=True), axis=0, keepdims=True)
    own = recv[pl.ds(lax.axis_index("mem") * stride + stride - 1, 1)]
    log_weights[0] = (own - peak - jnp.log(total))[:, :members]
    copy.wait()

    def body(k, carry):
        pair = lineage[0, k]
        first = lax.div(pair, members // 2) * stride + lax.rem(pair, members // 2) * rows
        out[k] = recv[pl.ds(first, rows)]
        return carry

    lax.fori_loop(0, pairs, body, 0, unroll=8)


VM = pl.BlockSpec(memory_space=pltpu.VMEM)
HB = pl.BlockSpec(memory_space=pltpu.MemorySpace.HBM)
PARAMS = pltpu.CompilerParams(vmem_limit_bytes=24 << 20)


def in_hbm(a):
    return pltpu.with_memory_space_constraint(a, pltpu.MemorySpace.HBM)


def sds(*shape):
    return jax.ShapeDtypeStruct(shape, F32)


def shards(fields, noise, ancestors, obs_cells, obs_values):
    members = fields.shape[0]
    devices = lax.axis_size("mem")
    total_y = T * lax.axis_size("gy")
    fields_vm, noise_vm, slots = pl.pallas_call(
        pack_kernel,
        out_shape=(sds(*fields.shape), sds(*noise.shape), sds(4, T, T)),
        in_specs=[HB] * 2,
        out_specs=[VM] * 3,
        scratch_shapes=[pltpu.SemaphoreType.DMA((members + 1,))],
        compiler_params=PARAMS,
        name="pack",
    )(in_hbm(fields), in_hbm(noise))
    recv = lax.all_to_all(slots, ("gx", "gy"), 0, 0)
    count = obs_cells.shape[-1]
    inner, ownrow, owncol, pick_y, cell_x, values = pl.pallas_call(
        functools.partial(interior_kernel, total_y),
        out_shape=(
            sds(members, 3, T, T),
            sds(4, 2 * members, 8, T),
            sds(4, T, T),
            jax.ShapeDtypeStruct((T, count), jnp.bfloat16),
            jax.ShapeDtypeStruct((1, count), jnp.int32),
            sds(1, count),
        ),
        in_specs=[VM] * 2 + [HB] * 2,
        out_specs=[VM] * 6,
        scratch_shapes=[
            pltpu.VMEM((members, 3, T, T), F32),
            pltpu.VMEM((1, count), jnp.int32),
            pltpu.SemaphoreType.DMA((2,)),
        ],
        compiler_params=PARAMS,
        cost_estimate=pl.CostEstimate(flops=50_000_000, bytes_accessed=2_500_000, transcendentals=0),
        name="interior",
    )(fields_vm, noise_vm, in_hbm(obs_cells.reshape(1, -1)), in_hbm(obs_values.reshape(1, -1)))
    rows = 768 // devices
    stride = members // 2 * rows + 1
    pieces = pl.pallas_call(
        functools.partial(merge_kernel, total_y, devices),
        out_shape=sds(devices * stride, T),
        in_specs=[VM] * 7,
        out_specs=VM,
        scratch_shapes=[
            pltpu.VMEM((4, T, T), F32),
            pltpu.VMEM((3, T, T), F32),
            pltpu.VMEM((4, T + 16, T), F32),
            pltpu.VMEM((3, T + 16, T), F32),
            pltpu.VMEM((members * T, T), F32),
        ],
        compiler_params=PARAMS,
        name="merge",
    )(inner, ownrow, owncol, recv, pick_y, cell_x, values)
    held = lax.all_to_all(pieces.reshape(devices, stride, 1, T), "mem", 0, 0).reshape(devices * stride, T)
    picked, log_weights = pl.pallas_call(
        functools.partial(select_kernel, members, devices),
        out_shape=(sds(devices * members // 2, rows, T), sds(1, 1, members)),
        in_specs=[HB, VM],
        out_specs=[VM] * 2,
        scratch_shapes=[pltpu.SMEM((1, devices * members // 2), jnp.int32), pltpu.SemaphoreType.DMA],
        compiler_params=PARAMS,
        name="select",
    )(in_hbm(ancestors.reshape(1, -1)), held)
    back = lax.all_to_all(picked.reshape(devices, members // 2, rows, T), "mem", 0, 0)
    resampled = back.transpose(1, 0, 2, 3).reshape(fields.shape)
    return (resampled, log_weights)


def solution(mesh):
    return jax.shard_map(
        shards,
        mesh=mesh,
        in_specs=(
            P("mem", None, "gx", "gy"),
            P("mem", "gx", "gy"),
            P("gx", "gy", None),
            P("gx", "gy", None),
            P("gx", "gy", None),
        ),
        out_specs=(P("mem", None, "gx", "gy"), P("gx", "gy", "mem")),
        check_vma=False,
    )
```

```python
import functools

import jax
import jax.numpy as jnp
from jax import lax
from jax.experimental import pallas as pl
from jax.experimental.pallas import tpu as pltpu
from jax.sharding import PartitionSpec as P

COURANT = 0.3
NOISE_AMP = 0.1
OBS_VAR = 0.25
T = 128
F32 = jnp.float32
CHUNK = 64


def lanes(shape):
    return lax.broadcasted_iota(jnp.int32, shape, len(shape) - 1)


def subl(shape):
    return lax.broadcasted_iota(jnp.int32, shape, len(shape) - 2)


def lroll(a, shift):
    return pltpu.roll(a, shift % T, 1)


def rows_at(ref, lead, start, off, count, total):
    first = start + off
    if first < 0:
        return pltpu.roll(ref[(*lead, pl.ds(0, count))], -first, 0)
    if first + count > total:
        over = first + count - total
        return pltpu.roll(ref[(*lead, pl.ds(total - count, count))], count - over, 0)
    return ref[(*lead, pl.ds(first, count))]


def one_step(ref, lead, start, count, total, force, cor):
    get = lambda f, off: rows_at(ref, (*lead, f), start, off, count, total)
    cen, low, high = [], [], []
    dx, dy, loc, q = [], [], [], []
    for f in range(3):
        a, am, ap = get(f, 0), get(f, -1), get(f, 1)
        far = get(f, -2) + get(f, 2)
        cross = am + ap
        yp, ym = lroll(a, -1), lroll(a, 1)
        cen.append(a)
        low.append(am)
        high.append(ap)
        dx.append(ap - am)
        dy.append(yp - ym)
        loc.append(0.71 * a + (0.09 * cross - 0.005 * far))
        q.append(0.09 * a - (0.01 * cross + 0.005 * (yp + ym)))
    eta, u, v = cen
    half = 0.5 * COURANT
    hv = half * ((1.0 + eta) * v)
    hu = (1.0 + high[0]) * high[1] - (1.0 + low[0]) * low[1]
    new_eta = loc[0] + lroll(q[0] - hv, -1) + lroll(q[0] + hv, 1) - half * hu + NOISE_AMP * force
    tend_u = u * dx[1] + v * dy[1] + dx[0]
    tend_v = u * dx[2] + v * dy[2] + dy[0]
    new_u = loc[1] + (lroll(q[1], -1) + lroll(q[1], 1)) - half * tend_u + (COURANT * cor) * v
    new_v = loc[2] + (lroll(q[2], -1) + lroll(q[2], 1)) - half * tend_v - (COURANT * cor) * u
    return new_eta, new_u, new_v


def coriolis(cols, total_y):
    y = lax.rem(lax.axis_index("gy") * T + cols + total_y, total_y)
    return 0.1 + 0.2 * ((y.astype(F32) + 0.5) / total_y - 0.5)


def pack_kernel(fields_hbm, noise_hbm, fields, noise, rowpack, colpack, sems):
    members = fields.shape[0]
    copies = [pltpu.make_async_copy(noise_hbm, noise, sems.at[members])]
    for m in range(members):
        copies.append(pltpu.make_async_copy(fields_hbm.at[m], fields.at[m], sems.at[m]))
    for copy in copies:
        copy.start()
    copies[0].wait()
    top = subl((8, T)) < 4
    ln = lanes((T, T)) // 8
    for p in range(members // 2):
        rowpack[3 * members + p] = jnp.where(top, noise[p, 0:8], noise[p, T - 8 : T])
    acc = jnp.zeros((T, T), F32)
    for m in range(members):
        acc = jnp.where(ln == 4 * m + 3, lroll(noise[m // 2], 32 * m + 28), acc)
    for m in range(members):
        copies[1 + m].wait()
        for f in range(3):
            rowpack[3 * m + f] = jnp.where(top, fields[m, f, 0:8], fields[m, f, T - 8 : T])
            acc = jnp.where(ln == 4 * m + f, lroll(fields[m, f], 32 * m + 8 * f + 4), acc)
    colpack[...] = acc


def own_columns(tiles):
    shape = tiles[0].shape
    ln = lanes(shape) // 8
    acc = jnp.zeros(shape, F32)
    for m, a in enumerate(tiles):
        acc = jnp.where(ln == 4 * m, lroll(a, 32 * m + 8), acc)
        acc = jnp.where(ln == 4 * m + 3, lroll(a, 32 * m + 24), acc)
    return acc


def interior_kernel(total_y, fields, noise, cells_hbm, values_hbm, inner, ownrow, owncol, pick_y, cell_x,
                    values, tmp, cells, sems):
    members = fields.shape[0]
    copies = [
        pltpu.make_async_copy(cells_hbm, cells, sems.at[0]),
        pltpu.make_async_copy(values_hbm, values, sems.at[1]),
    ]
    for copy in copies:
        copy.start()
    cor = coriolis(lanes((1, T)), total_y)
    for src, dst in ((fields, tmp), (tmp, inner)):
        for m in range(members):
            for r in range(0, T, CHUNK):
                new = one_step(src, (m,), r, CHUNK, T, noise[m // 2, r : r + CHUNK], cor)
                for f in range(3):
                    dst[m, f, r : r + CHUNK] = new[f]
    for m in range(members):
        for f in range(4):
            src = fields.at[m, f] if f < 3 else noise.at[m // 2]
            ownrow[f, 2 * m] = src[0:8]
            ownrow[f, 2 * m + 1] = src[T - 8 : T]
    for f in range(4):
        tiles = []
        for m in range(members):
            src = fields.at[m, f] if f < 3 else noise.at[m // 2]
            tiles.append(src[...])
        owncol[f] = own_columns(tiles)
    for copy in copies:
        copy.wait()
    cell = cells[...]
    line_y = lax.broadcasted_iota(jnp.int32, pick_y.shape, 0)
    pick_y[...] = jnp.where(line_y == lax.rem(cell, T), 1.0, 0.0).astype(pick_y.dtype)
    cell_x[...] = cell // T


def twice(a, a1, total, cor):
    chunk = total // 2
    for src, dst in ((a, a1), (a1, a)):
        for r in range(0, total, chunk):
            new = one_step(src, (), r, chunk, total, a[3, r : r + chunk], cor)
            for f in range(3):
                dst[f, r : r + chunk] = new[f]


def rows_kernel(total_y, ownrow, rowrecv, edge, rs, rs1):
    members = ownrow.shape[1] // 2
    for f in range(4):
        for m in range(members):
            halo = rowrecv[3 * m + f] if f < 3 else rowrecv[3 * members + m // 2]
            rs[f, 32 * m : 32 * m + 8] = halo
            rs[f, 32 * m + 8 : 32 * m + 16] = ownrow[f, 2 * m]
            rs[f, 32 * m + 16 : 32 * m + 24] = ownrow[f, 2 * m + 1]
            rs[f, 32 * m + 24 : 32 * m + 32] = halo
    twice(rs, rs1, T, coriolis(lanes((1, T)), total_y))
    for f in range(3):
        for m in range(members):
            edge[f, 2 * m] = rs[f, 32 * m + 8 : 32 * m + 16]
            edge[f, 2 * m + 1] = rs[f, 32 * m + 16 : 32 * m + 24]


def merge_kernel(total_y, devices, inner, edge, owncol, rowrecv, colrecv, cornrecv, pick_y, cell_x,
                 values, out, cs, cs1, eta_s):
    members = inner.shape[0]
    tall = T + 16
    l32 = lax.rem(lanes((1, T)), 32)
    cor_col = coriolis(jnp.where(l32 < 16, l32 + 120, l32 - 24), total_y)
    is_low = (l32 >= 20) & (l32 < 24)
    is_high = (l32 >= 8) & (l32 < 12)
    corn = jnp.where(subl((8, T)) < 4, cornrecv[0:8], cornrecv[T - 8 : T])

    for f in range(4):
        with_halo = lambda own, recv: jnp.where(
            is_low, lroll(recv, 20 - 8 * f), jnp.where(is_high, lroll(recv, 4 - 8 * f), own)
        )
        tiles = [rowrecv[3 * m + f] if f < 3 else rowrecv[3 * members + m // 2] for m in range(members)]
        ends = with_halo(own_columns(tiles), corn)
        cs[f, 0:8] = ends
        cs[f, T + 8 : T + 16] = ends
        cs[f, 8 : T + 8] = with_halo(owncol[f], colrecv[...])
    twice(cs, cs1, tall, cor_col)

    per = 96 // devices
    stride = members // 2 * 8 * per + 1
    top = subl((8, T)) < 4
    left = lanes((8, T)) < 4
    right = lanes((8, T)) >= T - 4
    for m in range(members):
        p, mm = m // 2, m % 2
        for f in range(3):
            for t in range(T // 8):
                a = inner[m, f, 8 * t : 8 * t + 8]
                if t == 0:
                    a = jnp.where(top, edge[f, 2 * m], a)
                if t == T // 8 - 1:
                    a = jnp.where(top, a, edge[f, 2 * m + 1])
                col = cs[f, 8 * t + 8 : 8 * t + 16]
                a = jnp.where(left, lroll(col, 104 - 32 * m), a)
                a = jnp.where(right, lroll(col, 120 - 32 * m), a)
                k = mm * 48 + f * 16 + t
                first = (k // per) * stride + p * 8 * per + 8 * (k % per)
                out[first : first + 8] = a
                if f == 0:
                    eta_s[m * T + 8 * t : m * T + 8 * t + 8] = a

    eta = eta_s[...]
    hi = eta.astype(jnp.bfloat16)
    rest = eta - hi.astype(F32)
    mid = rest.astype(jnp.bfloat16)
    low = (rest - mid.astype(F32)).astype(jnp.bfloat16)
    dot = lambda part: jnp.dot(part, pick_y[...], preferred_element_type=F32)
    seen = dot(hi) + (dot(mid) + dot(low))
    pick_x = lax.broadcasted_iota(jnp.int32, pick_y.shape, 0) == cell_x[...]
    logw = jnp.zeros((1, T), F32)
    for m in range(members):
        at = jnp.sum(jnp.where(pick_x, seen[m * T : (m + 1) * T], 0.0), axis=0, keepdims=True)
        miss = at - values[...]
        total = jnp.sum(miss * miss, axis=1, keepdims=True)
        logw = jnp.where(lanes((1, T)) == m, -0.5 * total / OBS_VAR, logw)
    for j in range(devices):
        out[(j + 1) * stride - 1 : (j + 1) * stride] = logw


def select_kernel(members, devices, lineage_hbm, recv, out, log_weights, lineage, sem):
    copy = pltpu.make_async_copy(lineage_hbm, lineage, sem)
    copy.start()
    pairs, rows = members // 2 * devices, out.shape[1]
    stride = members // 2 * rows + 1
    logw = recv[pl.ds(stride - 1, devices, stride)]
    logw = jnp.where(lanes(logw.shape) < members, logw, -jnp.inf)
    peak = jnp.max(jnp.max(logw, axis=1, keepdims=True), axis=0, keepdims=True)
    total = jnp.sum(jnp.sum(jnp.exp(logw - peak), axis=1, keepdims=True), axis=0, keepdims=True)
    own = recv[pl.ds(lax.axis_index("mem") * stride + stride - 1, 1)]
    log_weights[0] = (own - peak - jnp.log(total))[:, :members]
    copy.wait()

    def body(k, carry):
        pair = lineage[0, k]
        first = lax.div(pair, members // 2) * stride + lax.rem(pair, members // 2) * rows
        out[k] = recv[pl.ds(first, rows)]
        return carry

    lax.fori_loop(0, pairs, body, 0, unroll=8)


VM = pl.BlockSpec(memory_space=pltpu.VMEM)
HB = pl.BlockSpec(memory_space=pltpu.MemorySpace.HBM)
PARAMS = pltpu.CompilerParams(vmem_limit_bytes=24 << 20)


def in_hbm(a):
    return pltpu.with_memory_space_constraint(a, pltpu.MemorySpace.HBM)


def sds(*shape):
    return jax.ShapeDtypeStruct(shape, F32)


def shards(fields, noise, ancestors, obs_cells, obs_values):
    members = fields.shape[0]
    devices = lax.axis_size("mem")
    total_y = T * lax.axis_size("gy")
    fields_vm, noise_vm, rowpack, colpack = pl.pallas_call(
        pack_kernel,
        out_shape=(
            sds(*fields.shape),
            sds(*noise.shape),
            sds(3 * members + members // 2, 8, T),
            sds(T, T),
        ),
        in_specs=[HB] * 2,
        out_specs=[VM] * 4,
        scratch_shapes=[pltpu.SemaphoreType.DMA((members + 1,))],
        compiler_params=PARAMS,
        name="pack",
    )(in_hbm(fields), in_hbm(noise))
    swap = [(0, 1), (1, 0)]
    colrecv = lax.ppermute(colpack, "gy", swap)
    rowrecv = lax.ppermute(rowpack, "gx", swap)
    count = obs_cells.shape[-1]
    inner, ownrow, owncol, pick_y, cell_x, values = pl.pallas_call(
        functools.partial(interior_kernel, total_y),
        out_shape=(
            sds(members, 3, T, T),
            sds(4, 2 * members, 8, T),
            sds(4, T, T),
            jax.ShapeDtypeStruct((T, count), jnp.bfloat16),
            jax.ShapeDtypeStruct((1, count), jnp.int32),
            sds(1, count),
        ),
        in_specs=[VM] * 2 + [HB] * 2,
        out_specs=[VM] * 6,
        scratch_shapes=[
            pltpu.VMEM((members, 3, T, T), F32),
            pltpu.VMEM((1, count), jnp.int32),
            pltpu.SemaphoreType.DMA((2,)),
        ],
        compiler_params=PARAMS,
        cost_estimate=pl.CostEstimate(flops=50_000_000, bytes_accessed=2_500_000, transcendentals=0),
        name="interior",
    )(fields_vm, noise_vm, in_hbm(obs_cells.reshape(1, -1)), in_hbm(obs_values.reshape(1, -1)))
    colrecv, rowrecv, inner = lax.optimization_barrier((colrecv, rowrecv, inner))
    cornrecv = lax.ppermute(colrecv, "gx", swap)
    edge = pl.pallas_call(
        functools.partial(rows_kernel, total_y),
        out_shape=sds(3, 2 * members, 8, T),
        in_specs=[VM] * 2,
        out_specs=VM,
        scratch_shapes=[pltpu.VMEM((4, T, T), F32), pltpu.VMEM((3, T, T), F32)],
        compiler_params=PARAMS,
        cost_estimate=pl.CostEstimate(flops=12_000_000, bytes_accessed=250_000, transcendentals=0),
        name="rows",
    )(ownrow, rowrecv)
    rows = 768 // devices
    stride = members // 2 * rows + 1
    pieces = pl.pallas_call(
        functools.partial(merge_kernel, total_y, devices),
        out_shape=sds(devices * stride, T),
        in_specs=[VM] * 9,
        out_specs=VM,
        scratch_shapes=[
            pltpu.VMEM((4, T + 16, T), F32),
            pltpu.VMEM((3, T + 16, T), F32),
            pltpu.VMEM((members * T, T), F32),
        ],
        compiler_params=PARAMS,
        name="merge",
    )(inner, edge, owncol, rowrecv, colrecv, cornrecv, pick_y, cell_x, values)
    held = lax.all_to_all(pieces.reshape(devices, stride, 1, T), "mem", 0, 0).reshape(devices * stride, T)
    picked, log_weights = pl.pallas_call(
        functools.partial(select_kernel, members, devices),
        out_shape=(sds(devices * members // 2, rows, T), sds(1, 1, members)),
        in_specs=[HB, VM],
        out_specs=[VM] * 2,
        scratch_shapes=[pltpu.SMEM((1, devices * members // 2), jnp.int32), pltpu.SemaphoreType.DMA],
        compiler_params=PARAMS,
        name="select",
    )(in_hbm(ancestors.reshape(1, -1)), held)
    back = lax.all_to_all(picked.reshape(devices, members // 2, rows, T), "mem", 0, 0)
    resampled = back.transpose(1, 0, 2, 3).reshape(fields.shape)
    return (resampled, log_weights)


def solution(mesh):
    return jax.shard_map(
        shards,
        mesh=mesh,
        in_specs=(
            P("mem", None, "gx", "gy"),
            P("mem", "gx", "gy"),
            P("gx", "gy", None),
            P("gx", "gy", None),
            P("gx", "gy", None),
        ),
        out_specs=(P("mem", None, "gx", "gy"), P("gx", "gy", "mem")),
        check_vma=False,
    )
```

```python
import functools

import jax
import jax.numpy as jnp
from jax import lax
from jax.experimental import pallas as pl
from jax.experimental.pallas import tpu as pltpu
from jax.sharding import PartitionSpec as P

COURANT = 0.3
NOISE_AMP = 0.1
OBS_VAR = 0.25
T = 128
F32 = jnp.float32
CHUNK = 64


def lanes(shape):
    return lax.broadcasted_iota(jnp.int32, shape, len(shape) - 1)


def subl(shape):
    return lax.broadcasted_iota(jnp.int32, shape, len(shape) - 2)


def lroll(a, shift):
    return pltpu.roll(a, shift % T, 1)


def rows_at(ref, lead, start, off, count, total):
    first = start + off
    if first < 0:
        return pltpu.roll(ref[(*lead, pl.ds(0, count))], -first, 0)
    if first + count > total:
        over = first + count - total
        return pltpu.roll(ref[(*lead, pl.ds(total - count, count))], count - over, 0)
    return ref[(*lead, pl.ds(first, count))]


def one_step(ref, lead, start, count, total, force, cor):
    get = lambda f, off: rows_at(ref, (*lead, f), start, off, count, total)
    cen, low, high = [], [], []
    dx, dy, loc, q = [], [], [], []
    for f in range(3):
        a, am, ap = get(f, 0), get(f, -1), get(f, 1)
        far = get(f, -2) + get(f, 2)
        cross = am + ap
        yp, ym = lroll(a, -1), lroll(a, 1)
        cen.append(a)
        low.append(am)
        high.append(ap)
        dx.append(ap - am)
        dy.append(yp - ym)
        loc.append(0.71 * a + (0.09 * cross - 0.005 * far))
        q.append(0.09 * a - (0.01 * cross + 0.005 * (yp + ym)))
    eta, u, v = cen
    half = 0.5 * COURANT
    hv = half * ((1.0 + eta) * v)
    hu = (1.0 + high[0]) * high[1] - (1.0 + low[0]) * low[1]
    new_eta = loc[0] + lroll(q[0] - hv, -1) + lroll(q[0] + hv, 1) - half * hu + NOISE_AMP * force
    tend_u = u * dx[1] + v * dy[1] + dx[0]
    tend_v = u * dx[2] + v * dy[2] + dy[0]
    new_u = loc[1] + (lroll(q[1], -1) + lroll(q[1], 1)) - half * tend_u + (COURANT * cor) * v
    new_v = loc[2] + (lroll(q[2], -1) + lroll(q[2], 1)) - half * tend_v - (COURANT * cor) * u
    return new_eta, new_u, new_v


def coriolis(cols, total_y):
    y = lax.rem(lax.axis_index("gy") * T + cols + total_y, total_y)
    return 0.1 + 0.2 * ((y.astype(F32) + 0.5) / total_y - 0.5)


def pack_kernel(total_y, fields_hbm, noise_hbm, fields, noise, rowpack, colpack, inner, tmp, sems):
    members = fields.shape[0]
    copies = [pltpu.make_async_copy(noise_hbm, noise, sems.at[members])]
    for m in range(members):
        copies.append(pltpu.make_async_copy(fields_hbm.at[m], fields.at[m], sems.at[m]))
    for copy in copies:
        copy.start()
    copies[0].wait()
    top = subl((8, T)) < 4
    ln = lanes((T, T)) // 8
    for p in range(members // 2):
        rowpack[3 * members + p] = jnp.where(top, noise[p, 0:8], noise[p, T - 8 : T])
    acc = jnp.zeros((T, T), F32)
    for m in range(members):
        acc = jnp.where(ln == 4 * m + 3, lroll(noise[m // 2], 32 * m + 28), acc)
    for m in range(members):
        copies[1 + m].wait()
        for f in range(3):
            rowpack[3 * m + f] = jnp.where(top, fields[m, f, 0:8], fields[m, f, T - 8 : T])
            acc = jnp.where(ln == 4 * m + f, lroll(fields[m, f], 32 * m + 8 * f + 4), acc)
    colpack[...] = acc

    @pl.when(lax.axis_index("gy") == 0)
    def _():
        interior(total_y, fields, noise, inner, tmp)


def own_columns(tiles):
    shape = tiles[0].shape
    ln = lanes(shape) // 8
    acc = jnp.zeros(shape, F32)
    for m, a in enumerate(tiles):
        acc = jnp.where(ln == 4 * m, lroll(a, 32 * m + 8), acc)
        acc = jnp.where(ln == 4 * m + 3, lroll(a, 32 * m + 24), acc)
    return acc


def interior(total_y, fields, noise, inner, tmp):
    cor = coriolis(lanes((1, T)), total_y)
    for src, dst in ((fields, tmp), (tmp, inner)):
        for m in range(fields.shape[0]):
            for r in range(0, T, CHUNK):
                new = one_step(src, (m,), r, CHUNK, T, noise[m // 2, r : r + CHUNK], cor)
                for f in range(3):
                    dst[m, f, r : r + CHUNK] = new[f]


def interior_kernel(total_y, fields, noise, inner_in, cells_hbm, values_hbm, lineage_hbm, inner, ownrow, owncol,
                    pick_y, cell_x, values, lineage, tmp, cells, sems):
    members = fields.shape[0]
    copies = [
        pltpu.make_async_copy(cells_hbm, cells, sems.at[0]),
        pltpu.make_async_copy(values_hbm, values, sems.at[1]),
        pltpu.make_async_copy(lineage_hbm, lineage, sems.at[2]),
    ]
    for copy in copies:
        copy.start()

    @pl.when(lax.axis_index("gy") != 0)
    def _():
        interior(total_y, fields, noise, inner, tmp)

    for m in range(members):
        for f in range(4):
            src = fields.at[m, f] if f < 3 else noise.at[m // 2]
            ownrow[f, 2 * m] = src[0:8]
            ownrow[f, 2 * m + 1] = src[T - 8 : T]
    for f in range(4):
        tiles = []
        for m in range(members):
            src = fields.at[m, f] if f < 3 else noise.at[m // 2]
            tiles.append(src[...])
        owncol[f] = own_columns(tiles)
    for copy in copies:
        copy.wait()
    cell = cells[...]
    line_y = lax.broadcasted_iota(jnp.int32, pick_y.shape, 0)
    pick_y[...] = jnp.where(line_y == lax.rem(cell, T), 1.0, 0.0).astype(pick_y.dtype)
    cell_x[...] = cell // T


def twice(a, a1, total, cor):
    chunk = total // 2
    for src, dst in ((a, a1), (a1, a)):
        for r in range(0, total, chunk):
            new = one_step(src, (), r, chunk, total, a[3, r : r + chunk], cor)
            for f in range(3):
                dst[f, r : r + chunk] = new[f]


def rows_kernel(total_y, ownrow, rowrecv, edge, rs, rs1):
    members = ownrow.shape[1] // 2
    for f in range(4):
        for m in range(members):
            halo = rowrecv[3 * m + f] if f < 3 else rowrecv[3 * members + m // 2]
            rs[f, 32 * m : 32 * m + 8] = halo
            rs[f, 32 * m + 8 : 32 * m + 16] = ownrow[f, 2 * m]
            rs[f, 32 * m + 16 : 32 * m + 24] = ownrow[f, 2 * m + 1]
            rs[f, 32 * m + 24 : 32 * m + 32] = halo
    twice(rs, rs1, T, coriolis(lanes((1, T)), total_y))
    for f in range(3):
        for m in range(members):
            edge[f, 2 * m] = rs[f, 32 * m + 8 : 32 * m + 16]
            edge[f, 2 * m + 1] = rs[f, 32 * m + 16 : 32 * m + 24]


def merge_kernel(total_y, devices, inner, edge, owncol, rowrecv, colrecv, cornrecv, pick_y, cell_x,
                 values, out, cs, cs1, eta_s):
    members = inner.shape[0]
    tall = T + 16
    l32 = lax.rem(lanes((1, T)), 32)
    cor_col = coriolis(jnp.where(l32 < 16, l32 + 120, l32 - 24), total_y)
    is_low = (l32 >= 20) & (l32 < 24)
    is_high = (l32 >= 8) & (l32 < 12)
    corn = jnp.where(subl((8, T)) < 4, cornrecv[0:8], cornrecv[T - 8 : T])

    for f in range(4):
        with_halo = lambda own, recv: jnp.where(
            is_low, lroll(recv, 20 - 8 * f), jnp.where(is_high, lroll(recv, 4 - 8 * f), own)
        )
        tiles = [rowrecv[3 * m + f] if f < 3 else rowrecv[3 * members + m // 2] for m in range(members)]
        ends = with_halo(own_columns(tiles), corn)
        cs[f, 0:8] = ends
        cs[f, T + 8 : T + 16] = ends
        cs[f, 8 : T + 8] = with_halo(owncol[f], colrecv[...])
    twice(cs, cs1, tall, cor_col)

    per = 96 // devices
    stride = members // 2 * 8 * per + 1
    top = subl((8, T)) < 4
    left = lanes((8, T)) < 4
    right = lanes((8, T)) >= T - 4
    for m in range(members):
        p, mm = m // 2, m % 2
        for f in range(3):
            for t in range(T // 8):
                a = inner[m, f, 8 * t : 8 * t + 8]
                if t == 0:
                    a = jnp.where(top, edge[f, 2 * m], a)
                if t == T // 8 - 1:
                    a = jnp.where(top, a, edge[f, 2 * m + 1])
                col = cs[f, 8 * t + 8 : 8 * t + 16]
                a = jnp.where(left, lroll(col, 104 - 32 * m), a)
                a = jnp.where(right, lroll(col, 120 - 32 * m), a)
                k = mm * 48 + f * 16 + t
                first = (k // per) * stride + p * 8 * per + 8 * (k % per)
                out[first : first + 8] = a
                if f == 0:
                    eta_s[m * T + 8 * t : m * T + 8 * t + 8] = a

    eta = eta_s[...]
    hi = eta.astype(jnp.bfloat16)
    rest = eta - hi.astype(F32)
    mid = rest.astype(jnp.bfloat16)
    low = (rest - mid.astype(F32)).astype(jnp.bfloat16)
    dot = lambda part: jnp.dot(part, pick_y[...], preferred_element_type=F32)
    seen = dot(hi) + (dot(mid) + dot(low))
    pick_x = lax.broadcasted_iota(jnp.int32, pick_y.shape, 0) == cell_x[...]
    logw = jnp.zeros((1, T), F32)
    for m in range(members):
        at = jnp.sum(jnp.where(pick_x, seen[m * T : (m + 1) * T], 0.0), axis=0, keepdims=True)
        miss = at - values[...]
        total = jnp.sum(miss * miss, axis=1, keepdims=True)
        logw = jnp.where(lanes((1, T)) == m, -0.5 * total / OBS_VAR, logw)
    for j in range(devices):
        out[(j + 1) * stride - 1 : (j + 1) * stride] = logw


def select_kernel(members, lineage_vmem, recv, out, lineage, sem):
    copy = pltpu.make_async_copy(lineage_vmem, lineage, sem)
    copy.start()
    pairs, rows = out.shape[0], out.shape[1]
    per = members // 2
    copy.wait()
    for k in range(pairs):
        pair = lineage[0, k]
        out[k] = recv[pl.ds(lax.div(pair, per) * (per * rows + 1) + lax.rem(pair, per) * rows, rows)]


def finish_kernel(members, back, recv, out, log_weights, result, sems):
    devices = back.shape[0]
    copies = [pltpu.make_async_copy(back.at[:, p], out.at[p], sems.at[p]) for p in range(members // 2)]
    for copy in copies:
        copy.start()
    stride = recv.shape[0] // devices
    logw = recv[pl.ds(stride - 1, devices, stride)]
    logw = jnp.where(lanes(logw.shape) < members, logw, -jnp.inf)
    peak = jnp.max(jnp.max(logw, axis=1, keepdims=True), axis=0, keepdims=True)
    total = jnp.sum(jnp.sum(jnp.exp(logw - peak), axis=1, keepdims=True), axis=0, keepdims=True)
    own = recv[pl.ds(lax.axis_index("mem") * stride + stride - 1, 1)]
    result[0] = (own - peak - jnp.log(total))[:, :members]
    last = pltpu.make_async_copy(result, log_weights, sems.at[members // 2])
    last.start()
    for copy in copies:
        copy.wait()
    last.wait()


VM = pl.BlockSpec(memory_space=pltpu.VMEM)
HB = pl.BlockSpec(memory_space=pltpu.MemorySpace.HBM)
PARAMS = pltpu.CompilerParams(vmem_limit_bytes=24 << 20)


def in_hbm(a):
    return pltpu.with_memory_space_constraint(a, pltpu.MemorySpace.HBM)


def sds(*shape):
    return jax.ShapeDtypeStruct(shape, F32)


def shards(fields, noise, ancestors, obs_cells, obs_values):
    members = fields.shape[0]
    devices = lax.axis_size("mem")
    total_y = T * lax.axis_size("gy")
    fields_vm, noise_vm, rowpack, colpack, inner = pl.pallas_call(
        functools.partial(pack_kernel, total_y),
        out_shape=(
            sds(*fields.shape),
            sds(*noise.shape),
            sds(3 * members + members // 2, 8, T),
            sds(T, T),
            sds(members, 3, T, T),
        ),
        in_specs=[HB] * 2,
        out_specs=[VM] * 5,
        scratch_shapes=[pltpu.VMEM((members, 3, T, T), F32), pltpu.SemaphoreType.DMA((members + 1,))],
        compiler_params=PARAMS,
        name="pack",
    )(in_hbm(fields), in_hbm(noise))
    swap = [(0, 1), (1, 0)]
    colrecv = lax.ppermute(colpack, "gy", swap)
    rowrecv = lax.ppermute(rowpack, "gx", swap)
    count, pairs = obs_cells.shape[-1], ancestors.shape[-1]
    inner, ownrow, owncol, pick_y, cell_x, values, lineage = pl.pallas_call(
        functools.partial(interior_kernel, total_y),
        out_shape=(
            sds(members, 3, T, T),
            sds(4, 2 * members, 8, T),
            sds(4, T, T),
            jax.ShapeDtypeStruct((T, count), jnp.bfloat16),
            jax.ShapeDtypeStruct((1, count), jnp.int32),
            sds(1, count),
            jax.ShapeDtypeStruct((1, pairs), jnp.int32),
        ),
        in_specs=[VM] * 3 + [HB] * 3,
        out_specs=[VM] * 7,
        input_output_aliases={2: 0},
        scratch_shapes=[
            pltpu.VMEM((members, 3, T, T), F32),
            pltpu.VMEM((1, count), jnp.int32),
            pltpu.SemaphoreType.DMA((3,)),
        ],
        compiler_params=PARAMS,
        cost_estimate=pl.CostEstimate(flops=50_000_000, bytes_accessed=2_500_000, transcendentals=0),
        name="interior",
    )(
        fields_vm,
        noise_vm,
        inner,
        in_hbm(obs_cells.reshape(1, -1)),
        in_hbm(obs_values.reshape(1, -1)),
        in_hbm(ancestors.reshape(1, -1)),
    )
    colrecv, rowrecv, inner = lax.optimization_barrier((colrecv, rowrecv, inner))
    cornrecv = lax.ppermute(colrecv, "gx", swap)
    edge = pl.pallas_call(
        functools.partial(rows_kernel, total_y),
        out_shape=sds(3, 2 * members, 8, T),
        in_specs=[VM] * 2,
        out_specs=VM,
        scratch_shapes=[pltpu.VMEM((4, T, T), F32), pltpu.VMEM((3, T, T), F32)],
        compiler_params=PARAMS,
        cost_estimate=pl.CostEstimate(flops=12_000_000, bytes_accessed=250_000, transcendentals=0),
        name="rows",
    )(ownrow, rowrecv)
    rows = 768 // devices
    stride = members // 2 * rows + 1
    pieces = pl.pallas_call(
        functools.partial(merge_kernel, total_y, devices),
        out_shape=sds(devices * stride, T),
        in_specs=[VM] * 9,
        out_specs=VM,
        scratch_shapes=[
            pltpu.VMEM((4, T + 16, T), F32),
            pltpu.VMEM((3, T + 16, T), F32),
            pltpu.VMEM((members * T, T), F32),
        ],
        compiler_params=PARAMS,
        name="merge",
    )(inner, edge, owncol, rowrecv, colrecv, cornrecv, pick_y, cell_x, values)
    held = lax.all_to_all(pieces.reshape(devices, stride, 1, T), "mem", 0, 0).reshape(devices * stride, T)
    picked = pl.pallas_call(
        functools.partial(select_kernel, members),
        out_shape=sds(pairs, rows, T),
        in_specs=[VM, VM],
        out_specs=VM,
        scratch_shapes=[pltpu.SMEM((1, pairs), jnp.int32), pltpu.SemaphoreType.DMA],
        compiler_params=PARAMS,
        name="select",
    )(lineage, held)
    back = lax.all_to_all(picked.reshape(devices, members // 2, rows, T), "mem", 0, 0)
    resampled, log_weights = pl.pallas_call(
        functools.partial(finish_kernel, members),
        out_shape=(sds(members // 2, devices, rows, T), sds(1, 1, members)),
        in_specs=[VM, VM],
        out_specs=[HB, HB],
        scratch_shapes=[pltpu.VMEM((1, 1, members), F32), pltpu.SemaphoreType.DMA((members // 2 + 1,))],
        compiler_params=PARAMS,
        name="finish",
    )(back, held)
    return (resampled.reshape(fields.shape), log_weights)


def solution(mesh):
    return jax.shard_map(
        shards,
        mesh=mesh,
        in_specs=(
            P("mem", None, "gx", "gy"),
            P("mem", "gx", "gy"),
            P("gx", "gy", None),
            P("gx", "gy", None),
            P("gx", "gy", None),
        ),
        out_specs=(P("mem", None, "gx", "gy"), P("gx", "gy", "mem")),
        check_vma=False,
    )
```

```python
import functools

import jax
import jax.numpy as jnp
from jax import lax
from jax.experimental import pallas as pl
from jax.experimental.pallas import tpu as pltpu
from jax.sharding import PartitionSpec as P

COURANT = 0.3
NOISE_AMP = 0.1
OBS_VAR = 0.25
T = 128
F32 = jnp.float32
CHUNK = 128


def lanes(shape):
    return lax.broadcasted_iota(jnp.int32, shape, len(shape) - 1)


def subl(shape):
    return lax.broadcasted_iota(jnp.int32, shape, len(shape) - 2)


def lroll(a, shift):
    return pltpu.roll(a, shift % T, 1)


def rows_at(ref, lead, start, off, count, total):
    first = start + off
    if first < 0:
        return pltpu.roll(ref[(*lead, pl.ds(0, count))], -first, 0)
    if first + count > total:
        over = first + count - total
        return pltpu.roll(ref[(*lead, pl.ds(total - count, count))], count - over, 0)
    return ref[(*lead, pl.ds(first, count))]


def one_step(ref, lead, start, count, total, force, cor):
    get = lambda f, off: rows_at(ref, (*lead, f), start, off, count, total)
    cen, low, high = [], [], []
    dx, dy, loc, q = [], [], [], []
    for f in range(3):
        a, am, ap = get(f, 0), get(f, -1), get(f, 1)
        far = get(f, -2) + get(f, 2)
        cross = am + ap
        yp, ym = lroll(a, -1), lroll(a, 1)
        cen.append(a)
        low.append(am)
        high.append(ap)
        dx.append(ap - am)
        dy.append(yp - ym)
        loc.append(0.71 * a + (0.09 * cross - 0.005 * far))
        q.append(0.09 * a - (0.01 * cross + 0.005 * (yp + ym)))
    eta, u, v = cen
    half = 0.5 * COURANT
    hv = half * ((1.0 + eta) * v)
    hu = (1.0 + high[0]) * high[1] - (1.0 + low[0]) * low[1]
    new_eta = loc[0] + lroll(q[0] - hv, -1) + lroll(q[0] + hv, 1) - half * hu + NOISE_AMP * force
    tend_u = u * dx[1] + v * dy[1] + dx[0]
    tend_v = u * dx[2] + v * dy[2] + dy[0]
    new_u = loc[1] + (lroll(q[1], -1) + lroll(q[1], 1)) - half * tend_u + (COURANT * cor) * v
    new_v = loc[2] + (lroll(q[2], -1) + lroll(q[2], 1)) - half * tend_v - (COURANT * cor) * u
    return new_eta, new_u, new_v


def coriolis(cols, total_y):
    y = lax.rem(lax.axis_index("gy") * T + cols + total_y, total_y)
    return 0.1 + 0.2 * ((y.astype(F32) + 0.5) / total_y - 0.5)


def pack_kernel(fields_hbm, noise_hbm, fields, noise, rowpack, colpack, ownrow, owncol, sems):
    members = fields.shape[0]
    copies = [pltpu.make_async_copy(noise_hbm, noise, sems.at[members])]
    for m in range(members):
        copies.append(pltpu.make_async_copy(fields_hbm.at[m], fields.at[m], sems.at[m]))
    for copy in copies:
        copy.start()
    copies[0].wait()
    top = subl((8, T)) < 4
    ln = lanes((T, T)) // 8
    for p in range(members // 2):
        rowpack[3 * members + p] = jnp.where(top, noise[p, 0:8], noise[p, T - 8 : T])
    acc = jnp.zeros((T, T), F32)
    for m in range(members):
        acc = jnp.where(ln == 4 * m + 3, lroll(noise[m // 2], 32 * m + 28), acc)
    for m in range(members):
        copies[1 + m].wait()
        for f in range(3):
            rowpack[3 * m + f] = jnp.where(top, fields[m, f, 0:8], fields[m, f, T - 8 : T])
            acc = jnp.where(ln == 4 * m + f, lroll(fields[m, f], 32 * m + 8 * f + 4), acc)
    colpack[...] = acc

    @pl.when(lax.axis_index("gy") == 0)
    def _():
        own_strips(fields, noise, ownrow, owncol)


def own_columns(tiles):
    shape = tiles[0].shape
    ln = lanes(shape) // 8
    acc = jnp.zeros(shape, F32)
    for m, a in enumerate(tiles):
        acc = jnp.where(ln == 4 * m, lroll(a, 32 * m + 8), acc)
        acc = jnp.where(ln == 4 * m + 3, lroll(a, 32 * m + 24), acc)
    return acc


def own_strips(fields, noise, ownrow, owncol):
    members = fields.shape[0]
    for f in range(4):
        tiles = [fields[m, f] if f < 3 else noise[m // 2] for m in range(members)]
        for m, a in enumerate(tiles):
            ownrow[f, 2 * m] = a[0:8]
            ownrow[f, 2 * m + 1] = a[T - 8 : T]
        owncol[f] = own_columns(tiles)


def interior(total_y, fields, noise, inner, tmp):
    cor = coriolis(lanes((1, T)), total_y)
    for src, dst in ((fields, tmp), (tmp, inner)):
        for m in range(fields.shape[0]):
            for r in range(0, T, CHUNK):
                new = one_step(src, (m,), r, CHUNK, T, noise[m // 2, r : r + CHUNK], cor)
                for f in range(3):
                    dst[m, f, r : r + CHUNK] = new[f]


def interior_kernel(total_y, fields, noise, ownrow_in, owncol_in, cells_hbm, values_hbm, lineage_hbm,
                    ownrow, owncol, inner, pick_y, cell_x, values, lineage, tmp, cells, sems):
    members = fields.shape[0]
    copies = [
        pltpu.make_async_copy(cells_hbm, cells, sems.at[0]),
        pltpu.make_async_copy(values_hbm, values, sems.at[1]),
        pltpu.make_async_copy(lineage_hbm, lineage, sems.at[2]),
    ]
    for copy in copies:
        copy.start()

    @pl.when(lax.axis_index("gy") != 0)
    def _():
        own_strips(fields, noise, ownrow, owncol)

    interior(total_y, fields, noise, inner, tmp)
    for copy in copies:
        copy.wait()
    cell = cells[...]
    line_y = lax.broadcasted_iota(jnp.int32, pick_y.shape, 0)
    pick_y[...] = jnp.where(line_y == lax.rem(cell, T), 1.0, 0.0).astype(pick_y.dtype)
    cell_x[...] = cell // T


def twice(a, a1, total, cor):
    for src, dst in ((a, a1), (a1, a)):
        new = one_step(src, (), 0, total, total, a[3], cor)
        for f in range(3):
            dst[f, 0:total] = new[f]


def rows_kernel(total_y, ownrow, rowrecv, edge, rs, rs1):
    members = ownrow.shape[1] // 2
    for f in range(4):
        for m in range(members):
            halo = rowrecv[3 * m + f] if f < 3 else rowrecv[3 * members + m // 2]
            rs[f, 32 * m : 32 * m + 8] = halo
            rs[f, 32 * m + 8 : 32 * m + 16] = ownrow[f, 2 * m]
            rs[f, 32 * m + 16 : 32 * m + 24] = ownrow[f, 2 * m + 1]
            rs[f, 32 * m + 24 : 32 * m + 32] = halo
    twice(rs, rs1, T, coriolis(lanes((1, T)), total_y))
    for f in range(3):
        for m in range(members):
            edge[f, 2 * m] = rs[f, 32 * m + 8 : 32 * m + 16]
            edge[f, 2 * m + 1] = rs[f, 32 * m + 16 : 32 * m + 24]


def merge_kernel(total_y, devices, inner, edge, owncol, rowrecv, colrecv, cornrecv, pick_y, cell_x,
                 values, out, cs, cs1, eta_s):
    members = inner.shape[0]
    tall = T + 16
    l32 = lax.rem(lanes((1, T)), 32)
    cor_col = coriolis(jnp.where(l32 < 16, l32 + 120, l32 - 24), total_y)
    is_low = (l32 >= 20) & (l32 < 24)
    is_high = (l32 >= 8) & (l32 < 12)
    corn = jnp.where(subl((8, T)) < 4, cornrecv[0:8], cornrecv[T - 8 : T])

    for f in range(4):
        with_halo = lambda own, recv: jnp.where(
            is_low, lroll(recv, 20 - 8 * f), jnp.where(is_high, lroll(recv, 4 - 8 * f), own)
        )
        tiles = [rowrecv[3 * m + f] if f < 3 else rowrecv[3 * members + m // 2] for m in range(members)]
        ends = with_halo(own_columns(tiles), corn)
        cs[f, 0:8] = ends
        cs[f, T + 8 : T + 16] = ends
        cs[f, 8 : T + 8] = with_halo(owncol[f], colrecv[...])
    twice(cs, cs1, tall, cor_col)

    per = 96 // devices
    stride = members // 2 * 8 * per + 1
    top = subl((8, T)) < 4
    left = lanes((8, T)) < 4
    right = lanes((8, T)) >= T - 4
    for m in range(members):
        p, mm = m // 2, m % 2
        for f in range(3):
            for t in range(T // 8):
                a = inner[m, f, 8 * t : 8 * t + 8]
                if t == 0:
                    a = jnp.where(top, edge[f, 2 * m], a)
                if t == T // 8 - 1:
                    a = jnp.where(top, a, edge[f, 2 * m + 1])
                col = cs[f, 8 * t + 8 : 8 * t + 16]
                a = jnp.where(left, lroll(col, 104 - 32 * m), a)
                a = jnp.where(right, lroll(col, 120 - 32 * m), a)
                k = mm * 48 + f * 16 + t
                first = (k // per) * stride + p * 8 * per + 8 * (k % per)
                out[first : first + 8] = a
                if f == 0:
                    eta_s[m * T + 8 * t : m * T + 8 * t + 8] = a

    eta = eta_s[...]
    hi = eta.astype(jnp.bfloat16)
    rest = eta - hi.astype(F32)
    mid = rest.astype(jnp.bfloat16)
    low = (rest - mid.astype(F32)).astype(jnp.bfloat16)
    dot = lambda part: jnp.dot(part, pick_y[...], preferred_element_type=F32)
    seen = dot(hi) + (dot(mid) + dot(low))
    pick_x = lax.broadcasted_iota(jnp.int32, pick_y.shape, 0) == cell_x[...]
    logw = jnp.zeros((1, T), F32)
    for m in range(members):
        at = jnp.sum(jnp.where(pick_x, seen[m * T : (m + 1) * T], 0.0), axis=0, keepdims=True)
        miss = at - values[...]
        total = jnp.sum(miss * miss, axis=1, keepdims=True)
        logw = jnp.where(lanes((1, T)) == m, -0.5 * total / OBS_VAR, logw)
    for j in range(devices):
        out[(j + 1) * stride - 1 : (j + 1) * stride] = logw


def select_kernel(members, lineage_vmem, recv, out, lineage, sem):
    copy = pltpu.make_async_copy(lineage_vmem, lineage, sem)
    copy.start()
    pairs, rows = out.shape[0], out.shape[1]
    per = members // 2
    copy.wait()
    for k in range(pairs):
        pair = lineage[0, k]
        out[k] = recv[pl.ds(lax.div(pair, per) * (per * rows + 1) + lax.rem(pair, per) * rows, rows)]


def finish_kernel(members, back, recv, out, log_weights, result, sems):
    devices = back.shape[0]
    copies = [pltpu.make_async_copy(back.at[:, p], out.at[p], sems.at[p]) for p in range(members // 2)]
    for copy in copies:
        copy.start()
    stride = recv.shape[0] // devices
    logw = recv[pl.ds(stride - 1, devices, stride)]
    logw = jnp.where(lanes(logw.shape) < members, logw, -jnp.inf)
    peak = jnp.max(jnp.max(logw, axis=1, keepdims=True), axis=0, keepdims=True)
    total = jnp.sum(jnp.sum(jnp.exp(logw - peak), axis=1, keepdims=True), axis=0, keepdims=True)
    own = recv[pl.ds(lax.axis_index("mem") * stride + stride - 1, 1)]
    result[0] = (own - peak - jnp.log(total))[:, :members]
    last = pltpu.make_async_copy(result, log_weights, sems.at[members // 2])
    last.start()
    for copy in copies:
        copy.wait()
    last.wait()


VM = pl.BlockSpec(memory_space=pltpu.VMEM)
HB = pl.BlockSpec(memory_space=pltpu.MemorySpace.HBM)
PARAMS = pltpu.CompilerParams(vmem_limit_bytes=24 << 20)


def in_hbm(a):
    return pltpu.with_memory_space_constraint(a, pltpu.MemorySpace.HBM)


def sds(*shape):
    return jax.ShapeDtypeStruct(shape, F32)


def shards(fields, noise, ancestors, obs_cells, obs_values):
    members = fields.shape[0]
    devices = lax.axis_size("mem")
    total_y = T * lax.axis_size("gy")
    fields_vm, noise_vm, rowpack, colpack, ownrow, owncol = pl.pallas_call(
        pack_kernel,
        out_shape=(
            sds(*fields.shape),
            sds(*noise.shape),
            sds(3 * members + members // 2, 8, T),
            sds(T, T),
            sds(4, 2 * members, 8, T),
            sds(4, T, T),
        ),
        in_specs=[HB] * 2,
        out_specs=[VM] * 6,
        scratch_shapes=[pltpu.SemaphoreType.DMA((members + 1,))],
        compiler_params=PARAMS,
        name="pack",
    )(in_hbm(fields), in_hbm(noise))
    swap = [(0, 1), (1, 0)]
    colrecv = lax.ppermute(colpack, "gy", swap)
    rowrecv = lax.ppermute(rowpack, "gx", swap)
    count, pairs = obs_cells.shape[-1], ancestors.shape[-1]
    ownrow, owncol, inner, pick_y, cell_x, values, lineage = pl.pallas_call(
        functools.partial(interior_kernel, total_y),
        out_shape=(
            sds(4, 2 * members, 8, T),
            sds(4, T, T),
            sds(members, 3, T, T),
            jax.ShapeDtypeStruct((T, count), jnp.bfloat16),
            jax.ShapeDtypeStruct((1, count), jnp.int32),
            sds(1, count),
            jax.ShapeDtypeStruct((1, pairs), jnp.int32),
        ),
        in_specs=[VM] * 4 + [HB] * 3,
        out_specs=[VM] * 7,
        input_output_aliases={2: 0, 3: 1},
        scratch_shapes=[
            pltpu.VMEM((members, 3, T, T), F32),
            pltpu.VMEM((1, count), jnp.int32),
            pltpu.SemaphoreType.DMA((3,)),
        ],
        compiler_params=PARAMS,
        cost_estimate=pl.CostEstimate(flops=50_000_000, bytes_accessed=2_500_000, transcendentals=0),
        name="interior",
    )(
        fields_vm,
        noise_vm,
        ownrow,
        owncol,
        in_hbm(obs_cells.reshape(1, -1)),
        in_hbm(obs_values.reshape(1, -1)),
        in_hbm(ancestors.reshape(1, -1)),
    )
    colrecv, rowrecv, inner = lax.optimization_barrier((colrecv, rowrecv, inner))
    cornrecv = lax.ppermute(colrecv, "gx", swap)
    edge = pl.pallas_call(
        functools.partial(rows_kernel, total_y),
        out_shape=sds(3, 2 * members, 8, T),
        in_specs=[VM] * 2,
        out_specs=VM,
        scratch_shapes=[pltpu.VMEM((4, T, T), F32), pltpu.VMEM((3, T, T), F32)],
        compiler_params=PARAMS,
        cost_estimate=pl.CostEstimate(flops=12_000_000, bytes_accessed=250_000, transcendentals=0),
        name="rows",
    )(ownrow, rowrecv)
    rows = 768 // devices
    stride = members // 2 * rows + 1
    pieces = pl.pallas_call(
        functools.partial(merge_kernel, total_y, devices),
        out_shape=sds(devices * stride, T),
        in_specs=[VM] * 9,
        out_specs=VM,
        scratch_shapes=[
            pltpu.VMEM((4, T + 16, T), F32),
            pltpu.VMEM((3, T + 16, T), F32),
            pltpu.VMEM((members * T, T), F32),
        ],
        compiler_params=PARAMS,
        name="merge",
    )(inner, edge, owncol, rowrecv, colrecv, cornrecv, pick_y, cell_x, values)
    held = lax.all_to_all(pieces.reshape(devices, stride, 1, T), "mem", 0, 0).reshape(devices * stride, T)
    picked = pl.pallas_call(
        functools.partial(select_kernel, members),
        out_shape=sds(pairs, rows, T),
        in_specs=[VM, VM],
        out_specs=VM,
        scratch_shapes=[pltpu.SMEM((1, pairs), jnp.int32), pltpu.SemaphoreType.DMA],
        compiler_params=PARAMS,
        name="select",
    )(lineage, held)
    back = lax.all_to_all(picked.reshape(devices, members // 2, rows, T), "mem", 0, 0)
    resampled, log_weights = pl.pallas_call(
        functools.partial(finish_kernel, members),
        out_shape=(sds(members // 2, devices, rows, T), sds(1, 1, members)),
        in_specs=[VM, VM],
        out_specs=[HB, HB],
        scratch_shapes=[pltpu.VMEM((1, 1, members), F32), pltpu.SemaphoreType.DMA((members // 2 + 1,))],
        compiler_params=PARAMS,
        name="finish",
    )(back, held)
    return (resampled.reshape(fields.shape), log_weights)


def solution(mesh):
    return jax.shard_map(
        shards,
        mesh=mesh,
        in_specs=(
            P("mem", None, "gx", "gy"),
            P("mem", "gx", "gy"),
            P("gx", "gy", None),
            P("gx", "gy", None),
            P("gx", "gy", None),
        ),
        out_specs=(P("mem", None, "gx", "gy"), P("gx", "gy", "mem")),
        check_vma=False,
    )
```

```python
import functools

import jax
import jax.numpy as jnp
from jax import lax
from jax.experimental import pallas as pl
from jax.experimental.pallas import tpu as pltpu
from jax.sharding import PartitionSpec as P

COURANT = 0.3
NOISE_AMP = 0.1
OBS_VAR = 0.25
T = 128
F32 = jnp.float32
CHUNK = 128


def lanes(shape):
    return lax.broadcasted_iota(jnp.int32, shape, len(shape) - 1)


def subl(shape):
    return lax.broadcasted_iota(jnp.int32, shape, len(shape) - 2)


def lroll(a, shift):
    return pltpu.roll(a, shift % T, 1)


def rows_at(ref, lead, start, off, count, total):
    first = start + off
    if first < 0:
        return pltpu.roll(ref[(*lead, pl.ds(0, count))], -first, 0)
    if first + count > total:
        over = first + count - total
        return pltpu.roll(ref[(*lead, pl.ds(total - count, count))], count - over, 0)
    return ref[(*lead, pl.ds(first, count))]


def one_step(ref, lead, start, count, total, force, cor):
    get = lambda f, off: rows_at(ref, (*lead, f), start, off, count, total)
    cen, low, high = [], [], []
    dx, dy, loc, q = [], [], [], []
    for f in range(3):
        a, am, ap = get(f, 0), get(f, -1), get(f, 1)
        far = get(f, -2) + get(f, 2)
        cross = am + ap
        yp, ym = lroll(a, -1), lroll(a, 1)
        cen.append(a)
        low.append(am)
        high.append(ap)
        dx.append(ap - am)
        dy.append(yp - ym)
        loc.append(0.71 * a + (0.09 * cross - 0.005 * far))
        q.append(0.09 * a - (0.01 * cross + 0.005 * (yp + ym)))
    eta, u, v = cen
    half = 0.5 * COURANT
    hv = half * ((1.0 + eta) * v)
    hu = (1.0 + high[0]) * high[1] - (1.0 + low[0]) * low[1]
    new_eta = loc[0] + lroll(q[0] - hv, -1) + lroll(q[0] + hv, 1) - half * hu + NOISE_AMP * force
    tend_u = u * dx[1] + v * dy[1] + dx[0]
    tend_v = u * dx[2] + v * dy[2] + dy[0]
    new_u = loc[1] + (lroll(q[1], -1) + lroll(q[1], 1)) - half * tend_u + (COURANT * cor) * v
    new_v = loc[2] + (lroll(q[2], -1) + lroll(q[2], 1)) - half * tend_v - (COURANT * cor) * u
    return new_eta, new_u, new_v


def coriolis(cols, total_y):
    y = lax.rem(lax.axis_index("gy") * T + cols + total_y, total_y)
    return 0.1 + 0.2 * ((y.astype(F32) + 0.5) / total_y - 0.5)


def pack_kernel(fields_hbm, noise_hbm, fields, noise, rowpack, colpack, ownrow, owncol, sems):
    members = fields.shape[0]
    copies = [pltpu.make_async_copy(noise_hbm, noise, sems.at[members])]
    for m in range(members):
        copies.append(pltpu.make_async_copy(fields_hbm.at[m], fields.at[m], sems.at[m]))
    for copy in copies:
        copy.start()
    copies[0].wait()
    top = subl((8, T)) < 4
    ln = lanes((T, T)) // 8
    for p in range(members // 2):
        rowpack[3 * members + p] = jnp.where(top, noise[p, 0:8], noise[p, T - 8 : T])
    acc = jnp.zeros((T, T), F32)
    for m in range(members):
        acc = jnp.where(ln == 4 * m + 3, lroll(noise[m // 2], 32 * m + 28), acc)
    for m in range(members):
        copies[1 + m].wait()
        for f in range(3):
            rowpack[3 * m + f] = jnp.where(top, fields[m, f, 0:8], fields[m, f, T - 8 : T])
            acc = jnp.where(ln == 4 * m + f, lroll(fields[m, f], 32 * m + 8 * f + 4), acc)
    colpack[...] = acc

    @pl.when(lax.axis_index("gy") == 0)
    def _():
        own_strips(fields, noise, ownrow, owncol)


def own_columns(tiles):
    shape = tiles[0].shape
    ln = lanes(shape) // 8
    acc = jnp.zeros(shape, F32)
    for m, a in enumerate(tiles):
        acc = jnp.where(ln == 4 * m, lroll(a, 32 * m + 8), acc)
        acc = jnp.where(ln == 4 * m + 3, lroll(a, 32 * m + 24), acc)
    return acc


def own_strips(fields, noise, ownrow, owncol):
    members = fields.shape[0]
    for f in range(4):
        tiles = [fields[m, f] if f < 3 else noise[m // 2] for m in range(members)]
        for m, a in enumerate(tiles):
            ownrow[f, 2 * m] = a[0:8]
            ownrow[f, 2 * m + 1] = a[T - 8 : T]
        owncol[f] = own_columns(tiles)


def interior(total_y, fields, noise, inner, tmp):
    cor = coriolis(lanes((1, T)), total_y)
    for src, dst in ((fields, tmp), (tmp, inner)):
        for m in range(fields.shape[0]):
            for r in range(0, T, CHUNK):
                new = one_step(src, (m,), r, CHUNK, T, noise[m // 2, r : r + CHUNK], cor)
                for f in range(3):
                    dst[m, f, r : r + CHUNK] = new[f]


def interior_kernel(total_y, fields, noise, ownrow_in, owncol_in, cells_hbm, values_hbm, lineage_hbm,
                    ownrow, owncol, inner, pick_y, cell_x, values, lineage, tmp, cells, sems):
    members = fields.shape[0]
    copies = [
        pltpu.make_async_copy(cells_hbm, cells, sems.at[0]),
        pltpu.make_async_copy(values_hbm, values, sems.at[1]),
        pltpu.make_async_copy(lineage_hbm, lineage, sems.at[2]),
    ]
    for copy in copies:
        copy.start()

    @pl.when(lax.axis_index("gy") != 0)
    def _():
        own_strips(fields, noise, ownrow, owncol)

    interior(total_y, fields, noise, inner, tmp)
    for copy in copies:
        copy.wait()
    cell = cells[...]
    line_y = lax.broadcasted_iota(jnp.int32, pick_y.shape, 0)
    pick_y[...] = jnp.where(line_y == lax.rem(cell, T), 1.0, 0.0).astype(pick_y.dtype)
    cell_x[...] = cell // T


def twice(a, a1, total, cor):
    for src, dst in ((a, a1), (a1, a)):
        new = one_step(src, (), 0, total, total, a[3], cor)
        for f in range(3):
            dst[f, 0:total] = new[f]


def column_masks():
    l32 = lax.rem(lanes((1, T)), 32)
    cols = jnp.where(l32 < 16, l32 + 120, l32 - 24)
    return cols, (l32 >= 20) & (l32 < 24), (l32 >= 8) & (l32 < 12)


def with_halo(own, recv, f, is_low, is_high):
    return jnp.where(is_low, lroll(recv, 20 - 8 * f), jnp.where(is_high, lroll(recv, 4 - 8 * f), own))


def some_rows(src, dst, first, count, cor, force):
    new = one_step(src, (), first, count, T + 16, force[3, first : first + count], cor)
    for f in range(3):
        dst[f, first : first + count] = new[f]


def strips_kernel(total_y, ownrow, rowrecv, owncol, colrecv, edge, cs, cs1, rs, rs1):
    members = ownrow.shape[1] // 2
    cols, is_low, is_high = column_masks()
    halo = lambda m, f: rowrecv[3 * m + f] if f < 3 else rowrecv[3 * members + m // 2]
    for f in range(4):
        for m in range(members):
            rs[f, 32 * m : 32 * m + 8] = halo(m, f)
            rs[f, 32 * m + 8 : 32 * m + 16] = ownrow[f, 2 * m]
            rs[f, 32 * m + 16 : 32 * m + 24] = ownrow[f, 2 * m + 1]
            rs[f, 32 * m + 24 : 32 * m + 32] = halo(m, f)
        cs[f, 0:8] = own_columns([halo(m, f) for m in range(members)])
        cs[f, 8 : T + 8] = with_halo(owncol[f], colrecv[...], f, is_low, is_high)
    some_rows(cs, cs1, 16, T - 16, coriolis(cols, total_y), cs)
    twice(rs, rs1, T, coriolis(lanes((1, T)), total_y))
    for f in range(3):
        for m in range(members):
            edge[f, 2 * m] = rs[f, 32 * m + 8 : 32 * m + 16]
            edge[f, 2 * m + 1] = rs[f, 32 * m + 16 : 32 * m + 24]


def merge_kernel(total_y, devices, inner, edge, cs_in, cs1_in, cornrecv, pick_y, cell_x, values, cs, cs1, out, eta_s):
    members = inner.shape[0]
    cols, is_low, is_high = column_masks()
    cor_col = coriolis(cols, total_y)
    corn = jnp.where(subl((8, T)) < 4, cornrecv[0:8], cornrecv[T - 8 : T])
    for f in range(4):
        ends = with_halo(cs[f, 0:8], corn, f, is_low, is_high)
        cs[f, 0:8] = ends
        cs[f, T + 8 : T + 16] = ends
    some_rows(cs, cs1, 0, 16, cor_col, cs)
    some_rows(cs, cs1, T, 16, cor_col, cs)
    some_rows(cs1, cs, 8, T, cor_col, cs)

    per = 96 // devices
    stride = members // 2 * 8 * per + 1
    top = subl((8, T)) < 4
    left = lanes((8, T)) < 4
    right = lanes((8, T)) >= T - 4
    for m in range(members):
        p, mm = m // 2, m % 2
        for f in range(3):
            for t in range(T // 8):
                a = inner[m, f, 8 * t : 8 * t + 8]
                if t == 0:
                    a = jnp.where(top, edge[f, 2 * m], a)
                if t == T // 8 - 1:
                    a = jnp.where(top, a, edge[f, 2 * m + 1])
                col = cs[f, 8 * t + 8 : 8 * t + 16]
                a = jnp.where(left, lroll(col, 104 - 32 * m), a)
                a = jnp.where(right, lroll(col, 120 - 32 * m), a)
                k = mm * 48 + f * 16 + t
                first = (k // per) * stride + p * 8 * per + 8 * (k % per)
                out[first : first + 8] = a
                if f == 0:
                    eta_s[m * T + 8 * t : m * T + 8 * t + 8] = a

    eta = eta_s[...]
    hi = eta.astype(jnp.bfloat16)
    rest = eta - hi.astype(F32)
    mid = rest.astype(jnp.bfloat16)
    low = (rest - mid.astype(F32)).astype(jnp.bfloat16)
    dot = lambda part: jnp.dot(part, pick_y[...], preferred_element_type=F32)
    seen = dot(hi) + (dot(mid) + dot(low))
    pick_x = lax.broadcasted_iota(jnp.int32, pick_y.shape, 0) == cell_x[...]
    logw = jnp.zeros((1, T), F32)
    for m in range(members):
        at = jnp.sum(jnp.where(pick_x, seen[m * T : (m + 1) * T], 0.0), axis=0, keepdims=True)
        miss = at - values[...]
        total = jnp.sum(miss * miss, axis=1, keepdims=True)
        logw = jnp.where(lanes((1, T)) == m, -0.5 * total / OBS_VAR, logw)
    for j in range(devices):
        out[(j + 1) * stride - 1 : (j + 1) * stride] = logw


def select_kernel(members, lineage_vmem, recv, out, lineage, sem):
    copy = pltpu.make_async_copy(lineage_vmem, lineage, sem)
    copy.start()
    pairs, rows = out.shape[0], out.shape[1]
    per = members // 2
    copy.wait()
    for k in range(pairs):
        pair = lineage[0, k]
        out[k] = recv[pl.ds(lax.div(pair, per) * (per * rows + 1) + lax.rem(pair, per) * rows, rows)]


def finish_kernel(members, back, recv, out, log_weights, result, sems):
    devices = back.shape[0]
    copies = [pltpu.make_async_copy(back.at[:, p], out.at[p], sems.at[p]) for p in range(members // 2)]
    for copy in copies:
        copy.start()
    stride = recv.shape[0] // devices
    logw = recv[pl.ds(stride - 1, devices, stride)]
    logw = jnp.where(lanes(logw.shape) < members, logw, -jnp.inf)
    peak = jnp.max(jnp.max(logw, axis=1, keepdims=True), axis=0, keepdims=True)
    total = jnp.sum(jnp.sum(jnp.exp(logw - peak), axis=1, keepdims=True), axis=0, keepdims=True)
    own = recv[pl.ds(lax.axis_index("mem") * stride + stride - 1, 1)]
    result[0] = (own - peak - jnp.log(total))[:, :members]
    last = pltpu.make_async_copy(result, log_weights, sems.at[members // 2])
    last.start()
    for copy in copies:
        copy.wait()
    last.wait()


VM = pl.BlockSpec(memory_space=pltpu.VMEM)
HB = pl.BlockSpec(memory_space=pltpu.MemorySpace.HBM)
PARAMS = pltpu.CompilerParams(vmem_limit_bytes=24 << 20)


def in_hbm(a):
    return pltpu.with_memory_space_constraint(a, pltpu.MemorySpace.HBM)


def sds(*shape):
    return jax.ShapeDtypeStruct(shape, F32)


def shards(fields, noise, ancestors, obs_cells, obs_values):
    members = fields.shape[0]
    devices = lax.axis_size("mem")
    total_y = T * lax.axis_size("gy")
    fields_vm, noise_vm, rowpack, colpack, ownrow, owncol = pl.pallas_call(
        pack_kernel,
        out_shape=(
            sds(*fields.shape),
            sds(*noise.shape),
            sds(3 * members + members // 2, 8, T),
            sds(T, T),
            sds(4, 2 * members, 8, T),
            sds(4, T, T),
        ),
        in_specs=[HB] * 2,
        out_specs=[VM] * 6,
        scratch_shapes=[pltpu.SemaphoreType.DMA((members + 1,))],
        compiler_params=PARAMS,
        name="pack",
    )(in_hbm(fields), in_hbm(noise))
    swap = [(0, 1), (1, 0)]
    colrecv = lax.ppermute(colpack, "gy", swap)
    rowrecv = lax.ppermute(rowpack, "gx", swap)
    count, pairs = obs_cells.shape[-1], ancestors.shape[-1]
    ownrow, owncol, inner, pick_y, cell_x, values, lineage = pl.pallas_call(
        functools.partial(interior_kernel, total_y),
        out_shape=(
            sds(4, 2 * members, 8, T),
            sds(4, T, T),
            sds(members, 3, T, T),
            jax.ShapeDtypeStruct((T, count), jnp.bfloat16),
            jax.ShapeDtypeStruct((1, count), jnp.int32),
            sds(1, count),
            jax.ShapeDtypeStruct((1, pairs), jnp.int32),
        ),
        in_specs=[VM] * 4 + [HB] * 3,
        out_specs=[VM] * 7,
        input_output_aliases={2: 0, 3: 1},
        scratch_shapes=[
            pltpu.VMEM((members, 3, T, T), F32),
            pltpu.VMEM((1, count), jnp.int32),
            pltpu.SemaphoreType.DMA((3,)),
        ],
        compiler_params=PARAMS,
        cost_estimate=pl.CostEstimate(flops=50_000_000, bytes_accessed=2_500_000, transcendentals=0),
        name="interior",
    )(
        fields_vm,
        noise_vm,
        ownrow,
        owncol,
        in_hbm(obs_cells.reshape(1, -1)),
        in_hbm(obs_values.reshape(1, -1)),
        in_hbm(ancestors.reshape(1, -1)),
    )
    colrecv, rowrecv, inner = lax.optimization_barrier((colrecv, rowrecv, inner))
    cornrecv = lax.ppermute(colrecv, "gx", swap)
    edge, cs, cs1 = pl.pallas_call(
        functools.partial(strips_kernel, total_y),
        out_shape=(sds(3, 2 * members, 8, T), sds(4, T + 16, T), sds(3, T + 16, T)),
        in_specs=[VM] * 4,
        out_specs=[VM] * 3,
        scratch_shapes=[pltpu.VMEM((4, T, T), F32), pltpu.VMEM((3, T, T), F32)],
        compiler_params=PARAMS,
        cost_estimate=pl.CostEstimate(flops=18_000_000, bytes_accessed=700_000, transcendentals=0),
        name="strips",
    )(ownrow, rowrecv, owncol, colrecv)
    rows = 768 // devices
    stride = members // 2 * rows + 1
    _, _, pieces = pl.pallas_call(
        functools.partial(merge_kernel, total_y, devices),
        out_shape=(sds(4, T + 16, T), sds(3, T + 16, T), sds(devices * stride, T)),
        in_specs=[VM] * 8,
        out_specs=[VM] * 3,
        input_output_aliases={2: 0, 3: 1},
        scratch_shapes=[pltpu.VMEM((members * T, T), F32)],
        compiler_params=PARAMS,
        name="merge",
    )(inner, edge, cs, cs1, cornrecv, pick_y, cell_x, values)
    held = lax.all_to_all(pieces.reshape(devices, stride, 1, T), "mem", 0, 0).reshape(devices * stride, T)
    picked = pl.pallas_call(
        functools.partial(select_kernel, members),
        out_shape=sds(pairs, rows, T),
        in_specs=[VM, VM],
        out_specs=VM,
        scratch_shapes=[pltpu.SMEM((1, pairs), jnp.int32), pltpu.SemaphoreType.DMA],
        compiler_params=PARAMS,
        name="select",
    )(lineage, held)
    back = lax.all_to_all(picked.reshape(devices, members // 2, rows, T), "mem", 0, 0)
    resampled, log_weights = pl.pallas_call(
        functools.partial(finish_kernel, members),
        out_shape=(sds(members // 2, devices, rows, T), sds(1, 1, members)),
        in_specs=[VM, VM],
        out_specs=[HB, HB],
        scratch_shapes=[pltpu.VMEM((1, 1, members), F32), pltpu.SemaphoreType.DMA((members // 2 + 1,))],
        compiler_params=PARAMS,
        name="finish",
    )(back, held)
    return (resampled.reshape(fields.shape), log_weights)


def solution(mesh):
    return jax.shard_map(
        shards,
        mesh=mesh,
        in_specs=(
            P("mem", None, "gx", "gy"),
            P("mem", "gx", "gy"),
            P("gx", "gy", None),
            P("gx", "gy", None),
            P("gx", "gy", None),
        ),
        out_specs=(P("mem", None, "gx", "gy"), P("gx", "gy", "mem")),
        check_vma=False,
    )
```

```python
import functools

import jax
import jax.numpy as jnp
from jax import lax
from jax.experimental import pallas as pl
from jax.experimental.pallas import tpu as pltpu
from jax.sharding import PartitionSpec as P

COURANT = 0.3
NOISE_AMP = 0.1
OBS_VAR = 0.25
T = 128
F32 = jnp.float32
CHUNK = 128


def lanes(shape):
    return lax.broadcasted_iota(jnp.int32, shape, len(shape) - 1)


def subl(shape):
    return lax.broadcasted_iota(jnp.int32, shape, len(shape) - 2)


def lroll(a, shift):
    return pltpu.roll(a, shift % T, 1)


def rows_at(ref, lead, start, off, count, total):
    first = start + off
    if first < 0:
        return pltpu.roll(ref[(*lead, pl.ds(0, count))], -first, 0)
    if first + count > total:
        over = first + count - total
        return pltpu.roll(ref[(*lead, pl.ds(total - count, count))], count - over, 0)
    return ref[(*lead, pl.ds(first, count))]


def one_step(ref, lead, start, count, total, force, cor):
    get = lambda f, off: rows_at(ref, (*lead, f), start, off, count, total)
    cen, low, high = [], [], []
    dx, dy, loc, q = [], [], [], []
    for f in range(3):
        a, am, ap = get(f, 0), get(f, -1), get(f, 1)
        far = get(f, -2) + get(f, 2)
        cross = am + ap
        yp, ym = lroll(a, -1), lroll(a, 1)
        cen.append(a)
        low.append(am)
        high.append(ap)
        dx.append(ap - am)
        dy.append(yp - ym)
        loc.append(0.71 * a + (0.09 * cross - 0.005 * far))
        q.append(0.09 * a - (0.01 * cross + 0.005 * (yp + ym)))
    eta, u, v = cen
    half = 0.5 * COURANT
    hv = half * ((1.0 + eta) * v)
    hu = (1.0 + high[0]) * high[1] - (1.0 + low[0]) * low[1]
    new_eta = loc[0] + lroll(q[0] - hv, -1) + lroll(q[0] + hv, 1) - half * hu + NOISE_AMP * force
    tend_u = u * dx[1] + v * dy[1] + dx[0]
    tend_v = u * dx[2] + v * dy[2] + dy[0]
    new_u = loc[1] + (lroll(q[1], -1) + lroll(q[1], 1)) - half * tend_u + (COURANT * cor) * v
    new_v = loc[2] + (lroll(q[2], -1) + lroll(q[2], 1)) - half * tend_v - (COURANT * cor) * u
    return new_eta, new_u, new_v


def coriolis(cols, total_y):
    y = lax.rem(lax.axis_index("gy") * T + cols + total_y, total_y)
    return 0.1 + 0.2 * ((y.astype(F32) + 0.5) / total_y - 0.5)


def pack_kernel(fields_hbm, noise_hbm, fields, noise, rowpack, colpack, ownrow, owncol, sems):
    members = fields.shape[0]
    copies = [pltpu.make_async_copy(noise_hbm, noise, sems.at[members])]
    for m in range(members):
        copies.append(pltpu.make_async_copy(fields_hbm.at[m], fields.at[m], sems.at[m]))
    for copy in copies:
        copy.start()
    copies[0].wait()
    top = subl((8, T)) < 4
    ln = lanes((T, T)) // 8
    for p in range(members // 2):
        rowpack[3 * members + p] = jnp.where(top, noise[p, 0:8], noise[p, T - 8 : T])
    acc = jnp.zeros((T, T), F32)
    for m in range(members):
        acc = jnp.where(ln == 4 * m + 3, lroll(noise[m // 2], 32 * m + 28), acc)
    for m in range(members):
        copies[1 + m].wait()
        for f in range(3):
            rowpack[3 * m + f] = jnp.where(top, fields[m, f, 0:8], fields[m, f, T - 8 : T])
            acc = jnp.where(ln == 4 * m + f, lroll(fields[m, f], 32 * m + 8 * f + 4), acc)
    colpack[...] = acc

    @pl.when(lax.axis_index("gy") == 0)
    def _():
        own_strips(fields, noise, ownrow, owncol)


def own_columns(tiles):
    shape = tiles[0].shape
    ln = lanes(shape) // 8
    acc = jnp.zeros(shape, F32)
    for m, a in enumerate(tiles):
        acc = jnp.where(ln == 4 * m, lroll(a, 32 * m + 8), acc)
        acc = jnp.where(ln == 4 * m + 3, lroll(a, 32 * m + 24), acc)
    return acc


def own_strips(fields, noise, ownrow, owncol):
    members = fields.shape[0]
    for f in range(4):
        tiles = [fields[m, f] if f < 3 else noise[m // 2] for m in range(members)]
        for m, a in enumerate(tiles):
            ownrow[f, 2 * m] = a[0:8]
            ownrow[f, 2 * m + 1] = a[T - 8 : T]
        owncol[f] = own_columns(tiles)


def interior(total_y, fields, noise, inner, tmp):
    cor = coriolis(lanes((1, T)), total_y)
    for src, dst in ((fields, tmp), (tmp, inner)):
        for m in range(fields.shape[0]):
            for r in range(0, T, CHUNK):
                new = one_step(src, (m,), r, CHUNK, T, noise[m // 2, r : r + CHUNK], cor)
                for f in range(3):
                    dst[m, f, r : r + CHUNK] = new[f]


def interior_kernel(total_y, fields, noise, ownrow_in, owncol_in, cells_hbm, values_hbm, lineage_hbm,
                    ownrow, owncol, inner, pick_y, cell_x, values, lineage, tmp, cells, sems):
    members = fields.shape[0]
    copies = [
        pltpu.make_async_copy(cells_hbm, cells, sems.at[0]),
        pltpu.make_async_copy(values_hbm, values, sems.at[1]),
        pltpu.make_async_copy(lineage_hbm, lineage, sems.at[2]),
    ]
    for copy in copies:
        copy.start()

    @pl.when(lax.axis_index("gy") != 0)
    def _():
        own_strips(fields, noise, ownrow, owncol)

    interior(total_y, fields, noise, inner, tmp)
    for copy in copies:
        copy.wait()
    cell = cells[...]
    line_y = lax.broadcasted_iota(jnp.int32, pick_y.shape, 0)
    pick_y[...] = jnp.where(line_y == lax.rem(cell, T), 1.0, 0.0).astype(pick_y.dtype)
    cell_x[...] = cell // T


def twice(a, a1, total, cor):
    for src, dst in ((a, a1), (a1, a)):
        new = one_step(src, (), 0, total, total, a[3], cor)
        for f in range(3):
            dst[f, 0:total] = new[f]


def column_masks():
    l32 = lax.rem(lanes((1, T)), 32)
    cols = jnp.where(l32 < 16, l32 + 120, l32 - 24)
    return cols, (l32 >= 20) & (l32 < 24), (l32 >= 8) & (l32 < 12)


def with_halo(own, recv, f, is_low, is_high):
    return jnp.where(is_low, lroll(recv, 20 - 8 * f), jnp.where(is_high, lroll(recv, 4 - 8 * f), own))


def some_rows(src, dst, first, count, cor, force):
    new = one_step(src, (), first, count, T + 16, force[3, first : first + count], cor)
    for f in range(3):
        dst[f, first : first + count] = new[f]


def strips_kernel(total_y, ownrow, rowrecv, owncol, colrecv, edge, cs, cs1, rs, rs1):
    members = ownrow.shape[1] // 2
    cols, is_low, is_high = column_masks()
    halo = lambda m, f: rowrecv[3 * m + f] if f < 3 else rowrecv[3 * members + m // 2]
    for f in range(4):
        for m in range(members):
            rs[f, 32 * m : 32 * m + 8] = halo(m, f)
            rs[f, 32 * m + 8 : 32 * m + 16] = ownrow[f, 2 * m]
            rs[f, 32 * m + 16 : 32 * m + 24] = ownrow[f, 2 * m + 1]
            rs[f, 32 * m + 24 : 32 * m + 32] = halo(m, f)
        cs[f, 0:8] = own_columns([halo(m, f) for m in range(members)])
        cs[f, 8 : T + 8] = with_halo(owncol[f], colrecv[...], f, is_low, is_high)
    some_rows(cs, cs1, 16, T - 16, coriolis(cols, total_y), cs)
    twice(rs, rs1, T, coriolis(lanes((1, T)), total_y))
    for f in range(3):
        for m in range(members):
            edge[f, 2 * m] = rs[f, 32 * m + 8 : 32 * m + 16]
            edge[f, 2 * m + 1] = rs[f, 32 * m + 16 : 32 * m + 24]


def merge_kernel(total_y, devices, inner, edge, cs_in, cs1_in, cornrecv, pick_y, cell_x, values, cs, cs1, out, eta_s):
    members = inner.shape[0]
    cols, is_low, is_high = column_masks()
    cor_col = coriolis(cols, total_y)
    corn = jnp.where(subl((8, T)) < 4, cornrecv[0:8], cornrecv[T - 8 : T])
    for f in range(4):
        ends = with_halo(cs[f, 0:8], corn, f, is_low, is_high)
        cs[f, 0:8] = ends
        cs[f, T + 8 : T + 16] = ends
    some_rows(cs, cs1, 0, 16, cor_col, cs)
    some_rows(cs, cs1, T, 16, cor_col, cs)
    some_rows(cs1, cs, 8, T, cor_col, cs)

    per = 96 // devices
    stride = members // 2 * 8 * per + 1
    top = subl((8, T)) < 4
    left = lanes((8, T)) < 4
    right = lanes((8, T)) >= T - 4
    for m in range(members):
        p, mm = m // 2, m % 2
        for f in range(3):
            for t in range(T // 8):
                a = inner[m, f, 8 * t : 8 * t + 8]
                if t == 0:
                    a = jnp.where(top, edge[f, 2 * m], a)
                if t == T // 8 - 1:
                    a = jnp.where(top, a, edge[f, 2 * m + 1])
                col = cs[f, 8 * t + 8 : 8 * t + 16]
                a = jnp.where(left, lroll(col, 104 - 32 * m), a)
                a = jnp.where(right, lroll(col, 120 - 32 * m), a)
                k = mm * 48 + f * 16 + t
                first = (k // per) * stride + p * 8 * per + 8 * (k % per)
                out[first : first + 8] = a
                if f == 0:
                    eta_s[m * T + 8 * t : m * T + 8 * t + 8] = a

    eta = eta_s[...]
    hi = eta.astype(jnp.bfloat16)
    rest = eta - hi.astype(F32)
    mid = rest.astype(jnp.bfloat16)
    low = (rest - mid.astype(F32)).astype(jnp.bfloat16)
    dot = lambda part: jnp.dot(part, pick_y[...], preferred_element_type=F32)
    seen = dot(hi) + (dot(mid) + dot(low))
    pick_x = lax.broadcasted_iota(jnp.int32, pick_y.shape, 0) == cell_x[...]
    logw = jnp.zeros((1, T), F32)
    for m in range(members):
        at = jnp.sum(jnp.where(pick_x, seen[m * T : (m + 1) * T], 0.0), axis=0, keepdims=True)
        miss = at - values[...]
        total = jnp.sum(miss * miss, axis=1, keepdims=True)
        logw = jnp.where(lanes((1, T)) == m, -0.5 * total / OBS_VAR, logw)
    for j in range(devices):
        out[(j + 1) * stride - 1 : (j + 1) * stride] = logw


def select_kernel(members, lineage, recv, out):
    pairs, rows = out.shape[0], out.shape[1]
    per = members // 2
    for k in range(pairs):
        pair = lineage[0, k]
        out[k] = recv[pl.ds(lax.div(pair, per) * (per * rows + 1) + lax.rem(pair, per) * rows, rows)]


def finish_kernel(members, back, recv, out, log_weights, result, sems):
    devices = back.shape[0]
    copies = [pltpu.make_async_copy(back.at[:, p], out.at[p], sems.at[p]) for p in range(members // 2)]
    for copy in copies:
        copy.start()
    stride = recv.shape[0] // devices
    logw = recv[pl.ds(stride - 1, devices, stride)]
    logw = jnp.where(lanes(logw.shape) < members, logw, -jnp.inf)
    peak = jnp.max(jnp.max(logw, axis=1, keepdims=True), axis=0, keepdims=True)
    total = jnp.sum(jnp.sum(jnp.exp(logw - peak), axis=1, keepdims=True), axis=0, keepdims=True)
    own = recv[pl.ds(lax.axis_index("mem") * stride + stride - 1, 1)]
    result[0] = (own - peak - jnp.log(total))[:, :members]
    last = pltpu.make_async_copy(result, log_weights, sems.at[members // 2])
    last.start()
    for copy in copies:
        copy.wait()
    last.wait()


VM = pl.BlockSpec(memory_space=pltpu.VMEM)
HB = pl.BlockSpec(memory_space=pltpu.MemorySpace.HBM)
PARAMS = pltpu.CompilerParams(vmem_limit_bytes=24 << 20)


def in_hbm(a):
    return pltpu.with_memory_space_constraint(a, pltpu.MemorySpace.HBM)


def sds(*shape):
    return jax.ShapeDtypeStruct(shape, F32)


def shards(fields, noise, ancestors, obs_cells, obs_values):
    members = fields.shape[0]
    devices = lax.axis_size("mem")
    total_y = T * lax.axis_size("gy")
    fields_vm, noise_vm, rowpack, colpack, ownrow, owncol = pl.pallas_call(
        pack_kernel,
        out_shape=(
            sds(*fields.shape),
            sds(*noise.shape),
            sds(3 * members + members // 2, 8, T),
            sds(T, T),
            sds(4, 2 * members, 8, T),
            sds(4, T, T),
        ),
        in_specs=[HB] * 2,
        out_specs=[VM] * 6,
        scratch_shapes=[pltpu.SemaphoreType.DMA((members + 1,))],
        compiler_params=PARAMS,
        name="pack",
    )(in_hbm(fields), in_hbm(noise))
    swap = [(0, 1), (1, 0)]
    colrecv = lax.ppermute(colpack, "gy", swap)
    rowrecv = lax.ppermute(rowpack, "gx", swap)
    count, pairs = obs_cells.shape[-1], ancestors.shape[-1]
    ownrow, owncol, inner, pick_y, cell_x, values, lineage = pl.pallas_call(
        functools.partial(interior_kernel, total_y),
        out_shape=(
            sds(4, 2 * members, 8, T),
            sds(4, T, T),
            sds(members, 3, T, T),
            jax.ShapeDtypeStruct((T, count), jnp.bfloat16),
            jax.ShapeDtypeStruct((1, count), jnp.int32),
            sds(1, count),
            jax.ShapeDtypeStruct((1, pairs), jnp.int32),
        ),
        in_specs=[VM] * 4 + [HB] * 3,
        out_specs=[VM] * 7,
        input_output_aliases={2: 0, 3: 1},
        scratch_shapes=[
            pltpu.VMEM((members, 3, T, T), F32),
            pltpu.VMEM((1, count), jnp.int32),
            pltpu.SemaphoreType.DMA((3,)),
        ],
        compiler_params=PARAMS,
        cost_estimate=pl.CostEstimate(flops=50_000_000, bytes_accessed=2_500_000, transcendentals=0),
        name="interior",
    )(
        fields_vm,
        noise_vm,
        ownrow,
        owncol,
        in_hbm(obs_cells.reshape(1, -1)),
        in_hbm(obs_values.reshape(1, -1)),
        in_hbm(ancestors.reshape(1, -1)),
    )
    colrecv, rowrecv, inner = lax.optimization_barrier((colrecv, rowrecv, inner))
    cornrecv = lax.ppermute(colrecv, "gx", swap)
    edge, cs, cs1 = pl.pallas_call(
        functools.partial(strips_kernel, total_y),
        out_shape=(sds(3, 2 * members, 8, T), sds(4, T + 16, T), sds(3, T + 16, T)),
        in_specs=[VM] * 4,
        out_specs=[VM] * 3,
        scratch_shapes=[pltpu.VMEM((4, T, T), F32), pltpu.VMEM((3, T, T), F32)],
        compiler_params=PARAMS,
        cost_estimate=pl.CostEstimate(flops=18_000_000, bytes_accessed=700_000, transcendentals=0),
        name="strips",
    )(ownrow, rowrecv, owncol, colrecv)
    rows = 768 // devices
    stride = members // 2 * rows + 1
    _, _, pieces = pl.pallas_call(
        functools.partial(merge_kernel, total_y, devices),
        out_shape=(sds(4, T + 16, T), sds(3, T + 16, T), sds(devices * stride, T)),
        in_specs=[VM] * 8,
        out_specs=[VM] * 3,
        input_output_aliases={2: 0, 3: 1},
        scratch_shapes=[pltpu.VMEM((members * T, T), F32)],
        compiler_params=PARAMS,
        name="merge",
    )(inner, edge, cs, cs1, cornrecv, pick_y, cell_x, values)
    held = lax.all_to_all(pieces.reshape(devices, stride, 1, T), "mem", 0, 0).reshape(devices * stride, T)
    picked = pl.pallas_call(
        functools.partial(select_kernel, members),
        out_shape=sds(pairs, rows, T),
        in_specs=[VM, VM],
        out_specs=VM,
        compiler_params=PARAMS,
        name="select",
    )(lineage, held)
    back = lax.all_to_all(picked.reshape(devices, members // 2, rows, T), "mem", 0, 0)
    resampled, log_weights = pl.pallas_call(
        functools.partial(finish_kernel, members),
        out_shape=(sds(members // 2, devices, rows, T), sds(1, 1, members)),
        in_specs=[VM, VM],
        out_specs=[HB, HB],
        scratch_shapes=[pltpu.VMEM((1, 1, members), F32), pltpu.SemaphoreType.DMA((members // 2 + 1,))],
        compiler_params=PARAMS,
        name="finish",
    )(back, held)
    return (resampled.reshape(fields.shape), log_weights)


def solution(mesh):
    return jax.shard_map(
        shards,
        mesh=mesh,
        in_specs=(
            P("mem", None, "gx", "gy"),
            P("mem", "gx", "gy"),
            P("gx", "gy", None),
            P("gx", "gy", None),
            P("gx", "gy", None),
        ),
        out_specs=(P("mem", None, "gx", "gy"), P("gx", "gy", "mem")),
        check_vma=False,
    )
```

```python
import functools

import jax
import jax.numpy as jnp
from jax import lax
from jax.experimental import pallas as pl
from jax.experimental.pallas import tpu as pltpu
from jax.sharding import PartitionSpec as P

COURANT = 0.3
NOISE_AMP = 0.1
OBS_VAR = 0.25
T = 128
F32 = jnp.float32
CHUNK = 128


def lanes(shape):
    return lax.broadcasted_iota(jnp.int32, shape, len(shape) - 1)


def subl(shape):
    return lax.broadcasted_iota(jnp.int32, shape, len(shape) - 2)


def lroll(a, shift):
    return pltpu.roll(a, shift % T, 1)


def rows_at(ref, lead, start, off, count, total):
    first = start + off
    if first < 0:
        return pltpu.roll(ref[(*lead, pl.ds(0, count))], -first, 0)
    if first + count > total:
        over = first + count - total
        return pltpu.roll(ref[(*lead, pl.ds(total - count, count))], count - over, 0)
    return ref[(*lead, pl.ds(first, count))]


def one_step(ref, lead, start, count, total, force, cor):
    get = lambda f, off: rows_at(ref, (*lead, f), start, off, count, total)
    cen, low, high = [], [], []
    dx, dy, loc, q = [], [], [], []
    for f in range(3):
        a, am, ap = get(f, 0), get(f, -1), get(f, 1)
        far = get(f, -2) + get(f, 2)
        cross = am + ap
        yp, ym = lroll(a, -1), lroll(a, 1)
        cen.append(a)
        low.append(am)
        high.append(ap)
        dx.append(ap - am)
        dy.append(yp - ym)
        loc.append(0.71 * a + (0.09 * cross - 0.005 * far))
        q.append(0.09 * a - (0.01 * cross + 0.005 * (yp + ym)))
    eta, u, v = cen
    half = 0.5 * COURANT
    hv = half * ((1.0 + eta) * v)
    hu = (1.0 + high[0]) * high[1] - (1.0 + low[0]) * low[1]
    new_eta = loc[0] + lroll(q[0] - hv, -1) + lroll(q[0] + hv, 1) - half * hu + NOISE_AMP * force
    tend_u = u * dx[1] + v * dy[1] + dx[0]
    tend_v = u * dx[2] + v * dy[2] + dy[0]
    new_u = loc[1] + (lroll(q[1], -1) + lroll(q[1], 1)) - half * tend_u + (COURANT * cor) * v
    new_v = loc[2] + (lroll(q[2], -1) + lroll(q[2], 1)) - half * tend_v - (COURANT * cor) * u
    return new_eta, new_u, new_v


def coriolis(cols, total_y):
    y = lax.rem(lax.axis_index("gy") * T + cols + total_y, total_y)
    return 0.1 + 0.2 * ((y.astype(F32) + 0.5) / total_y - 0.5)


USED = (0, 1, 2, 4, 5, 6, 8, 9, 10, 12, 13, 14, 3)
SPARE = (7, 11, 15)


def fold(acc):
    ln = lanes((8, T)) // 8
    short = []
    for i, group in enumerate(USED):
        tile = acc[8 * i : 8 * i + 8]
        for j, spare in enumerate(SPARE):
            last = acc[8 * (len(USED) + j) : 8 * (len(USED) + j) + 8]
            tile = jnp.where(ln == spare, lroll(last, 8 * (spare - group)), tile)
        short.append(tile)
    return short


def unfold(ref, j):
    ln = lanes((8, T)) // 8
    tile = jnp.zeros((8, T), F32)
    for i, group in enumerate(USED):
        tile = jnp.where(ln == group, lroll(ref[8 * i : 8 * i + 8], 8 * (group - SPARE[j])), tile)
    return tile


def pack_kernel(fields_hbm, noise_hbm, fields, noise, rowpack, colpack, ownrow, owncol, sems):
    members = fields.shape[0]
    copies = [pltpu.make_async_copy(noise_hbm, noise, sems.at[members])]
    for m in range(members):
        copies.append(pltpu.make_async_copy(fields_hbm.at[m], fields.at[m], sems.at[m]))
    for copy in copies:
        copy.start()
    copies[0].wait()
    top = subl((8, T)) < 4
    ln = lanes((T, T)) // 8
    sub, lane = subl((8, T)), lanes((T, T))
    near = jnp.where(sub < 2, noise[0, 0:8], pltpu.roll(noise[1, 0:8], 2, 0))
    far = jnp.where(sub < 6, pltpu.roll(noise[1, T - 8 : T], 6, 0), noise[0, T - 8 : T])
    rowpack[3 * members] = jnp.where(top, near, far)
    acc = jnp.where((lane >= 24) & (lane < 28), lroll(noise[0], 26), 0.0)
    acc = jnp.where((lane >= 28) & (lane < 32), lroll(noise[1], 30), acc)
    for m in range(members):
        copies[1 + m].wait()
        for f in range(3):
            rowpack[3 * m + f] = jnp.where(top, fields[m, f, 0:8], fields[m, f, T - 8 : T])
            acc = jnp.where(ln == 4 * m + f, lroll(fields[m, f], 32 * m + 8 * f + 4), acc)
    for i, tile in enumerate(fold(acc)):
        colpack[8 * i : 8 * i + 8] = tile

    @pl.when(lax.axis_index("gy") == 0)
    def _():
        own_strips(fields, noise, ownrow, owncol)


def own_columns(tiles):
    shape = tiles[0].shape
    ln = lanes(shape) // 8
    acc = jnp.zeros(shape, F32)
    for m, a in enumerate(tiles):
        acc = jnp.where(ln == 4 * m, lroll(a, 32 * m + 8), acc)
        acc = jnp.where(ln == 4 * m + 3, lroll(a, 32 * m + 24), acc)
    return acc


def own_strips(fields, noise, ownrow, owncol):
    members = fields.shape[0]
    for f in range(4):
        tiles = [fields[m, f] if f < 3 else noise[m // 2] for m in range(members)]
        for m, a in enumerate(tiles):
            ownrow[f, 2 * m] = a[0:8]
            ownrow[f, 2 * m + 1] = a[T - 8 : T]
        owncol[f] = own_columns(tiles)


def interior(total_y, fields, noise, inner, tmp):
    cor = coriolis(lanes((1, T)), total_y)
    for src, dst in ((fields, tmp), (tmp, inner)):
        for m in range(fields.shape[0]):
            for r in range(0, T, CHUNK):
                new = one_step(src, (m,), r, CHUNK, T, noise[m // 2, r : r + CHUNK], cor)
                for f in range(3):
                    dst[m, f, r : r + CHUNK] = new[f]


def interior_kernel(total_y, fields, noise, ownrow_in, owncol_in, cells_hbm, values_hbm, lineage_hbm,
                    ownrow, owncol, inner, pick_y, cell_x, values, lineage, tmp, cells, sems):
    members = fields.shape[0]
    copies = [
        pltpu.make_async_copy(cells_hbm, cells, sems.at[0]),
        pltpu.make_async_copy(values_hbm, values, sems.at[1]),
        pltpu.make_async_copy(lineage_hbm, lineage, sems.at[2]),
    ]
    for copy in copies:
        copy.start()

    @pl.when(lax.axis_index("gy") != 0)
    def _():
        own_strips(fields, noise, ownrow, owncol)

    interior(total_y, fields, noise, inner, tmp)
    for copy in copies:
        copy.wait()
    cell = cells[...]
    line_y = lax.broadcasted_iota(jnp.int32, pick_y.shape, 0)
    pick_y[...] = jnp.where(line_y == lax.rem(cell, T), 1.0, 0.0).astype(pick_y.dtype)
    cell_x[...] = cell // T


def twice(a, a1, total, cor):
    for src, dst in ((a, a1), (a1, a)):
        new = one_step(src, (), 0, total, total, a[3], cor)
        for f in range(3):
            dst[f, 0:total] = new[f]


def column_masks():
    l32 = lax.rem(lanes((1, T)), 32)
    cols = jnp.where(l32 < 16, l32 + 120, l32 - 24)
    return cols, (l32 >= 20) & (l32 < 24), (l32 >= 8) & (l32 < 12)


def with_halo(own, recv, f, is_low, is_high):
    if f == 3:
        lane = lanes((1, T))
        for m in range(4):
            p = m // 2
            own = jnp.where(lane // 2 == 16 * m + 11, lroll(recv, 32 * m - 2 - 4 * p), own)
            own = jnp.where(lane // 2 == 16 * m + 4, lroll(recv, 32 * m - 18 - 4 * p), own)
        return own
    return jnp.where(is_low, lroll(recv, 20 - 8 * f), jnp.where(is_high, lroll(recv, 4 - 8 * f), own))


def some_rows(src, dst, first, count, cor, force):
    new = one_step(src, (), first, count, T + 16, force[3, first : first + count], cor)
    for f in range(3):
        dst[f, first : first + count] = new[f]


def strips_kernel(total_y, ownrow, rowrecv, owncol, colrecv, edge, cs, cs1, rs, rs1):
    members = ownrow.shape[1] // 2
    cols, is_low, is_high = column_masks()
    noise = rowrecv[3 * members]
    inside = jnp.where(subl((8, T)) < 4, pltpu.roll(noise, 6, 0), pltpu.roll(noise, 2, 0))
    halo = lambda m, f: rowrecv[3 * m + f] if f < 3 else (noise, inside)[m // 2]
    held = 8 * len(USED)
    last = [unfold(colrecv, j) for j in range(len(SPARE))]
    for f in range(4):
        for m in range(members):
            rs[f, 32 * m : 32 * m + 8] = halo(m, f)
            rs[f, 32 * m + 8 : 32 * m + 16] = ownrow[f, 2 * m]
            rs[f, 32 * m + 16 : 32 * m + 24] = ownrow[f, 2 * m + 1]
            rs[f, 32 * m + 24 : 32 * m + 32] = halo(m, f)
        cs[f, 0:8] = own_columns([halo(m, f) for m in range(members)])
        cs[f, 8 : held + 8] = with_halo(owncol[f, 0:held], colrecv[...], f, is_low, is_high)
        for j, tile in enumerate(last):
            k = held + 8 * j
            cs[f, k + 8 : k + 16] = with_halo(owncol[f, k : k + 8], tile, f, is_low, is_high)
    some_rows(cs, cs1, 16, T - 16, coriolis(cols, total_y), cs)
    twice(rs, rs1, T, coriolis(lanes((1, T)), total_y))
    for f in range(3):
        for m in range(members):
            edge[f, 2 * m] = rs[f, 32 * m + 8 : 32 * m + 16]
            edge[f, 2 * m + 1] = rs[f, 32 * m + 16 : 32 * m + 24]


def merge_kernel(total_y, devices, inner, edge, cs_in, cs1_in, cornrecv, pick_y, cell_x, values, cs, cs1, out, eta_s):
    members = inner.shape[0]
    cols, is_low, is_high = column_masks()
    cor_col = coriolis(cols, total_y)
    corn = jnp.where(subl((8, T)) < 4, cornrecv[0:8], unfold(cornrecv, len(SPARE) - 1))
    for f in range(4):
        ends = with_halo(cs[f, 0:8], corn, f, is_low, is_high)
        cs[f, 0:8] = ends
        cs[f, T + 8 : T + 16] = ends
    some_rows(cs, cs1, 0, 16, cor_col, cs)
    some_rows(cs, cs1, T, 16, cor_col, cs)
    some_rows(cs1, cs, 8, T, cor_col, cs)

    per = 96 // devices
    stride = members // 2 * 8 * per + 1
    top = subl((8, T)) < 4
    left = lanes((8, T)) < 4
    right = lanes((8, T)) >= T - 4
    for m in range(members):
        p, mm = m // 2, m % 2
        for f in range(3):
            for t in range(T // 8):
                a = inner[m, f, 8 * t : 8 * t + 8]
                if t == 0:
                    a = jnp.where(top, edge[f, 2 * m], a)
                if t == T // 8 - 1:
                    a = jnp.where(top, a, edge[f, 2 * m + 1])
                col = cs[f, 8 * t + 8 : 8 * t + 16]
                a = jnp.where(left, lroll(col, 104 - 32 * m), a)
                a = jnp.where(right, lroll(col, 120 - 32 * m), a)
                k = mm * 48 + f * 16 + t
                first = (k // per) * stride + p * 8 * per + 8 * (k % per)
                out[first : first + 8] = a
                if f == 0:
                    eta_s[m * T + 8 * t : m * T + 8 * t + 8] = a

    eta = eta_s[...]
    hi = eta.astype(jnp.bfloat16)
    rest = eta - hi.astype(F32)
    mid = rest.astype(jnp.bfloat16)
    low = (rest - mid.astype(F32)).astype(jnp.bfloat16)
    dot = lambda part: jnp.dot(part, pick_y[...], preferred_element_type=F32)
    seen = dot(hi) + (dot(mid) + dot(low))
    pick_x = lax.broadcasted_iota(jnp.int32, pick_y.shape, 0) == cell_x[...]
    logw = jnp.zeros((1, T), F32)
    for m in range(members):
        at = jnp.sum(jnp.where(pick_x, seen[m * T : (m + 1) * T], 0.0), axis=0, keepdims=True)
        miss = at - values[...]
        total = jnp.sum(miss * miss, axis=1, keepdims=True)
        logw = jnp.where(lanes((1, T)) == m, -0.5 * total / OBS_VAR, logw)
    for j in range(devices):
        out[(j + 1) * stride - 1 : (j + 1) * stride] = logw


def select_kernel(members, lineage, recv, out):
    pairs, rows = out.shape[0], out.shape[1]
    per = members // 2
    for k in range(pairs):
        pair = lineage[0, k]
        out[k] = recv[pl.ds(lax.div(pair, per) * (per * rows + 1) + lax.rem(pair, per) * rows, rows)]


def finish_kernel(members, back, recv, out, log_weights, result, sems):
    devices = back.shape[0]
    copies = [pltpu.make_async_copy(back.at[:, p], out.at[p], sems.at[p]) for p in range(members // 2)]
    for copy in copies:
        copy.start()
    stride = recv.shape[0] // devices
    logw = recv[pl.ds(stride - 1, devices, stride)]
    logw = jnp.where(lanes(logw.shape) < members, logw, -jnp.inf)
    peak = jnp.max(jnp.max(logw, axis=1, keepdims=True), axis=0, keepdims=True)
    total = jnp.sum(jnp.sum(jnp.exp(logw - peak), axis=1, keepdims=True), axis=0, keepdims=True)
    own = recv[pl.ds(lax.axis_index("mem") * stride + stride - 1, 1)]
    result[0] = (own - peak - jnp.log(total))[:, :members]
    last = pltpu.make_async_copy(result, log_weights, sems.at[members // 2])
    last.start()
    for copy in copies:
        copy.wait()
    last.wait()


VM = pl.BlockSpec(memory_space=pltpu.VMEM)
HB = pl.BlockSpec(memory_space=pltpu.MemorySpace.HBM)
PARAMS = pltpu.CompilerParams(vmem_limit_bytes=24 << 20)


def in_hbm(a):
    return pltpu.with_memory_space_constraint(a, pltpu.MemorySpace.HBM)


def sds(*shape):
    return jax.ShapeDtypeStruct(shape, F32)


def shards(fields, noise, ancestors, obs_cells, obs_values):
    members = fields.shape[0]
    devices = lax.axis_size("mem")
    total_y = T * lax.axis_size("gy")
    fields_vm, noise_vm, rowpack, colpack, ownrow, owncol = pl.pallas_call(
        pack_kernel,
        out_shape=(
            sds(*fields.shape),
            sds(*noise.shape),
            sds(3 * members + 1, 8, T),
            sds(8 * len(USED), T),
            sds(4, 2 * members, 8, T),
            sds(4, T, T),
        ),
        in_specs=[HB] * 2,
        out_specs=[VM] * 6,
        scratch_shapes=[pltpu.SemaphoreType.DMA((members + 1,))],
        compiler_params=PARAMS,
        name="pack",
    )(in_hbm(fields), in_hbm(noise))
    swap = [(0, 1), (1, 0)]
    colrecv = lax.ppermute(colpack, "gy", swap)
    rowrecv = lax.ppermute(rowpack, "gx", swap)
    count, pairs = obs_cells.shape[-1], ancestors.shape[-1]
    ownrow, owncol, inner, pick_y, cell_x, values, lineage = pl.pallas_call(
        functools.partial(interior_kernel, total_y),
        out_shape=(
            sds(4, 2 * members, 8, T),
            sds(4, T, T),
            sds(members, 3, T, T),
            jax.ShapeDtypeStruct((T, count), jnp.bfloat16),
            jax.ShapeDtypeStruct((1, count), jnp.int32),
            sds(1, count),
            jax.ShapeDtypeStruct((1, pairs), jnp.int32),
        ),
        in_specs=[VM] * 4 + [HB] * 3,
        out_specs=[VM] * 7,
        input_output_aliases={2: 0, 3: 1},
        scratch_shapes=[
            pltpu.VMEM((members, 3, T, T), F32),
            pltpu.VMEM((1, count), jnp.int32),
            pltpu.SemaphoreType.DMA((3,)),
        ],
        compiler_params=PARAMS,
        cost_estimate=pl.CostEstimate(flops=50_000_000, bytes_accessed=2_500_000, transcendentals=0),
        name="interior",
    )(
        fields_vm,
        noise_vm,
        ownrow,
        owncol,
        in_hbm(obs_cells.reshape(1, -1)),
        in_hbm(obs_values.reshape(1, -1)),
        in_hbm(ancestors.reshape(1, -1)),
    )
    colrecv, rowrecv, inner = lax.optimization_barrier((colrecv, rowrecv, inner))
    cornrecv = lax.ppermute(colrecv, "gx", swap)
    edge, cs, cs1 = pl.pallas_call(
        functools.partial(strips_kernel, total_y),
        out_shape=(sds(3, 2 * members, 8, T), sds(4, T + 16, T), sds(3, T + 16, T)),
        in_specs=[VM] * 4,
        out_specs=[VM] * 3,
        scratch_shapes=[pltpu.VMEM((4, T, T), F32), pltpu.VMEM((3, T, T), F32)],
        compiler_params=PARAMS,
        cost_estimate=pl.CostEstimate(flops=18_000_000, bytes_accessed=700_000, transcendentals=0),
        name="strips",
    )(ownrow, rowrecv, owncol, colrecv)
    rows = 768 // devices
    stride = members // 2 * rows + 1
    _, _, pieces = pl.pallas_call(
        functools.partial(merge_kernel, total_y, devices),
        out_shape=(sds(4, T + 16, T), sds(3, T + 16, T), sds(devices * stride, T)),
        in_specs=[VM] * 8,
        out_specs=[VM] * 3,
        input_output_aliases={2: 0, 3: 1},
        scratch_shapes=[pltpu.VMEM((members * T, T), F32)],
        compiler_params=PARAMS,
        name="merge",
    )(inner, edge, cs, cs1, cornrecv, pick_y, cell_x, values)
    held = lax.all_to_all(pieces.reshape(devices, stride, 1, T), "mem", 0, 0).reshape(devices * stride, T)
    picked = pl.pallas_call(
        functools.partial(select_kernel, members),
        out_shape=sds(pairs, rows, T),
        in_specs=[VM, VM],
        out_specs=VM,
        compiler_params=PARAMS,
        name="select",
    )(lineage, held)
    back = lax.all_to_all(picked.reshape(devices, members // 2, rows, T), "mem", 0, 0)
    resampled, log_weights = pl.pallas_call(
        functools.partial(finish_kernel, members),
        out_shape=(sds(members // 2, devices, rows, T), sds(1, 1, members)),
        in_specs=[VM, VM],
        out_specs=[HB, HB],
        scratch_shapes=[pltpu.VMEM((1, 1, members), F32), pltpu.SemaphoreType.DMA((members // 2 + 1,))],
        compiler_params=PARAMS,
        name="finish",
    )(back, held)
    return (resampled.reshape(fields.shape), log_weights)


def solution(mesh):
    return jax.shard_map(
        shards,
        mesh=mesh,
        in_specs=(
            P("mem", None, "gx", "gy"),
            P("mem", "gx", "gy"),
            P("gx", "gy", None),
            P("gx", "gy", None),
            P("gx", "gy", None),
        ),
        out_specs=(P("mem", None, "gx", "gy"), P("gx", "gy", "mem")),
        check_vma=False,
    )
```

```python
import functools

import jax
import jax.numpy as jnp
from jax import lax
from jax.experimental import pallas as pl
from jax.experimental.pallas import tpu as pltpu
from jax.sharding import PartitionSpec as P

COURANT = 0.3
NOISE_AMP = 0.1
OBS_VAR = 0.25
T = 128
F32 = jnp.float32
CHUNK = 128


def lanes(shape):
    return lax.broadcasted_iota(jnp.int32, shape, len(shape) - 1)


def subl(shape):
    return lax.broadcasted_iota(jnp.int32, shape, len(shape) - 2)


def lroll(a, shift):
    return pltpu.roll(a, shift % T, 1)


def rows_at(ref, lead, start, off, count, total):
    first = start + off
    if first < 0:
        return pltpu.roll(ref[(*lead, pl.ds(0, count))], -first, 0)
    if first + count > total:
        over = first + count - total
        return pltpu.roll(ref[(*lead, pl.ds(total - count, count))], count - over, 0)
    return ref[(*lead, pl.ds(first, count))]


def one_step(ref, lead, start, count, total, force, cor):
    get = lambda f, off: rows_at(ref, (*lead, f), start, off, count, total)
    cen, low, high = [], [], []
    dx, dy, loc, q = [], [], [], []
    for f in range(3):
        a, am, ap = get(f, 0), get(f, -1), get(f, 1)
        far = get(f, -2) + get(f, 2)
        cross = am + ap
        yp, ym = lroll(a, -1), lroll(a, 1)
        cen.append(a)
        low.append(am)
        high.append(ap)
        dx.append(ap - am)
        dy.append(yp - ym)
        loc.append(0.71 * a + (0.09 * cross - 0.005 * far))
        q.append(0.09 * a - (0.01 * cross + 0.005 * (yp + ym)))
    eta, u, v = cen
    half = 0.5 * COURANT
    hv = half * ((1.0 + eta) * v)
    hu = (1.0 + high[0]) * high[1] - (1.0 + low[0]) * low[1]
    new_eta = loc[0] + lroll(q[0] - hv, -1) + lroll(q[0] + hv, 1) - half * hu + NOISE_AMP * force
    tend_u = u * dx[1] + v * dy[1] + dx[0]
    tend_v = u * dx[2] + v * dy[2] + dy[0]
    new_u = loc[1] + (lroll(q[1], -1) + lroll(q[1], 1)) - half * tend_u + (COURANT * cor) * v
    new_v = loc[2] + (lroll(q[2], -1) + lroll(q[2], 1)) - half * tend_v - (COURANT * cor) * u
    return new_eta, new_u, new_v


def coriolis(cols, total_y):
    y = lax.rem(lax.axis_index("gy") * T + cols + total_y, total_y)
    return 0.1 + 0.2 * ((y.astype(F32) + 0.5) / total_y - 0.5)


def pack_kernel(fields_hbm, noise_hbm, fields, noise, rowpack, colpack, sems):
    members = fields.shape[0]
    copies = [pltpu.make_async_copy(noise_hbm, noise, sems.at[members])]
    for m in range(members):
        copies.append(pltpu.make_async_copy(fields_hbm.at[m], fields.at[m], sems.at[m]))
    for copy in copies:
        copy.start()
    copies[0].wait()
    top = subl((8, T)) < 4
    ln = lanes((T, T)) // 8
    for p in range(members // 2):
        rowpack[3 * members + p] = jnp.where(top, noise[p, 0:8], noise[p, T - 8 : T])
    acc = jnp.zeros((T, T), F32)
    for m in range(members):
        acc = jnp.where(ln == 4 * m + 3, lroll(noise[m // 2], 32 * m + 28), acc)
    for m in range(members):
        copies[1 + m].wait()
        for f in range(3):
            rowpack[3 * m + f] = jnp.where(top, fields[m, f, 0:8], fields[m, f, T - 8 : T])
            acc = jnp.where(ln == 4 * m + f, lroll(fields[m, f], 32 * m + 8 * f + 4), acc)
    colpack[...] = acc


def own_columns(tiles):
    shape = tiles[0].shape
    ln = lanes(shape) // 8
    acc = jnp.zeros(shape, F32)
    for m, a in enumerate(tiles):
        acc = jnp.where(ln == 4 * m, lroll(a, 32 * m + 8), acc)
        acc = jnp.where(ln == 4 * m + 3, lroll(a, 32 * m + 24), acc)
    return acc


def own_strips(fields, noise, ownrow, owncol):
    members = fields.shape[0]
    for f in range(4):
        tiles = [fields[m, f] if f < 3 else noise[m // 2] for m in range(members)]
        for m, a in enumerate(tiles):
            ownrow[f, 2 * m] = a[0:8]
            ownrow[f, 2 * m + 1] = a[T - 8 : T]
        owncol[f] = own_columns(tiles)


def interior(total_y, fields, noise, inner, tmp):
    cor = coriolis(lanes((1, T)), total_y)
    for src, dst in ((fields, tmp), (tmp, inner)):
        for m in range(fields.shape[0]):
            for r in range(0, T, CHUNK):
                new = one_step(src, (m,), r, CHUNK, T, noise[m // 2, r : r + CHUNK], cor)
                for f in range(3):
                    dst[m, f, r : r + CHUNK] = new[f]


def interior_kernel(total_y, fields, noise, cells_hbm, values_hbm, lineage_hbm,
                    ownrow, owncol, inner, pick_y, cell_x, values, lineage, tmp, cells, sems):
    members = fields.shape[0]
    copies = [
        pltpu.make_async_copy(cells_hbm, cells, sems.at[0]),
        pltpu.make_async_copy(values_hbm, values, sems.at[1]),
        pltpu.make_async_copy(lineage_hbm, lineage, sems.at[2]),
    ]
    for copy in copies:
        copy.start()

    own_strips(fields, noise, ownrow, owncol)
    interior(total_y, fields, noise, inner, tmp)
    for copy in copies:
        copy.wait()
    cell = cells[...]
    line_y = lax.broadcasted_iota(jnp.int32, pick_y.shape, 0)
    pick_y[...] = jnp.where(line_y == lax.rem(cell, T), 1.0, 0.0).astype(pick_y.dtype)
    cell_x[...] = cell // T


def twice(a, a1, total, cor):
    for src, dst in ((a, a1), (a1, a)):
        new = one_step(src, (), 0, total, total, a[3], cor)
        for f in range(3):
            dst[f, 0:total] = new[f]


def column_masks():
    l32 = lax.rem(lanes((1, T)), 32)
    cols = jnp.where(l32 < 16, l32 + 120, l32 - 24)
    return cols, (l32 >= 20) & (l32 < 24), (l32 >= 8) & (l32 < 12)


def with_halo(own, recv, f, is_low, is_high):
    return jnp.where(is_low, lroll(recv, 20 - 8 * f), jnp.where(is_high, lroll(recv, 4 - 8 * f), own))


def some_rows(src, dst, first, count, cor, force):
    new = one_step(src, (), first, count, T + 16, force[3, first : first + count], cor)
    for f in range(3):
        dst[f, first : first + count] = new[f]


def strips_kernel(total_y, ownrow, rowrecv, owncol, colrecv, edge, cs, cs1, rs, rs1):
    members = ownrow.shape[1] // 2
    cols, is_low, is_high = column_masks()
    halo = lambda m, f: rowrecv[3 * m + f] if f < 3 else rowrecv[3 * members + m // 2]
    for f in range(4):
        for m in range(members):
            rs[f, 32 * m : 32 * m + 8] = halo(m, f)
            rs[f, 32 * m + 8 : 32 * m + 16] = ownrow[f, 2 * m]
            rs[f, 32 * m + 16 : 32 * m + 24] = ownrow[f, 2 * m + 1]
            rs[f, 32 * m + 24 : 32 * m + 32] = halo(m, f)
        cs[f, 0:8] = own_columns([halo(m, f) for m in range(members)])
        cs[f, 8 : T + 8] = with_halo(owncol[f], colrecv[...], f, is_low, is_high)
    some_rows(cs, cs1, 16, T - 16, coriolis(cols, total_y), cs)
    twice(rs, rs1, T, coriolis(lanes((1, T)), total_y))
    for f in range(3):
        for m in range(members):
            edge[f, 2 * m] = rs[f, 32 * m + 8 : 32 * m + 16]
            edge[f, 2 * m + 1] = rs[f, 32 * m + 16 : 32 * m + 24]


def merge_kernel(total_y, devices, inner, edge, cs_in, cs1_in, cornrecv, pick_y, cell_x, values, cs, cs1, out, eta_s):
    members = inner.shape[0]
    cols, is_low, is_high = column_masks()
    cor_col = coriolis(cols, total_y)
    corn = jnp.where(subl((8, T)) < 4, cornrecv[0:8], cornrecv[T - 8 : T])
    for f in range(4):
        ends = with_halo(cs[f, 0:8], corn, f, is_low, is_high)
        cs[f, 0:8] = ends
        cs[f, T + 8 : T + 16] = ends
    some_rows(cs, cs1, 0, 16, cor_col, cs)
    some_rows(cs, cs1, T, 16, cor_col, cs)
    some_rows(cs1, cs, 8, T, cor_col, cs)

    per = 96 // devices
    stride = members // 2 * 8 * per + 1
    top = subl((8, T)) < 4
    left = lanes((8, T)) < 4
    right = lanes((8, T)) >= T - 4
    for m in range(members):
        p, mm = m // 2, m % 2
        for f in range(3):
            for t in range(T // 8):
                a = inner[m, f, 8 * t : 8 * t + 8]
                if t == 0:
                    a = jnp.where(top, edge[f, 2 * m], a)
                if t == T // 8 - 1:
                    a = jnp.where(top, a, edge[f, 2 * m + 1])
                col = cs[f, 8 * t + 8 : 8 * t + 16]
                a = jnp.where(left, lroll(col, 104 - 32 * m), a)
                a = jnp.where(right, lroll(col, 120 - 32 * m), a)
                k = mm * 48 + f * 16 + t
                first = (k // per) * stride + p * 8 * per + 8 * (k % per)
                out[first : first + 8] = a
                if f == 0:
                    eta_s[m * T + 8 * t : m * T + 8 * t + 8] = a

    eta = eta_s[...]
    hi = eta.astype(jnp.bfloat16)
    rest = eta - hi.astype(F32)
    mid = rest.astype(jnp.bfloat16)
    low = (rest - mid.astype(F32)).astype(jnp.bfloat16)
    dot = lambda part: jnp.dot(part, pick_y[...], preferred_element_type=F32)
    seen = dot(hi) + (dot(mid) + dot(low))
    pick_x = lax.broadcasted_iota(jnp.int32, pick_y.shape, 0) == cell_x[...]
    logw = jnp.zeros((1, T), F32)
    for m in range(members):
        at = jnp.sum(jnp.where(pick_x, seen[m * T : (m + 1) * T], 0.0), axis=0, keepdims=True)
        miss = at - values[...]
        total = jnp.sum(miss * miss, axis=1, keepdims=True)
        logw = jnp.where(lanes((1, T)) == m, -0.5 * total / OBS_VAR, logw)
    for j in range(devices):
        out[(j + 1) * stride - 1 : (j + 1) * stride] = logw


def select_kernel(members, lineage, recv, out):
    pairs, rows = out.shape[0], out.shape[1]
    per = members // 2
    for k in range(pairs):
        pair = lineage[0, k]
        out[k] = recv[pl.ds(lax.div(pair, per) * (per * rows + 1) + lax.rem(pair, per) * rows, rows)]


def finish_kernel(members, back, recv, out, log_weights, result, sems):
    devices = back.shape[0]
    copies = [pltpu.make_async_copy(back.at[:, p], out.at[p], sems.at[p]) for p in range(members // 2)]
    for copy in copies:
        copy.start()
    stride = recv.shape[0] // devices
    logw = recv[pl.ds(stride - 1, devices, stride)]
    logw = jnp.where(lanes(logw.shape) < members, logw, -jnp.inf)
    peak = jnp.max(jnp.max(logw, axis=1, keepdims=True), axis=0, keepdims=True)
    total = jnp.sum(jnp.sum(jnp.exp(logw - peak), axis=1, keepdims=True), axis=0, keepdims=True)
    own = recv[pl.ds(lax.axis_index("mem") * stride + stride - 1, 1)]
    result[0] = (own - peak - jnp.log(total))[:, :members]
    last = pltpu.make_async_copy(result, log_weights, sems.at[members // 2])
    last.start()
    for copy in copies:
        copy.wait()
    last.wait()


VM = pl.BlockSpec(memory_space=pltpu.VMEM)
HB = pl.BlockSpec(memory_space=pltpu.MemorySpace.HBM)
PARAMS = pltpu.CompilerParams(vmem_limit_bytes=24 << 20)


def in_hbm(a):
    return pltpu.with_memory_space_constraint(a, pltpu.MemorySpace.HBM)


def sds(*shape):
    return jax.ShapeDtypeStruct(shape, F32)


def shards(fields, noise, ancestors, obs_cells, obs_values):
    members = fields.shape[0]
    devices = lax.axis_size("mem")
    total_y = T * lax.axis_size("gy")
    fields_vm, noise_vm, rowpack, colpack = pl.pallas_call(
        pack_kernel,
        out_shape=(
            sds(*fields.shape),
            sds(*noise.shape),
            sds(3 * members + members // 2, 8, T),
            sds(T, T),
        ),
        in_specs=[HB] * 2,
        out_specs=[VM] * 4,
        scratch_shapes=[pltpu.SemaphoreType.DMA((members + 1,))],
        compiler_params=PARAMS,
        name="pack",
    )(in_hbm(fields), in_hbm(noise))
    swap = [(0, 1), (1, 0)]
    colrecv = lax.ppermute(colpack, "gy", swap)
    rowrecv = lax.ppermute(rowpack, "gx", swap)
    count, pairs = obs_cells.shape[-1], ancestors.shape[-1]
    ownrow, owncol, inner, pick_y, cell_x, values, lineage = pl.pallas_call(
        functools.partial(interior_kernel, total_y),
        out_shape=(
            sds(4, 2 * members, 8, T),
            sds(4, T, T),
            sds(members, 3, T, T),
            jax.ShapeDtypeStruct((T, count), jnp.bfloat16),
            jax.ShapeDtypeStruct((1, count), jnp.int32),
            sds(1, count),
            jax.ShapeDtypeStruct((1, pairs), jnp.int32),
        ),
        in_specs=[VM] * 2 + [HB] * 3,
        out_specs=[VM] * 7,
        scratch_shapes=[
            pltpu.VMEM((members, 3, T, T), F32),
            pltpu.VMEM((1, count), jnp.int32),
            pltpu.SemaphoreType.DMA((3,)),
        ],
        compiler_params=PARAMS,
        cost_estimate=pl.CostEstimate(flops=50_000_000, bytes_accessed=2_500_000, transcendentals=0),
        name="interior",
    )(
        fields_vm,
        noise_vm,
        in_hbm(obs_cells.reshape(1, -1)),
        in_hbm(obs_values.reshape(1, -1)),
        in_hbm(ancestors.reshape(1, -1)),
    )
    colrecv, rowrecv, inner = lax.optimization_barrier((colrecv, rowrecv, inner))
    cornrecv = lax.ppermute(colrecv, "gx", swap)
    edge, cs, cs1 = pl.pallas_call(
        functools.partial(strips_kernel, total_y),
        out_shape=(sds(3, 2 * members, 8, T), sds(4, T + 16, T), sds(3, T + 16, T)),
        in_specs=[VM] * 4,
        out_specs=[VM] * 3,
        scratch_shapes=[pltpu.VMEM((4, T, T), F32), pltpu.VMEM((3, T, T), F32)],
        compiler_params=PARAMS,
        cost_estimate=pl.CostEstimate(flops=18_000_000, bytes_accessed=700_000, transcendentals=0),
        name="strips",
    )(ownrow, rowrecv, owncol, colrecv)
    rows = 768 // devices
    stride = members // 2 * rows + 1
    _, _, pieces = pl.pallas_call(
        functools.partial(merge_kernel, total_y, devices),
        out_shape=(sds(4, T + 16, T), sds(3, T + 16, T), sds(devices * stride, T)),
        in_specs=[VM] * 8,
        out_specs=[VM] * 3,
        input_output_aliases={2: 0, 3: 1},
        scratch_shapes=[pltpu.VMEM((members * T, T), F32)],
        compiler_params=PARAMS,
        name="merge",
    )(inner, edge, cs, cs1, cornrecv, pick_y, cell_x, values)
    held = lax.all_to_all(pieces.reshape(devices, stride, 1, T), "mem", 0, 0).reshape(devices * stride, T)
    picked = pl.pallas_call(
        functools.partial(select_kernel, members),
        out_shape=sds(pairs, rows, T),
        in_specs=[VM, VM],
        out_specs=VM,
        compiler_params=PARAMS,
        name="select",
    )(lineage, held)
    back = lax.all_to_all(picked.reshape(devices, members // 2, rows, T), "mem", 0, 0)
    resampled, log_weights = pl.pallas_call(
        functools.partial(finish_kernel, members),
        out_shape=(sds(members // 2, devices, rows, T), sds(1, 1, members)),
        in_specs=[VM, VM],
        out_specs=[HB, HB],
        scratch_shapes=[pltpu.VMEM((1, 1, members), F32), pltpu.SemaphoreType.DMA((members // 2 + 1,))],
        compiler_params=PARAMS,
        name="finish",
    )(back, held)
    return (resampled.reshape(fields.shape), log_weights)


def solution(mesh):
    return jax.shard_map(
        shards,
        mesh=mesh,
        in_specs=(
            P("mem", None, "gx", "gy"),
            P("mem", "gx", "gy"),
            P("gx", "gy", None),
            P("gx", "gy", None),
            P("gx", "gy", None),
        ),
        out_specs=(P("mem", None, "gx", "gy"), P("gx", "gy", "mem")),
        check_vma=False,
    )
```

```python
import functools

import jax
import jax.numpy as jnp
from jax import lax
from jax.experimental import pallas as pl
from jax.experimental.pallas import tpu as pltpu
from jax.sharding import PartitionSpec as P

COURANT = 0.3
NOISE_AMP = 0.1
OBS_VAR = 0.25
T = 128
F32 = jnp.float32
CHUNK = 128


def lanes(shape):
    return lax.broadcasted_iota(jnp.int32, shape, len(shape) - 1)


def subl(shape):
    return lax.broadcasted_iota(jnp.int32, shape, len(shape) - 2)


def lroll(a, shift):
    return pltpu.roll(a, shift % T, 1)


def rows_at(ref, lead, start, off, count, total):
    first = start + off
    if first < 0:
        return pltpu.roll(ref[(*lead, pl.ds(0, count))], -first, 0)
    if first + count > total:
        over = first + count - total
        return pltpu.roll(ref[(*lead, pl.ds(total - count, count))], count - over, 0)
    return ref[(*lead, pl.ds(first, count))]


def one_step(ref, lead, start, count, total, force, cor):
    get = lambda f, off: rows_at(ref, (*lead, f), start, off, count, total)
    cen, low, high = [], [], []
    dx, dy, loc, q = [], [], [], []
    for f in range(3):
        a, am, ap = get(f, 0), get(f, -1), get(f, 1)
        far = get(f, -2) + get(f, 2)
        cross = am + ap
        yp, ym = lroll(a, -1), lroll(a, 1)
        cen.append(a)
        low.append(am)
        high.append(ap)
        dx.append(ap - am)
        dy.append(yp - ym)
        loc.append(0.71 * a + (0.09 * cross - 0.005 * far))
        q.append(0.09 * a - (0.01 * cross + 0.005 * (yp + ym)))
    eta, u, v = cen
    half = 0.5 * COURANT
    hv = half * ((1.0 + eta) * v)
    hu = (1.0 + high[0]) * high[1] - (1.0 + low[0]) * low[1]
    new_eta = loc[0] + lroll(q[0] - hv, -1) + lroll(q[0] + hv, 1) - half * hu + NOISE_AMP * force
    tend_u = u * dx[1] + v * dy[1] + dx[0]
    tend_v = u * dx[2] + v * dy[2] + dy[0]
    new_u = loc[1] + (lroll(q[1], -1) + lroll(q[1], 1)) - half * tend_u + (COURANT * cor) * v
    new_v = loc[2] + (lroll(q[2], -1) + lroll(q[2], 1)) - half * tend_v - (COURANT * cor) * u
    return new_eta, new_u, new_v


def coriolis(cols, total_y):
    y = lax.rem(lax.axis_index("gy") * T + cols + total_y, total_y)
    return 0.1 + 0.2 * ((y.astype(F32) + 0.5) / total_y - 0.5)


def pack_kernel(fields_hbm, noise_hbm, fields, noise, rowpack, colpack, sems):
    members = fields.shape[0]
    half = members // 2
    copies = [pltpu.make_async_copy(noise_hbm, noise, sems.at[2])]
    for i in range(2):
        part = slice(i * half, (i + 1) * half)
        copies.append(pltpu.make_async_copy(fields_hbm.at[part], fields.at[part], sems.at[i]))
    for copy in copies:
        copy.start()
    copies[0].wait()
    top = subl((8, T)) < 4
    ln = lanes((T, T)) // 8
    for p in range(members // 2):
        rowpack[3 * members + p] = jnp.where(top, noise[p, 0:8], noise[p, T - 8 : T])
    acc = jnp.zeros((T, T), F32)
    for m in range(members):
        acc = jnp.where(ln == 4 * m + 3, lroll(noise[m // 2], 32 * m + 28), acc)
    for m in range(members):
        if m % half == 0:
            copies[1 + m // half].wait()
        for f in range(3):
            rowpack[3 * m + f] = jnp.where(top, fields[m, f, 0:8], fields[m, f, T - 8 : T])
            acc = jnp.where(ln == 4 * m + f, lroll(fields[m, f], 32 * m + 8 * f + 4), acc)
    colpack[...] = acc


def own_columns(tiles, every=1):
    shape = tiles[0].shape
    ln = lanes(shape) // 8
    acc = jnp.zeros(shape, F32)
    for m in range(0, len(tiles), every):
        a = tiles[m]
        acc = jnp.where(ln == 4 * m, lroll(a, 32 * m + 8), acc)
        acc = jnp.where(ln == 4 * m + 3, lroll(a, 32 * m + 24), acc)
    return acc


def own_strips(fields, noise, ownrow, owncol):
    members = fields.shape[0]
    for f in range(4):
        tiles = [fields[m, f] if f < 3 else noise[m // 2] for m in range(members)]
        for m, a in enumerate(tiles):
            ownrow[f, 2 * m] = a[0:8]
            ownrow[f, 2 * m + 1] = a[T - 8 : T]
        if f < 3:
            owncol[f] = own_columns(tiles)
        else:
            even = own_columns(tiles, 2)
            owncol[f] = even + lroll(even, 32)


def interior(total_y, fields, noise, inner, tmp):
    cor = coriolis(lanes((1, T)), total_y)
    for src, dst in ((fields, tmp), (tmp, inner)):
        for m in range(fields.shape[0]):
            for r in range(0, T, CHUNK):
                new = one_step(src, (m,), r, CHUNK, T, noise[m // 2, r : r + CHUNK], cor)
                for f in range(3):
                    dst[m, f, r : r + CHUNK] = new[f]


def interior_kernel(total_y, fields, noise, cells_hbm, values_hbm, lineage_hbm,
                    ownrow, owncol, inner, pick_y, cell_x, values, lineage, tmp, cells, sems):
    members = fields.shape[0]
    copies = [
        pltpu.make_async_copy(cells_hbm, cells, sems.at[0]),
        pltpu.make_async_copy(values_hbm, values, sems.at[1]),
        pltpu.make_async_copy(lineage_hbm, lineage, sems.at[2]),
    ]
    for copy in copies:
        copy.start()

    own_strips(fields, noise, ownrow, owncol)
    interior(total_y, fields, noise, inner, tmp)
    for copy in copies:
        copy.wait()
    cell = cells[...]
    line_y = lax.broadcasted_iota(jnp.int32, pick_y.shape, 0)
    pick_y[...] = jnp.where(line_y == lax.rem(cell, T), 1.0, 0.0).astype(pick_y.dtype)
    cell_x[...] = cell // T


def twice(a, a1, total, cor):
    for src, dst in ((a, a1), (a1, a)):
        new = one_step(src, (), 0, total, total, a[3], cor)
        for f in range(3):
            dst[f, 0:total] = new[f]


def column_masks():
    l32 = lax.rem(lanes((1, T)), 32)
    cols = jnp.where(l32 < 16, l32 + 120, l32 - 24)
    return cols, (l32 >= 20) & (l32 < 24), (l32 >= 8) & (l32 < 12)


def with_halo(own, recv, f, is_low, is_high):
    return jnp.where(is_low, lroll(recv, 20 - 8 * f), jnp.where(is_high, lroll(recv, 4 - 8 * f), own))


def some_rows(src, dst, first, count, cor, force):
    new = one_step(src, (), first, count, T + 16, force[3, first : first + count], cor)
    for f in range(3):
        dst[f, first : first + count] = new[f]


def strips_kernel(total_y, ownrow, rowrecv, owncol, colrecv, edge, cs, cs1, rs, rs1):
    members = ownrow.shape[1] // 2
    cols, is_low, is_high = column_masks()
    halo = lambda m, f: rowrecv[3 * m + f] if f < 3 else rowrecv[3 * members + m // 2]
    for f in range(4):
        for m in range(members):
            rs[f, 32 * m : 32 * m + 8] = halo(m, f)
            rs[f, 32 * m + 8 : 32 * m + 16] = ownrow[f, 2 * m]
            rs[f, 32 * m + 16 : 32 * m + 24] = ownrow[f, 2 * m + 1]
            rs[f, 32 * m + 24 : 32 * m + 32] = halo(m, f)
        cs[f, 0:8] = own_columns([halo(m, f) for m in range(members)])
        cs[f, 8 : T + 8] = with_halo(owncol[f], colrecv[...], f, is_low, is_high)
    some_rows(cs, cs1, 16, T - 16, coriolis(cols, total_y), cs)
    twice(rs, rs1, T, coriolis(lanes((1, T)), total_y))
    for f in range(3):
        for m in range(members):
            edge[f, 2 * m] = rs[f, 32 * m + 8 : 32 * m + 16]
            edge[f, 2 * m + 1] = rs[f, 32 * m + 16 : 32 * m + 24]


def merge_kernel(total_y, devices, inner, edge, cs_in, cs1_in, cornrecv, pick_y, cell_x, values, cs, cs1, out, eta_s):
    members = inner.shape[0]
    cols, is_low, is_high = column_masks()
    cor_col = coriolis(cols, total_y)
    corn = jnp.where(subl((8, T)) < 4, cornrecv[0:8], cornrecv[T - 8 : T])
    for f in range(4):
        ends = with_halo(cs[f, 0:8], corn, f, is_low, is_high)
        cs[f, 0:8] = ends
        cs[f, T + 8 : T + 16] = ends
    some_rows(cs, cs1, 0, 16, cor_col, cs)
    some_rows(cs, cs1, T, 16, cor_col, cs)
    some_rows(cs1, cs, 8, T, cor_col, cs)

    per = 96 // devices
    stride = members // 2 * 8 * per + 1
    top = subl((8, T)) < 4
    left = lanes((8, T)) < 4
    right = lanes((8, T)) >= T - 4
    for m in range(members):
        p, mm = m // 2, m % 2
        for f in range(3):
            for t in range(T // 8):
                a = inner[m, f, 8 * t : 8 * t + 8]
                if t == 0:
                    a = jnp.where(top, edge[f, 2 * m], a)
                if t == T // 8 - 1:
                    a = jnp.where(top, a, edge[f, 2 * m + 1])
                col = cs[f, 8 * t + 8 : 8 * t + 16]
                a = jnp.where(left, lroll(col, 104 - 32 * m), a)
                a = jnp.where(right, lroll(col, 120 - 32 * m), a)
                k = mm * 48 + f * 16 + t
                first = (k // per) * stride + p * 8 * per + 8 * (k % per)
                out[first : first + 8] = a
                if f == 0:
                    eta_s[m * T + 8 * t : m * T + 8 * t + 8] = a

    eta = eta_s[...]
    hi = eta.astype(jnp.bfloat16)
    rest = eta - hi.astype(F32)
    mid = rest.astype(jnp.bfloat16)
    low = (rest - mid.astype(F32)).astype(jnp.bfloat16)
    dot = lambda part: jnp.dot(part, pick_y[...], preferred_element_type=F32)
    seen = dot(hi) + (dot(mid) + dot(low))
    pick_x = lax.broadcasted_iota(jnp.int32, pick_y.shape, 0) == cell_x[...]
    logw = jnp.zeros((1, T), F32)
    for m in range(members):
        at = jnp.sum(jnp.where(pick_x, seen[m * T : (m + 1) * T], 0.0), axis=0, keepdims=True)
        miss = at - values[...]
        total = jnp.sum(miss * miss, axis=1, keepdims=True)
        logw = jnp.where(lanes((1, T)) == m, -0.5 * total / OBS_VAR, logw)
    for j in range(devices):
        out[(j + 1) * stride - 1 : (j + 1) * stride] = logw


def select_kernel(members, lineage, recv, out):
    pairs, rows = out.shape[0], out.shape[1]
    per = members // 2
    for k in range(pairs):
        pair = lineage[0, k]
        out[k] = recv[pl.ds(lax.div(pair, per) * (per * rows + 1) + lax.rem(pair, per) * rows, rows)]


def finish_kernel(members, back, recv, out, log_weights, result, sems):
    devices = back.shape[0]
    copies = [pltpu.make_async_copy(back.at[:, p], out.at[p], sems.at[p]) for p in range(members // 2)]
    for copy in copies:
        copy.start()
    stride = recv.shape[0] // devices
    logw = recv[pl.ds(stride - 1, devices, stride)]
    logw = jnp.where(lanes(logw.shape) < members, logw, -jnp.inf)
    peak = jnp.max(jnp.max(logw, axis=1, keepdims=True), axis=0, keepdims=True)
    total = jnp.sum(jnp.sum(jnp.exp(logw - peak), axis=1, keepdims=True), axis=0, keepdims=True)
    own = recv[pl.ds(lax.axis_index("mem") * stride + stride - 1, 1)]
    result[0] = (own - peak - jnp.log(total))[:, :members]
    last = pltpu.make_async_copy(result, log_weights, sems.at[members // 2])
    last.start()
    for copy in copies:
        copy.wait()
    last.wait()


VM = pl.BlockSpec(memory_space=pltpu.VMEM)
HB = pl.BlockSpec(memory_space=pltpu.MemorySpace.HBM)
PARAMS = pltpu.CompilerParams(vmem_limit_bytes=24 << 20)


def in_hbm(a):
    return pltpu.with_memory_space_constraint(a, pltpu.MemorySpace.HBM)


def sds(*shape):
    return jax.ShapeDtypeStruct(shape, F32)


def shards(fields, noise, ancestors, obs_cells, obs_values):
    members = fields.shape[0]
    devices = lax.axis_size("mem")
    total_y = T * lax.axis_size("gy")
    fields_vm, noise_vm, rowpack, colpack = pl.pallas_call(
        pack_kernel,
        out_shape=(
            sds(*fields.shape),
            sds(*noise.shape),
            sds(3 * members + members // 2, 8, T),
            sds(T, T),
        ),
        in_specs=[HB] * 2,
        out_specs=[VM] * 4,
        scratch_shapes=[pltpu.SemaphoreType.DMA((3,))],
        compiler_params=PARAMS,
        name="pack",
    )(in_hbm(fields), in_hbm(noise))
    swap = [(0, 1), (1, 0)]
    colrecv = lax.ppermute(colpack, "gy", swap)
    rowrecv = lax.ppermute(rowpack, "gx", swap)
    count, pairs = obs_cells.shape[-1], ancestors.shape[-1]
    ownrow, owncol, inner, pick_y, cell_x, values, lineage = pl.pallas_call(
        functools.partial(interior_kernel, total_y),
        out_shape=(
            sds(4, 2 * members, 8, T),
            sds(4, T, T),
            sds(members, 3, T, T),
            jax.ShapeDtypeStruct((T, count), jnp.bfloat16),
            jax.ShapeDtypeStruct((1, count), jnp.int32),
            sds(1, count),
            jax.ShapeDtypeStruct((1, pairs), jnp.int32),
        ),
        in_specs=[VM] * 2 + [HB] * 3,
        out_specs=[VM] * 7,
        scratch_shapes=[
            pltpu.VMEM((members, 3, T, T), F32),
            pltpu.VMEM((1, count), jnp.int32),
            pltpu.SemaphoreType.DMA((3,)),
        ],
        compiler_params=PARAMS,
        cost_estimate=pl.CostEstimate(flops=50_000_000, bytes_accessed=2_500_000, transcendentals=0),
        name="interior",
    )(
        fields_vm,
        noise_vm,
        in_hbm(obs_cells.reshape(1, -1)),
        in_hbm(obs_values.reshape(1, -1)),
        in_hbm(ancestors.reshape(1, -1)),
    )
    colrecv, rowrecv, inner = lax.optimization_barrier((colrecv, rowrecv, inner))
    cornrecv = lax.ppermute(colrecv, "gx", swap)
    edge, cs, cs1 = pl.pallas_call(
        functools.partial(strips_kernel, total_y),
        out_shape=(sds(3, 2 * members, 8, T), sds(4, T + 16, T), sds(3, T + 16, T)),
        in_specs=[VM] * 4,
        out_specs=[VM] * 3,
        scratch_shapes=[pltpu.VMEM((4, T, T), F32), pltpu.VMEM((3, T, T), F32)],
        compiler_params=PARAMS,
        cost_estimate=pl.CostEstimate(flops=18_000_000, bytes_accessed=700_000, transcendentals=0),
        name="strips",
    )(ownrow, rowrecv, owncol, colrecv)
    rows = 768 // devices
    stride = members // 2 * rows + 1
    _, _, pieces = pl.pallas_call(
        functools.partial(merge_kernel, total_y, devices),
        out_shape=(sds(4, T + 16, T), sds(3, T + 16, T), sds(devices * stride, T)),
        in_specs=[VM] * 8,
        out_specs=[VM] * 3,
        input_output_aliases={2: 0, 3: 1},
        scratch_shapes=[pltpu.VMEM((members * T, T), F32)],
        compiler_params=PARAMS,
        name="merge",
    )(inner, edge, cs, cs1, cornrecv, pick_y, cell_x, values)
    held = lax.all_to_all(pieces.reshape(devices, stride, 1, T), "mem", 0, 0).reshape(devices * stride, T)
    picked = pl.pallas_call(
        functools.partial(select_kernel, members),
        out_shape=sds(pairs, rows, T),
        in_specs=[VM, VM],
        out_specs=VM,
        compiler_params=PARAMS,
        name="select",
    )(lineage, held)
    back = lax.all_to_all(picked.reshape(devices, members // 2, rows, T), "mem", 0, 0)
    resampled, log_weights = pl.pallas_call(
        functools.partial(finish_kernel, members),
        out_shape=(sds(members // 2, devices, rows, T), sds(1, 1, members)),
        in_specs=[VM, VM],
        out_specs=[HB, HB],
        scratch_shapes=[pltpu.VMEM((1, 1, members), F32), pltpu.SemaphoreType.DMA((members // 2 + 1,))],
        compiler_params=PARAMS,
        name="finish",
    )(back, held)
    return (resampled.reshape(fields.shape), log_weights)


def solution(mesh):
    return jax.shard_map(
        shards,
        mesh=mesh,
        in_specs=(
            P("mem", None, "gx", "gy"),
            P("mem", "gx", "gy"),
            P("gx", "gy", None),
            P("gx", "gy", None),
            P("gx", "gy", None),
        ),
        out_specs=(P("mem", None, "gx", "gy"), P("gx", "gy", "mem")),
        check_vma=False,
    )
```

```python
import functools

import jax
import jax.numpy as jnp
from jax import lax
from jax.experimental import pallas as pl
from jax.experimental.pallas import tpu as pltpu
from jax.sharding import PartitionSpec as P

COURANT = 0.3
NOISE_AMP = 0.1
OBS_VAR = 0.25
T = 128
F32 = jnp.float32
CHUNK = 128


def lanes(shape):
    return lax.broadcasted_iota(jnp.int32, shape, len(shape) - 1)


def subl(shape):
    return lax.broadcasted_iota(jnp.int32, shape, len(shape) - 2)


def lroll(a, shift):
    return pltpu.roll(a, shift % T, 1)


def rows_at(ref, lead, start, off, count, total):
    first = start + off
    if first < 0:
        return pltpu.roll(ref[(*lead, pl.ds(0, count))], -first, 0)
    if first + count > total:
        over = first + count - total
        return pltpu.roll(ref[(*lead, pl.ds(total - count, count))], count - over, 0)
    return ref[(*lead, pl.ds(first, count))]


def one_step(ref, lead, start, count, total, force, cor):
    get = lambda f, off: rows_at(ref, (*lead, f), start, off, count, total)
    cen, low, high = [], [], []
    dx, dy, loc, q = [], [], [], []
    for f in range(3):
        a, am, ap = get(f, 0), get(f, -1), get(f, 1)
        far = get(f, -2) + get(f, 2)
        cross = am + ap
        yp, ym = lroll(a, -1), lroll(a, 1)
        cen.append(a)
        low.append(am)
        high.append(ap)
        dx.append(ap - am)
        dy.append(yp - ym)
        loc.append(0.71 * a + (0.09 * cross - 0.005 * far))
        q.append(0.09 * a - (0.01 * cross + 0.005 * (yp + ym)))
    eta, u, v = cen
    half = 0.5 * COURANT
    hv = half * ((1.0 + eta) * v)
    hu = (1.0 + high[0]) * high[1] - (1.0 + low[0]) * low[1]
    new_eta = loc[0] + lroll(q[0] - hv, -1) + lroll(q[0] + hv, 1) - half * hu + NOISE_AMP * force
    tend_u = u * dx[1] + v * dy[1] + dx[0]
    tend_v = u * dx[2] + v * dy[2] + dy[0]
    new_u = loc[1] + (lroll(q[1], -1) + lroll(q[1], 1)) - half * tend_u + (COURANT * cor) * v
    new_v = loc[2] + (lroll(q[2], -1) + lroll(q[2], 1)) - half * tend_v - (COURANT * cor) * u
    return new_eta, new_u, new_v


def coriolis(cols, total_y):
    y = lax.rem(lax.axis_index("gy") * T + cols + total_y, total_y)
    return 0.1 + 0.2 * ((y.astype(F32) + 0.5) / total_y - 0.5)


def pack_kernel(fields_hbm, noise_hbm, fields, noise, rowpack, colpack, ownrow, owncol, sems):
    members = fields.shape[0]
    half = members // 2
    copies = [pltpu.make_async_copy(noise_hbm, noise, sems.at[2])]
    for i in range(2):
        part = slice(i * half, (i + 1) * half)
        copies.append(pltpu.make_async_copy(fields_hbm.at[part], fields.at[part], sems.at[i]))
    for copy in copies:
        copy.start()
    copies[0].wait()
    top = subl((8, T)) < 4
    ln = lanes((T, T)) // 8
    for p in range(members // 2):
        rowpack[3 * members + p] = jnp.where(top, noise[p, 0:8], noise[p, T - 8 : T])
    acc = jnp.zeros((T, T), F32)
    for m in range(members):
        acc = jnp.where(ln == 4 * m + 3, lroll(noise[m // 2], 32 * m + 28), acc)
    for m in range(members):
        if m % half == 0:
            copies[1 + m // half].wait()
        for f in range(3):
            rowpack[3 * m + f] = jnp.where(top, fields[m, f, 0:8], fields[m, f, T - 8 : T])
            acc = jnp.where(ln == 4 * m + f, lroll(fields[m, f], 32 * m + 8 * f + 4), acc)
    colpack[...] = acc

    @pl.when(strips_first())
    def _():
        own_strips(fields, noise, ownrow, owncol)


def strips_first():
    return (lax.axis_index("gx") != 0) & (lax.axis_index("gy") == 0)


def own_columns(tiles, every=1):
    shape = tiles[0].shape
    ln = lanes(shape) // 8
    acc = jnp.zeros(shape, F32)
    for m in range(0, len(tiles), every):
        a = tiles[m]
        acc = jnp.where(ln == 4 * m, lroll(a, 32 * m + 8), acc)
        acc = jnp.where(ln == 4 * m + 3, lroll(a, 32 * m + 24), acc)
    return acc


def own_strips(fields, noise, ownrow, owncol):
    members = fields.shape[0]
    for f in range(4):
        tiles = [fields[m, f] if f < 3 else noise[m // 2] for m in range(members)]
        for m, a in enumerate(tiles):
            ownrow[f, 2 * m] = a[0:8]
            ownrow[f, 2 * m + 1] = a[T - 8 : T]
        if f < 3:
            owncol[f] = own_columns(tiles)
        else:
            even = own_columns(tiles, 2)
            owncol[f] = even + lroll(even, 32)


def interior(total_y, fields, noise, inner, tmp):
    cor = coriolis(lanes((1, T)), total_y)
    for src, dst in ((fields, tmp), (tmp, inner)):
        for m in range(fields.shape[0]):
            for r in range(0, T, CHUNK):
                new = one_step(src, (m,), r, CHUNK, T, noise[m // 2, r : r + CHUNK], cor)
                for f in range(3):
                    dst[m, f, r : r + CHUNK] = new[f]


def interior_kernel(total_y, fields, noise, ownrow_in, owncol_in, cells_hbm, values_hbm, lineage_hbm,
                    ownrow, owncol, inner, pick_y, cell_x, values, lineage, tmp, cells, sems):
    members = fields.shape[0]
    copies = [
        pltpu.make_async_copy(cells_hbm, cells, sems.at[0]),
        pltpu.make_async_copy(values_hbm, values, sems.at[1]),
        pltpu.make_async_copy(lineage_hbm, lineage, sems.at[2]),
    ]
    for copy in copies:
        copy.start()

    @pl.when(jnp.logical_not(strips_first()))
    def _():
        own_strips(fields, noise, ownrow, owncol)

    interior(total_y, fields, noise, inner, tmp)
    for copy in copies:
        copy.wait()
    cell = cells[...]
    line_y = lax.broadcasted_iota(jnp.int32, pick_y.shape, 0)
    pick_y[...] = jnp.where(line_y == lax.rem(cell, T), 1.0, 0.0).astype(pick_y.dtype)
    cell_x[...] = cell // T


def twice(a, a1, total, cor):
    for src, dst in ((a, a1), (a1, a)):
        new = one_step(src, (), 0, total, total, a[3], cor)
        for f in range(3):
            dst[f, 0:total] = new[f]


def column_masks():
    l32 = lax.rem(lanes((1, T)), 32)
    cols = jnp.where(l32 < 16, l32 + 120, l32 - 24)
    return cols, (l32 >= 20) & (l32 < 24), (l32 >= 8) & (l32 < 12)


def with_halo(own, recv, f, is_low, is_high):
    return jnp.where(is_low, lroll(recv, 20 - 8 * f), jnp.where(is_high, lroll(recv, 4 - 8 * f), own))


def some_rows(src, dst, first, count, cor, force):
    new = one_step(src, (), first, count, T + 16, force[3, first : first + count], cor)
    for f in range(3):
        dst[f, first : first + count] = new[f]


def strips_kernel(total_y, ownrow, rowrecv, owncol, colrecv, edge, cs, cs1, rs, rs1):
    members = ownrow.shape[1] // 2
    cols, is_low, is_high = column_masks()
    halo = lambda m, f: rowrecv[3 * m + f] if f < 3 else rowrecv[3 * members + m // 2]
    for f in range(4):
        for m in range(members):
            rs[f, 32 * m : 32 * m + 8] = halo(m, f)
            rs[f, 32 * m + 8 : 32 * m + 16] = ownrow[f, 2 * m]
            rs[f, 32 * m + 16 : 32 * m + 24] = ownrow[f, 2 * m + 1]
            rs[f, 32 * m + 24 : 32 * m + 32] = halo(m, f)
        cs[f, 0:8] = own_columns([halo(m, f) for m in range(members)])
        cs[f, 8 : T + 8] = with_halo(owncol[f], colrecv[...], f, is_low, is_high)
    some_rows(cs, cs1, 16, T - 16, coriolis(cols, total_y), cs)
    twice(rs, rs1, T, coriolis(lanes((1, T)), total_y))
    for f in range(3):
        for m in range(members):
            edge[f, 2 * m] = rs[f, 32 * m + 8 : 32 * m + 16]
            edge[f, 2 * m + 1] = rs[f, 32 * m + 16 : 32 * m + 24]


def merge_kernel(total_y, devices, inner, edge, cs_in, cs1_in, cornrecv, pick_y, cell_x, values, cs, cs1, out, eta_s):
    members = inner.shape[0]
    cols, is_low, is_high = column_masks()
    cor_col = coriolis(cols, total_y)
    corn = jnp.where(subl((8, T)) < 4, cornrecv[0:8], cornrecv[T - 8 : T])
    for f in range(4):
        ends = with_halo(cs[f, 0:8], corn, f, is_low, is_high)
        cs[f, 0:8] = ends
        cs[f, T + 8 : T + 16] = ends
    some_rows(cs, cs1, 0, 16, cor_col, cs)
    some_rows(cs, cs1, T, 16, cor_col, cs)
    some_rows(cs1, cs, 8, T, cor_col, cs)

    per = 96 // devices
    stride = members // 2 * 8 * per + 1
    top = subl((8, T)) < 4
    left = lanes((8, T)) < 4
    right = lanes((8, T)) >= T - 4
    for m in range(members):
        p, mm = m // 2, m % 2
        for f in range(3):
            for t in range(T // 8):
                a = inner[m, f, 8 * t : 8 * t + 8]
                if t == 0:
                    a = jnp.where(top, edge[f, 2 * m], a)
                if t == T // 8 - 1:
                    a = jnp.where(top, a, edge[f, 2 * m + 1])
                col = cs[f, 8 * t + 8 : 8 * t + 16]
                a = jnp.where(left, lroll(col, 104 - 32 * m), a)
                a = jnp.where(right, lroll(col, 120 - 32 * m), a)
                k = mm * 48 + f * 16 + t
                first = (k // per) * stride + p * 8 * per + 8 * (k % per)
                out[first : first + 8] = a
                if f == 0:
                    eta_s[m * T + 8 * t : m * T + 8 * t + 8] = a

    eta = eta_s[...]
    hi = eta.astype(jnp.bfloat16)
    rest = eta - hi.astype(F32)
    mid = rest.astype(jnp.bfloat16)
    low = (rest - mid.astype(F32)).astype(jnp.bfloat16)
    dot = lambda part: jnp.dot(part, pick_y[...], preferred_element_type=F32)
    seen = dot(hi) + (dot(mid) + dot(low))
    pick_x = lax.broadcasted_iota(jnp.int32, pick_y.shape, 0) == cell_x[...]
    logw = jnp.zeros((1, T), F32)
    for m in range(members):
        at = jnp.sum(jnp.where(pick_x, seen[m * T : (m + 1) * T], 0.0), axis=0, keepdims=True)
        miss = at - values[...]
        total = jnp.sum(miss * miss, axis=1, keepdims=True)
        logw = jnp.where(lanes((1, T)) == m, -0.5 * total / OBS_VAR, logw)
    for j in range(devices):
        out[(j + 1) * stride - 1 : (j + 1) * stride] = logw


def select_kernel(members, lineage, recv, out):
    pairs, rows = out.shape[0], out.shape[1]
    per = members // 2
    for k in range(pairs):
        pair = lineage[0, k]
        out[k] = recv[pl.ds(lax.div(pair, per) * (per * rows + 1) + lax.rem(pair, per) * rows, rows)]


def finish_kernel(members, back, recv, out, log_weights, result, sems):
    devices = back.shape[0]
    copies = [pltpu.make_async_copy(back.at[:, p], out.at[p], sems.at[p]) for p in range(members // 2)]
    for copy in copies:
        copy.start()
    stride = recv.shape[0] // devices
    logw = recv[pl.ds(stride - 1, devices, stride)]
    logw = jnp.where(lanes(logw.shape) < members, logw, -jnp.inf)
    peak = jnp.max(jnp.max(logw, axis=1, keepdims=True), axis=0, keepdims=True)
    total = jnp.sum(jnp.sum(jnp.exp(logw - peak), axis=1, keepdims=True), axis=0, keepdims=True)
    own = recv[pl.ds(lax.axis_index("mem") * stride + stride - 1, 1)]
    result[0] = (own - peak - jnp.log(total))[:, :members]
    last = pltpu.make_async_copy(result, log_weights, sems.at[members // 2])
    last.start()
    for copy in copies:
        copy.wait()
    last.wait()


VM = pl.BlockSpec(memory_space=pltpu.VMEM)
HB = pl.BlockSpec(memory_space=pltpu.MemorySpace.HBM)
PARAMS = pltpu.CompilerParams(vmem_limit_bytes=24 << 20)


def in_hbm(a):
    return pltpu.with_memory_space_constraint(a, pltpu.MemorySpace.HBM)


def sds(*shape):
    return jax.ShapeDtypeStruct(shape, F32)


def shards(fields, noise, ancestors, obs_cells, obs_values):
    members = fields.shape[0]
    devices = lax.axis_size("mem")
    total_y = T * lax.axis_size("gy")
    fields_vm, noise_vm, rowpack, colpack, ownrow, owncol = pl.pallas_call(
        pack_kernel,
        out_shape=(
            sds(*fields.shape),
            sds(*noise.shape),
            sds(3 * members + members // 2, 8, T),
            sds(T, T),
            sds(4, 2 * members, 8, T),
            sds(4, T, T),
        ),
        in_specs=[HB] * 2,
        out_specs=[VM] * 6,
        scratch_shapes=[pltpu.SemaphoreType.DMA((3,))],
        compiler_params=PARAMS,
        name="pack",
    )(in_hbm(fields), in_hbm(noise))
    swap = [(0, 1), (1, 0)]
    colrecv = lax.ppermute(colpack, "gy", swap)
    rowrecv = lax.ppermute(rowpack, "gx", swap)
    count, pairs = obs_cells.shape[-1], ancestors.shape[-1]
    ownrow, owncol, inner, pick_y, cell_x, values, lineage = pl.pallas_call(
        functools.partial(interior_kernel, total_y),
        out_shape=(
            sds(4, 2 * members, 8, T),
            sds(4, T, T),
            sds(members, 3, T, T),
            jax.ShapeDtypeStruct((T, count), jnp.bfloat16),
            jax.ShapeDtypeStruct((1, count), jnp.int32),
            sds(1, count),
            jax.ShapeDtypeStruct((1, pairs), jnp.int32),
        ),
        in_specs=[VM] * 4 + [HB] * 3,
        out_specs=[VM] * 7,
        input_output_aliases={2: 0, 3: 1},
        scratch_shapes=[
            pltpu.VMEM((members, 3, T, T), F32),
            pltpu.VMEM((1, count), jnp.int32),
            pltpu.SemaphoreType.DMA((3,)),
        ],
        compiler_params=PARAMS,
        cost_estimate=pl.CostEstimate(flops=50_000_000, bytes_accessed=2_500_000, transcendentals=0),
        name="interior",
    )(
        fields_vm,
        noise_vm,
        ownrow,
        owncol,
        in_hbm(obs_cells.reshape(1, -1)),
        in_hbm(obs_values.reshape(1, -1)),
        in_hbm(ancestors.reshape(1, -1)),
    )
    colrecv, rowrecv, inner = lax.optimization_barrier((colrecv, rowrecv, inner))
    cornrecv = lax.ppermute(colrecv, "gx", swap)
    edge, cs, cs1 = pl.pallas_call(
        functools.partial(strips_kernel, total_y),
        out_shape=(sds(3, 2 * members, 8, T), sds(4, T + 16, T), sds(3, T + 16, T)),
        in_specs=[VM] * 4,
        out_specs=[VM] * 3,
        scratch_shapes=[pltpu.VMEM((4, T, T), F32), pltpu.VMEM((3, T, T), F32)],
        compiler_params=PARAMS,
        cost_estimate=pl.CostEstimate(flops=18_000_000, bytes_accessed=700_000, transcendentals=0),
        name="strips",
    )(ownrow, rowrecv, owncol, colrecv)
    rows = 768 // devices
    stride = members // 2 * rows + 1
    _, _, pieces = pl.pallas_call(
        functools.partial(merge_kernel, total_y, devices),
        out_shape=(sds(4, T + 16, T), sds(3, T + 16, T), sds(devices * stride, T)),
        in_specs=[VM] * 8,
        out_specs=[VM] * 3,
        input_output_aliases={2: 0, 3: 1},
        scratch_shapes=[pltpu.VMEM((members * T, T), F32)],
        compiler_params=PARAMS,
        name="merge",
    )(inner, edge, cs, cs1, cornrecv, pick_y, cell_x, values)
    held = lax.all_to_all(pieces.reshape(devices, stride, 1, T), "mem", 0, 0).reshape(devices * stride, T)
    picked = pl.pallas_call(
        functools.partial(select_kernel, members),
        out_shape=sds(pairs, rows, T),
        in_specs=[VM, VM],
        out_specs=VM,
        compiler_params=PARAMS,
        name="select",
    )(lineage, held)
    back = lax.all_to_all(picked.reshape(devices, members // 2, rows, T), "mem", 0, 0)
    resampled, log_weights = pl.pallas_call(
        functools.partial(finish_kernel, members),
        out_shape=(sds(members // 2, devices, rows, T), sds(1, 1, members)),
        in_specs=[VM, VM],
        out_specs=[HB, HB],
        scratch_shapes=[pltpu.VMEM((1, 1, members), F32), pltpu.SemaphoreType.DMA((members // 2 + 1,))],
        compiler_params=PARAMS,
        name="finish",
    )(back, held)
    return (resampled.reshape(fields.shape), log_weights)


def solution(mesh):
    return jax.shard_map(
        shards,
        mesh=mesh,
        in_specs=(
            P("mem", None, "gx", "gy"),
            P("mem", "gx", "gy"),
            P("gx", "gy", None),
            P("gx", "gy", None),
            P("gx", "gy", None),
        ),
        out_specs=(P("mem", None, "gx", "gy"), P("gx", "gy", "mem")),
        check_vma=False,
    )
```

```python
import functools

import jax
import jax.numpy as jnp
from jax import lax
from jax.experimental import pallas as pl
from jax.experimental.pallas import tpu as pltpu
from jax.sharding import PartitionSpec as P

COURANT = 0.3
NOISE_AMP = 0.1
OBS_VAR = 0.25
T = 128
F32 = jnp.float32
CHUNK = 128


def lanes(shape):
    return lax.broadcasted_iota(jnp.int32, shape, len(shape) - 1)


def subl(shape):
    return lax.broadcasted_iota(jnp.int32, shape, len(shape) - 2)


def lroll(a, shift):
    return pltpu.roll(a, shift % T, 1)


def rows_at(ref, lead, start, off, count, total):
    first = start + off
    if first < 0:
        return pltpu.roll(ref[(*lead, pl.ds(0, count))], -first, 0)
    if first + count > total:
        over = first + count - total
        return pltpu.roll(ref[(*lead, pl.ds(total - count, count))], count - over, 0)
    return ref[(*lead, pl.ds(first, count))]


def one_step(ref, lead, start, count, total, force, cor):
    get = lambda f, off: rows_at(ref, (*lead, f), start, off, count, total)
    cen, low, high = [], [], []
    dx, dy, loc, q = [], [], [], []
    for f in range(3):
        a, am, ap = get(f, 0), get(f, -1), get(f, 1)
        far = get(f, -2) + get(f, 2)
        cross = am + ap
        yp, ym = lroll(a, -1), lroll(a, 1)
        cen.append(a)
        low.append(am)
        high.append(ap)
        dx.append(ap - am)
        dy.append(yp - ym)
        loc.append(0.71 * a + (0.09 * cross - 0.005 * far))
        q.append(0.09 * a - (0.01 * cross + 0.005 * (yp + ym)))
    eta, u, v = cen
    half = 0.5 * COURANT
    hv = half * ((1.0 + eta) * v)
    hu = (1.0 + high[0]) * high[1] - (1.0 + low[0]) * low[1]
    new_eta = loc[0] + lroll(q[0] - hv, -1) + lroll(q[0] + hv, 1) - half * hu + NOISE_AMP * force
    tend_u = u * dx[1] + v * dy[1] + dx[0]
    tend_v = u * dx[2] + v * dy[2] + dy[0]
    new_u = loc[1] + (lroll(q[1], -1) + lroll(q[1], 1)) - half * tend_u + (COURANT * cor) * v
    new_v = loc[2] + (lroll(q[2], -1) + lroll(q[2], 1)) - half * tend_v - (COURANT * cor) * u
    return new_eta, new_u, new_v


def coriolis(cols, total_y):
    y = lax.rem(lax.axis_index("gy") * T + cols + total_y, total_y)
    return 0.1 + 0.2 * ((y.astype(F32) + 0.5) / total_y - 0.5)


def pack_kernel(fields_hbm, noise_hbm, fields, noise, rowpack, colpack, ownrow, owncol, sems):
    members = fields.shape[0]
    half = members // 2
    copies = [pltpu.make_async_copy(noise_hbm, noise, sems.at[2])]
    for i in range(2):
        part = slice(i * half, (i + 1) * half)
        copies.append(pltpu.make_async_copy(fields_hbm.at[part], fields.at[part], sems.at[i]))
    for copy in copies:
        copy.start()
    copies[0].wait()
    top = subl((8, T)) < 4
    ln = lanes((T, T)) // 8
    for p in range(members // 2):
        rowpack[3 * members + p] = jnp.where(top, noise[p, 0:8], noise[p, T - 8 : T])
    acc = jnp.zeros((T, T), F32)
    for m in range(members):
        acc = jnp.where(ln == 4 * m + 3, lroll(noise[m // 2], 32 * m + 28), acc)
    for m in range(members):
        if m % half == 0:
            copies[1 + m // half].wait()
        for f in range(3):
            rowpack[3 * m + f] = jnp.where(top, fields[m, f, 0:8], fields[m, f, T - 8 : T])
            acc = jnp.where(ln == 4 * m + f, lroll(fields[m, f], 32 * m + 8 * f + 4), acc)
    colpack[...] = acc

    @pl.when(strips_first())
    def _():
        own_strips(fields, noise, ownrow, owncol)


def strips_first():
    return (lax.axis_index("gx") != 0) & (lax.axis_index("gy") == 0)


def own_columns(tiles, every=1):
    shape = tiles[0].shape
    lane = lanes(shape)
    acc = jnp.zeros(shape, F32)
    for m in range(0, len(tiles), every):
        acc = jnp.where(lane // 32 == m, lroll(tiles[m], 32 * m + 24), acc)
    return jnp.where(lane % 32 < 8, lroll(acc, -16), acc)


def own_strips(fields, noise, ownrow, owncol):
    members = fields.shape[0]
    for f in range(4):
        tiles = [fields[m, f] if f < 3 else noise[m // 2] for m in range(members)]
        for m, a in enumerate(tiles):
            ownrow[f, 2 * m] = a[0:8]
            ownrow[f, 2 * m + 1] = a[T - 8 : T]
        if f < 3:
            owncol[f] = own_columns(tiles)
        else:
            even = own_columns(tiles, 2)
            owncol[f] = even + lroll(even, 32)


def interior(total_y, fields, noise, inner, tmp):
    cor = coriolis(lanes((1, T)), total_y)
    for src, dst in ((fields, tmp), (tmp, inner)):
        for m in range(fields.shape[0]):
            for r in range(0, T, CHUNK):
                new = one_step(src, (m,), r, CHUNK, T, noise[m // 2, r : r + CHUNK], cor)
                for f in range(3):
                    dst[m, f, r : r + CHUNK] = new[f]


def interior_kernel(total_y, fields, noise, ownrow_in, owncol_in, cells_hbm, values_hbm, lineage_hbm,
                    ownrow, owncol, inner, pick_y, cell_x, values, lineage, tmp, cells, sems):
    members = fields.shape[0]
    copies = [
        pltpu.make_async_copy(cells_hbm, cells, sems.at[0]),
        pltpu.make_async_copy(values_hbm, values, sems.at[1]),
        pltpu.make_async_copy(lineage_hbm, lineage, sems.at[2]),
    ]
    for copy in copies:
        copy.start()

    @pl.when(jnp.logical_not(strips_first()))
    def _():
        own_strips(fields, noise, ownrow, owncol)

    interior(total_y, fields, noise, inner, tmp)
    for copy in copies:
        copy.wait()
    cell = cells[...]
    line_y = lax.broadcasted_iota(jnp.int32, pick_y.shape, 0)
    pick_y[...] = jnp.where(line_y == lax.rem(cell, T), 1.0, 0.0).astype(pick_y.dtype)
    cell_x[...] = cell // T


def twice(a, a1, total, cor):
    for src, dst in ((a, a1), (a1, a)):
        new = one_step(src, (), 0, total, total, a[3], cor)
        for f in range(3):
            dst[f, 0:total] = new[f]


def column_masks():
    l32 = lax.rem(lanes((1, T)), 32)
    cols = jnp.where(l32 < 16, l32 + 120, l32 - 24)
    return cols, (l32 >= 20) & (l32 < 24), (l32 >= 8) & (l32 < 12)


def with_halo(own, recv, f, is_low, is_high):
    return jnp.where(is_low, lroll(recv, 20 - 8 * f), jnp.where(is_high, lroll(recv, 4 - 8 * f), own))


def some_rows(src, dst, first, count, cor, force):
    new = one_step(src, (), first, count, T + 16, force[3, first : first + count], cor)
    for f in range(3):
        dst[f, first : first + count] = new[f]


def strips_kernel(total_y, ownrow, rowrecv, owncol, colrecv, edge, cs, cs1, rs, rs1):
    members = ownrow.shape[1] // 2
    cols, is_low, is_high = column_masks()
    halo = lambda m, f: rowrecv[3 * m + f] if f < 3 else rowrecv[3 * members + m // 2]
    for f in range(4):
        for m in range(members):
            rs[f, 32 * m : 32 * m + 8] = halo(m, f)
            rs[f, 32 * m + 8 : 32 * m + 16] = ownrow[f, 2 * m]
            rs[f, 32 * m + 16 : 32 * m + 24] = ownrow[f, 2 * m + 1]
            rs[f, 32 * m + 24 : 32 * m + 32] = halo(m, f)
        cs[f, 0:8] = own_columns([halo(m, f) for m in range(members)])
        cs[f, 8 : T + 8] = with_halo(owncol[f], colrecv[...], f, is_low, is_high)
    some_rows(cs, cs1, 16, T - 16, coriolis(cols, total_y), cs)
    twice(rs, rs1, T, coriolis(lanes((1, T)), total_y))
    for f in range(3):
        for m in range(members):
            edge[f, 2 * m] = rs[f, 32 * m + 8 : 32 * m + 16]
            edge[f, 2 * m + 1] = rs[f, 32 * m + 16 : 32 * m + 24]


def merge_kernel(total_y, devices, inner, edge, cs_in, cs1_in, cornrecv, pick_y, cell_x, values, cs, cs1, out, eta_s):
    members = inner.shape[0]
    cols, is_low, is_high = column_masks()
    cor_col = coriolis(cols, total_y)
    corn = jnp.where(subl((8, T)) < 4, cornrecv[0:8], cornrecv[T - 8 : T])
    for f in range(4):
        ends = with_halo(cs[f, 0:8], corn, f, is_low, is_high)
        cs[f, 0:8] = ends
        cs[f, T + 8 : T + 16] = ends
    some_rows(cs, cs1, 0, 16, cor_col, cs)
    some_rows(cs, cs1, T, 16, cor_col, cs)
    some_rows(cs1, cs, 8, T, cor_col, cs)

    per = 96 // devices
    stride = members // 2 * 8 * per + 1
    top = subl((8, T)) < 4
    lane = lanes((8, T))
    moved = (lane % 32 >= 20) & (lane % 32 < 24)
    outer = (lane < 4) | (lane >= T - 4)
    for f in range(3):
        for t in range(T // 8):
            col = cs[f, 8 * t + 8 : 8 * t + 16]
            col = jnp.where(moved, lroll(col, 16), col)
            for m in range(members):
                p, mm = m // 2, m % 2
                a = inner[m, f, 8 * t : 8 * t + 8]
                if t == 0:
                    a = jnp.where(top, edge[f, 2 * m], a)
                if t == T // 8 - 1:
                    a = jnp.where(top, a, edge[f, 2 * m + 1])
                a = jnp.where(outer, lroll(col, 104 - 32 * m), a)
                k = mm * 48 + f * 16 + t
                first = (k // per) * stride + p * 8 * per + 8 * (k % per)
                out[first : first + 8] = a
                if f == 0:
                    eta_s[m * T + 8 * t : m * T + 8 * t + 8] = a

    eta = eta_s[...]
    hi = eta.astype(jnp.bfloat16)
    rest = eta - hi.astype(F32)
    mid = rest.astype(jnp.bfloat16)
    low = (rest - mid.astype(F32)).astype(jnp.bfloat16)
    dot = lambda part: jnp.dot(part, pick_y[...], preferred_element_type=F32)
    seen = dot(hi) + (dot(mid) + dot(low))
    pick_x = lax.broadcasted_iota(jnp.int32, pick_y.shape, 0) == cell_x[...]
    logw = jnp.zeros((1, T), F32)
    for m in range(members):
        at = jnp.sum(jnp.where(pick_x, seen[m * T : (m + 1) * T], 0.0), axis=0, keepdims=True)
        miss = at - values[...]
        total = jnp.sum(miss * miss, axis=1, keepdims=True)
        logw = jnp.where(lanes((1, T)) == m, -0.5 * total / OBS_VAR, logw)
    for j in range(devices):
        out[(j + 1) * stride - 1 : (j + 1) * stride] = logw


def select_kernel(members, lineage, recv, out):
    pairs, rows = out.shape[0], out.shape[1]
    per = members // 2
    for k in range(pairs):
        pair = lineage[0, k]
        out[k] = recv[pl.ds(lax.div(pair, per) * (per * rows + 1) + lax.rem(pair, per) * rows, rows)]


def finish_kernel(members, back, recv, out, log_weights, result, sems):
    devices = back.shape[0]
    copies = [pltpu.make_async_copy(back.at[:, p], out.at[p], sems.at[p]) for p in range(members // 2)]
    for copy in copies:
        copy.start()
    stride = recv.shape[0] // devices
    logw = recv[pl.ds(stride - 1, devices, stride)]
    logw = jnp.where(lanes(logw.shape) < members, logw, -jnp.inf)
    peak = jnp.max(jnp.max(logw, axis=1, keepdims=True), axis=0, keepdims=True)
    total = jnp.sum(jnp.sum(jnp.exp(logw - peak), axis=1, keepdims=True), axis=0, keepdims=True)
    own = recv[pl.ds(lax.axis_index("mem") * stride + stride - 1, 1)]
    result[0] = (own - peak - jnp.log(total))[:, :members]
    last = pltpu.make_async_copy(result, log_weights, sems.at[members // 2])
    last.start()
    for copy in copies:
        copy.wait()
    last.wait()


VM = pl.BlockSpec(memory_space=pltpu.VMEM)
HB = pl.BlockSpec(memory_space=pltpu.MemorySpace.HBM)
PARAMS = pltpu.CompilerParams(vmem_limit_bytes=24 << 20)


def in_hbm(a):
    return pltpu.with_memory_space_constraint(a, pltpu.MemorySpace.HBM)


def sds(*shape):
    return jax.ShapeDtypeStruct(shape, F32)


def shards(fields, noise, ancestors, obs_cells, obs_values):
    members = fields.shape[0]
    devices = lax.axis_size("mem")
    total_y = T * lax.axis_size("gy")
    fields_vm, noise_vm, rowpack, colpack, ownrow, owncol = pl.pallas_call(
        pack_kernel,
        out_shape=(
            sds(*fields.shape),
            sds(*noise.shape),
            sds(3 * members + members // 2, 8, T),
            sds(T, T),
            sds(4, 2 * members, 8, T),
            sds(4, T, T),
        ),
        in_specs=[HB] * 2,
        out_specs=[VM] * 6,
        scratch_shapes=[pltpu.SemaphoreType.DMA((3,))],
        compiler_params=PARAMS,
        name="pack",
    )(in_hbm(fields), in_hbm(noise))
    swap = [(0, 1), (1, 0)]
    colrecv = lax.ppermute(colpack, "gy", swap)
    rowrecv = lax.ppermute(rowpack, "gx", swap)
    count, pairs = obs_cells.shape[-1], ancestors.shape[-1]
    ownrow, owncol, inner, pick_y, cell_x, values, lineage = pl.pallas_call(
        functools.partial(interior_kernel, total_y),
        out_shape=(
            sds(4, 2 * members, 8, T),
            sds(4, T, T),
            sds(members, 3, T, T),
            jax.ShapeDtypeStruct((T, count), jnp.bfloat16),
            jax.ShapeDtypeStruct((1, count), jnp.int32),
            sds(1, count),
            jax.ShapeDtypeStruct((1, pairs), jnp.int32),
        ),
        in_specs=[VM] * 4 + [HB] * 3,
        out_specs=[VM] * 7,
        input_output_aliases={2: 0, 3: 1},
        scratch_shapes=[
            pltpu.VMEM((members, 3, T, T), F32),
            pltpu.VMEM((1, count), jnp.int32),
            pltpu.SemaphoreType.DMA((3,)),
        ],
        compiler_params=PARAMS,
        cost_estimate=pl.CostEstimate(flops=50_000_000, bytes_accessed=2_500_000, transcendentals=0),
        name="interior",
    )(
        fields_vm,
        noise_vm,
        ownrow,
        owncol,
        in_hbm(obs_cells.reshape(1, -1)),
        in_hbm(obs_values.reshape(1, -1)),
        in_hbm(ancestors.reshape(1, -1)),
    )
    colrecv, rowrecv, inner = lax.optimization_barrier((colrecv, rowrecv, inner))
    cornrecv = lax.ppermute(colrecv, "gx", swap)
    edge, cs, cs1 = pl.pallas_call(
        functools.partial(strips_kernel, total_y),
        out_shape=(sds(3, 2 * members, 8, T), sds(4, T + 16, T), sds(3, T + 16, T)),
        in_specs=[VM] * 4,
        out_specs=[VM] * 3,
        scratch_shapes=[pltpu.VMEM((4, T, T), F32), pltpu.VMEM((3, T, T), F32)],
        compiler_params=PARAMS,
        cost_estimate=pl.CostEstimate(flops=18_000_000, bytes_accessed=700_000, transcendentals=0),
        name="strips",
    )(ownrow, rowrecv, owncol, colrecv)
    rows = 768 // devices
    stride = members // 2 * rows + 1
    _, _, pieces = pl.pallas_call(
        functools.partial(merge_kernel, total_y, devices),
        out_shape=(sds(4, T + 16, T), sds(3, T + 16, T), sds(devices * stride, T)),
        in_specs=[VM] * 8,
        out_specs=[VM] * 3,
        input_output_aliases={2: 0, 3: 1},
        scratch_shapes=[pltpu.VMEM((members * T, T), F32)],
        compiler_params=PARAMS,
        name="merge",
    )(inner, edge, cs, cs1, cornrecv, pick_y, cell_x, values)
    held = lax.all_to_all(pieces.reshape(devices, stride, 1, T), "mem", 0, 0).reshape(devices * stride, T)
    picked = pl.pallas_call(
        functools.partial(select_kernel, members),
        out_shape=sds(pairs, rows, T),
        in_specs=[VM, VM],
        out_specs=VM,
        compiler_params=PARAMS,
        name="select",
    )(lineage, held)
    back = lax.all_to_all(picked.reshape(devices, members // 2, rows, T), "mem", 0, 0)
    resampled, log_weights = pl.pallas_call(
        functools.partial(finish_kernel, members),
        out_shape=(sds(members // 2, devices, rows, T), sds(1, 1, members)),
        in_specs=[VM, VM],
        out_specs=[HB, HB],
        scratch_shapes=[pltpu.VMEM((1, 1, members), F32), pltpu.SemaphoreType.DMA((members // 2 + 1,))],
        compiler_params=PARAMS,
        name="finish",
    )(back, held)
    return (resampled.reshape(fields.shape), log_weights)


def solution(mesh):
    return jax.shard_map(
        shards,
        mesh=mesh,
        in_specs=(
            P("mem", None, "gx", "gy"),
            P("mem", "gx", "gy"),
            P("gx", "gy", None),
            P("gx", "gy", None),
            P("gx", "gy", None),
        ),
        out_specs=(P("mem", None, "gx", "gy"), P("gx", "gy", "mem")),
        check_vma=False,
    )
```

```python
import functools

import jax
import jax.numpy as jnp
from jax import lax
from jax.experimental import pallas as pl
from jax.experimental.pallas import tpu as pltpu
from jax.sharding import PartitionSpec as P

COURANT = 0.3
NOISE_AMP = 0.1
OBS_VAR = 0.25
T = 128
F32 = jnp.float32
CHUNK = 128


def lanes(shape):
    return lax.broadcasted_iota(jnp.int32, shape, len(shape) - 1)


def subl(shape):
    return lax.broadcasted_iota(jnp.int32, shape, len(shape) - 2)


def lroll(a, shift):
    return pltpu.roll(a, shift % T, 1)


def rows_at(ref, lead, start, off, count, total):
    first = start + off
    if first < 0:
        return pltpu.roll(ref[(*lead, pl.ds(0, count))], -first, 0)
    if first + count > total:
        over = first + count - total
        return pltpu.roll(ref[(*lead, pl.ds(total - count, count))], count - over, 0)
    return ref[(*lead, pl.ds(first, count))]


def one_step(ref, lead, start, count, total, force, cor):
    get = lambda f, off: rows_at(ref, (*lead, f), start, off, count, total)
    cen, low, high = [], [], []
    dx, dy, loc, q = [], [], [], []
    for f in range(3):
        a, am, ap = get(f, 0), get(f, -1), get(f, 1)
        far = get(f, -2) + get(f, 2)
        cross = am + ap
        yp, ym = lroll(a, -1), lroll(a, 1)
        cen.append(a)
        low.append(am)
        high.append(ap)
        dx.append(ap - am)
        dy.append(yp - ym)
        loc.append(0.71 * a + (0.09 * cross - 0.005 * far))
        q.append(0.09 * a - (0.01 * cross + 0.005 * (yp + ym)))
    eta, u, v = cen
    half = 0.5 * COURANT
    hv = half * ((1.0 + eta) * v)
    hu = (1.0 + high[0]) * high[1] - (1.0 + low[0]) * low[1]
    new_eta = loc[0] + lroll(q[0] - hv, -1) + lroll(q[0] + hv, 1) - half * hu + NOISE_AMP * force
    tend_u = u * dx[1] + v * dy[1] + dx[0]
    tend_v = u * dx[2] + v * dy[2] + dy[0]
    new_u = loc[1] + (lroll(q[1], -1) + lroll(q[1], 1)) - half * tend_u + (COURANT * cor) * v
    new_v = loc[2] + (lroll(q[2], -1) + lroll(q[2], 1)) - half * tend_v - (COURANT * cor) * u
    return new_eta, new_u, new_v


def coriolis(cols, total_y):
    y = lax.rem(lax.axis_index("gy") * T + cols + total_y, total_y)
    return 0.1 + 0.2 * ((y.astype(F32) + 0.5) / total_y - 0.5)


def pack_kernel(fields_hbm, noise_hbm, fields, noise, rowpack, colpack, ownrow, owncol, sems):
    members = fields.shape[0]
    half = members // 2
    copies = [pltpu.make_async_copy(noise_hbm, noise, sems.at[2])]
    for i in range(2):
        part = slice(i * half, (i + 1) * half)
        copies.append(pltpu.make_async_copy(fields_hbm.at[part], fields.at[part], sems.at[i]))
    for copy in copies:
        copy.start()
    copies[0].wait()
    top = subl((8, T)) < 4
    ln = lanes((T, T)) // 8
    for p in range(members // 2):
        rowpack[3 * members + p] = jnp.where(top, noise[p, 0:8], noise[p, T - 8 : T])
    acc = jnp.zeros((T, T), F32)
    for m in range(members):
        acc = jnp.where(ln == 4 * m + 3, lroll(noise[m // 2], 32 * m + 28), acc)
    for m in range(members):
        if m % half == 0:
            copies[1 + m // half].wait()
        for f in range(3):
            rowpack[3 * m + f] = jnp.where(top, fields[m, f, 0:8], fields[m, f, T - 8 : T])
            acc = jnp.where(ln == 4 * m + f, lroll(fields[m, f], 32 * m + 8 * f + 4), acc)
    colpack[...] = acc

    @pl.when(strips_first())
    def _():
        own_strips(fields, noise, ownrow, owncol)


def strips_first():
    return (lax.axis_index("gx") != 0) & (lax.axis_index("gy") == 0)


def own_columns(tiles, every=1):
    shape = tiles[0].shape
    ln = lanes(shape) // 8
    acc = jnp.zeros(shape, F32)
    for m in range(0, len(tiles), every):
        a = tiles[m]
        acc = jnp.where(ln == 4 * m, lroll(a, 32 * m + 8), acc)
        acc = jnp.where(ln == 4 * m + 3, lroll(a, 32 * m + 24), acc)
    return acc


def own_tall(tiles, every=1):
    lane = lanes((T, T))
    acc = jnp.zeros((T, T), F32)
    for m in range(0, len(tiles), every):
        acc = jnp.where(lane // 32 == m, lroll(tiles[m], 32 * m + 24), acc)
    return jnp.where(lane % 32 < 8, lroll(acc, -16), acc)


def own_strips(fields, noise, ownrow, owncol):
    members = fields.shape[0]
    for f in range(4):
        tiles = [fields[m, f] if f < 3 else noise[m // 2] for m in range(members)]
        for m, a in enumerate(tiles):
            ownrow[f, 2 * m] = a[0:8]
            ownrow[f, 2 * m + 1] = a[T - 8 : T]
        if f < 3:
            owncol[f] = own_tall(tiles)
        else:
            even = own_tall(tiles, 2)
            owncol[f] = even + lroll(even, 32)


def interior(total_y, fields, noise, inner, tmp):
    cor = coriolis(lanes((1, T)), total_y)
    for src, dst in ((fields, tmp), (tmp, inner)):
        for m in range(fields.shape[0]):
            for r in range(0, T, CHUNK):
                new = one_step(src, (m,), r, CHUNK, T, noise[m // 2, r : r + CHUNK], cor)
                for f in range(3):
                    dst[m, f, r : r + CHUNK] = new[f]


def interior_kernel(total_y, fields, noise, ownrow_in, owncol_in, cells_hbm, values_hbm, lineage_hbm,
                    ownrow, owncol, inner, pick_y, cell_x, values, lineage, tmp, cells, sems):
    members = fields.shape[0]
    copies = [
        pltpu.make_async_copy(cells_hbm, cells, sems.at[0]),
        pltpu.make_async_copy(values_hbm, values, sems.at[1]),
        pltpu.make_async_copy(lineage_hbm, lineage, sems.at[2]),
    ]
    for copy in copies:
        copy.start()

    @pl.when(jnp.logical_not(strips_first()))
    def _():
        own_strips(fields, noise, ownrow, owncol)

    interior(total_y, fields, noise, inner, tmp)
    for copy in copies:
        copy.wait()
    cell = cells[...]
    line_y = lax.broadcasted_iota(jnp.int32, pick_y.shape, 0)
    pick_y[...] = jnp.where(line_y == lax.rem(cell, T), 1.0, 0.0).astype(pick_y.dtype)
    cell_x[...] = cell // T


def twice(a, a1, total, cor):
    for src, dst in ((a, a1), (a1, a)):
        new = one_step(src, (), 0, total, total, a[3], cor)
        for f in range(3):
            dst[f, 0:total] = new[f]


def column_masks():
    l32 = lax.rem(lanes((1, T)), 32)
    cols = jnp.where(l32 < 16, l32 + 120, l32 - 24)
    return cols, (l32 >= 20) & (l32 < 24), (l32 >= 8) & (l32 < 12)


def with_halo(own, recv, f, is_low, is_high):
    return jnp.where(is_low, lroll(recv, 20 - 8 * f), jnp.where(is_high, lroll(recv, 4 - 8 * f), own))


def some_rows(src, dst, first, count, cor, force):
    new = one_step(src, (), first, count, T + 16, force[3, first : first + count], cor)
    for f in range(3):
        dst[f, first : first + count] = new[f]


def strips_kernel(total_y, ownrow, rowrecv, owncol, colrecv, edge, cs, cs1, rs, rs1):
    members = ownrow.shape[1] // 2
    cols, is_low, is_high = column_masks()
    halo = lambda m, f: rowrecv[3 * m + f] if f < 3 else rowrecv[3 * members + m // 2]
    for f in range(4):
        for m in range(members):
            rs[f, 32 * m : 32 * m + 8] = halo(m, f)
            rs[f, 32 * m + 8 : 32 * m + 16] = ownrow[f, 2 * m]
            rs[f, 32 * m + 16 : 32 * m + 24] = ownrow[f, 2 * m + 1]
            rs[f, 32 * m + 24 : 32 * m + 32] = halo(m, f)
        cs[f, 0:8] = own_columns([halo(m, f) for m in range(members)])
        cs[f, 8 : T + 8] = with_halo(owncol[f], colrecv[...], f, is_low, is_high)
    some_rows(cs, cs1, 16, T - 16, coriolis(cols, total_y), cs)
    twice(rs, rs1, T, coriolis(lanes((1, T)), total_y))
    for f in range(3):
        for m in range(members):
            edge[f, 2 * m] = rs[f, 32 * m + 8 : 32 * m + 16]
            edge[f, 2 * m + 1] = rs[f, 32 * m + 16 : 32 * m + 24]


def merge_kernel(total_y, devices, inner, edge, cs_in, cs1_in, cornrecv, pick_y, cell_x, values, cs, cs1, out, eta_s):
    members = inner.shape[0]
    cols, is_low, is_high = column_masks()
    cor_col = coriolis(cols, total_y)
    corn = jnp.where(subl((8, T)) < 4, cornrecv[0:8], cornrecv[T - 8 : T])
    for f in range(4):
        ends = with_halo(cs[f, 0:8], corn, f, is_low, is_high)
        cs[f, 0:8] = ends
        cs[f, T + 8 : T + 16] = ends
    some_rows(cs, cs1, 0, 16, cor_col, cs)
    some_rows(cs, cs1, T, 16, cor_col, cs)
    some_rows(cs1, cs, 8, T, cor_col, cs)

    per = 96 // devices
    stride = members // 2 * 8 * per + 1
    top = subl((8, T)) < 4
    left = lanes((8, T)) < 4
    right = lanes((8, T)) >= T - 4
    for f in range(3):
        for m in range(members):
            p, mm = m // 2, m % 2
            for t in range(T // 8):
                a = inner[m, f, 8 * t : 8 * t + 8]
                if t == 0:
                    a = jnp.where(top, edge[f, 2 * m], a)
                if t == T // 8 - 1:
                    a = jnp.where(top, a, edge[f, 2 * m + 1])
                col = cs[f, 8 * t + 8 : 8 * t + 16]
                a = jnp.where(left, lroll(col, 104 - 32 * m), a)
                a = jnp.where(right, lroll(col, 120 - 32 * m), a)
                k = mm * 48 + f * 16 + t
                first = (k // per) * stride + p * 8 * per + 8 * (k % per)
                out[first : first + 8] = a
                if f == 0:
                    eta_s[m * T + 8 * t : m * T + 8 * t + 8] = a
        if f == 0:
            eta = eta_s[...]
            hi = eta.astype(jnp.bfloat16)
            rest = eta - hi.astype(F32)
            mid = rest.astype(jnp.bfloat16)
            low = (rest - mid.astype(F32)).astype(jnp.bfloat16)
            dot = lambda part: jnp.dot(part, pick_y[...], preferred_element_type=F32)
            seen = dot(hi) + (dot(mid) + dot(low))
    pick_x = lax.broadcasted_iota(jnp.int32, pick_y.shape, 0) == cell_x[...]
    logw = jnp.zeros((1, T), F32)
    for m in range(members):
        at = jnp.sum(jnp.where(pick_x, seen[m * T : (m + 1) * T], 0.0), axis=0, keepdims=True)
        miss = at - values[...]
        total = jnp.sum(miss * miss, axis=1, keepdims=True)
        logw = jnp.where(lanes((1, T)) == m, -0.5 * total / OBS_VAR, logw)
    for j in range(devices):
        out[(j + 1) * stride - 1 : (j + 1) * stride] = logw


def select_kernel(members, lineage, recv, out):
    pairs, rows = out.shape[0], out.shape[1]
    per = members // 2
    for k in range(pairs):
        pair = lineage[0, k]
        out[k] = recv[pl.ds(lax.div(pair, per) * (per * rows + 1) + lax.rem(pair, per) * rows, rows)]


def finish_kernel(members, back, recv, out, log_weights, result, sems):
    devices = back.shape[0]
    copies = [pltpu.make_async_copy(back.at[:, p], out.at[p], sems.at[p]) for p in range(members // 2)]
    for copy in copies:
        copy.start()
    stride = recv.shape[0] // devices
    logw = recv[pl.ds(stride - 1, devices, stride)]
    logw = jnp.where(lanes(logw.shape) < members, logw, -jnp.inf)
    peak = jnp.max(jnp.max(logw, axis=1, keepdims=True), axis=0, keepdims=True)
    total = jnp.sum(jnp.sum(jnp.exp(logw - peak), axis=1, keepdims=True), axis=0, keepdims=True)
    own = recv[pl.ds(lax.axis_index("mem") * stride + stride - 1, 1)]
    result[0] = (own - peak - jnp.log(total))[:, :members]
    last = pltpu.make_async_copy(result, log_weights, sems.at[members // 2])
    last.start()
    for copy in copies:
        copy.wait()
    last.wait()


VM = pl.BlockSpec(memory_space=pltpu.VMEM)
HB = pl.BlockSpec(memory_space=pltpu.MemorySpace.HBM)
PARAMS = pltpu.CompilerParams(vmem_limit_bytes=24 << 20)


def in_hbm(a):
    return pltpu.with_memory_space_constraint(a, pltpu.MemorySpace.HBM)


def sds(*shape):
    return jax.ShapeDtypeStruct(shape, F32)


def shards(fields, noise, ancestors, obs_cells, obs_values):
    members = fields.shape[0]
    devices = lax.axis_size("mem")
    total_y = T * lax.axis_size("gy")
    fields_vm, noise_vm, rowpack, colpack, ownrow, owncol = pl.pallas_call(
        pack_kernel,
        out_shape=(
            sds(*fields.shape),
            sds(*noise.shape),
            sds(3 * members + members // 2, 8, T),
            sds(T, T),
            sds(4, 2 * members, 8, T),
            sds(4, T, T),
        ),
        in_specs=[HB] * 2,
        out_specs=[VM] * 6,
        scratch_shapes=[pltpu.SemaphoreType.DMA((3,))],
        compiler_params=PARAMS,
        name="pack",
    )(in_hbm(fields), in_hbm(noise))
    swap = [(0, 1), (1, 0)]
    colrecv = lax.ppermute(colpack, "gy", swap)
    rowrecv = lax.ppermute(rowpack, "gx", swap)
    count, pairs = obs_cells.shape[-1], ancestors.shape[-1]
    ownrow, owncol, inner, pick_y, cell_x, values, lineage = pl.pallas_call(
        functools.partial(interior_kernel, total_y),
        out_shape=(
            sds(4, 2 * members, 8, T),
            sds(4, T, T),
            sds(members, 3, T, T),
            jax.ShapeDtypeStruct((T, count), jnp.bfloat16),
            jax.ShapeDtypeStruct((1, count), jnp.int32),
            sds(1, count),
            jax.ShapeDtypeStruct((1, pairs), jnp.int32),
        ),
        in_specs=[VM] * 4 + [HB] * 3,
        out_specs=[VM] * 7,
        input_output_aliases={2: 0, 3: 1},
        scratch_shapes=[
            pltpu.VMEM((members, 3, T, T), F32),
            pltpu.VMEM((1, count), jnp.int32),
            pltpu.SemaphoreType.DMA((3,)),
        ],
        compiler_params=PARAMS,
        cost_estimate=pl.CostEstimate(flops=50_000_000, bytes_accessed=2_500_000, transcendentals=0),
        name="interior",
    )(
        fields_vm,
        noise_vm,
        ownrow,
        owncol,
        in_hbm(obs_cells.reshape(1, -1)),
        in_hbm(obs_values.reshape(1, -1)),
        in_hbm(ancestors.reshape(1, -1)),
    )
    colrecv, rowrecv, inner = lax.optimization_barrier((colrecv, rowrecv, inner))
    cornrecv = lax.ppermute(colrecv, "gx", swap)
    edge, cs, cs1 = pl.pallas_call(
        functools.partial(strips_kernel, total_y),
        out_shape=(sds(3, 2 * members, 8, T), sds(4, T + 16, T), sds(3, T + 16, T)),
        in_specs=[VM] * 4,
        out_specs=[VM] * 3,
        scratch_shapes=[pltpu.VMEM((4, T, T), F32), pltpu.VMEM((3, T, T), F32)],
        compiler_params=PARAMS,
        cost_estimate=pl.CostEstimate(flops=18_000_000, bytes_accessed=700_000, transcendentals=0),
        name="strips",
    )(ownrow, rowrecv, owncol, colrecv)
    rows = 768 // devices
    stride = members // 2 * rows + 1
    _, _, pieces = pl.pallas_call(
        functools.partial(merge_kernel, total_y, devices),
        out_shape=(sds(4, T + 16, T), sds(3, T + 16, T), sds(devices * stride, T)),
        in_specs=[VM] * 8,
        out_specs=[VM] * 3,
        input_output_aliases={2: 0, 3: 1},
        scratch_shapes=[pltpu.VMEM((members * T, T), F32)],
        compiler_params=PARAMS,
        name="merge",
    )(inner, edge, cs, cs1, cornrecv, pick_y, cell_x, values)
    held = lax.all_to_all(pieces.reshape(devices, stride, 1, T), "mem", 0, 0).reshape(devices * stride, T)
    picked = pl.pallas_call(
        functools.partial(select_kernel, members),
        out_shape=sds(pairs, rows, T),
        in_specs=[VM, VM],
        out_specs=VM,
        compiler_params=PARAMS,
        name="select",
    )(lineage, held)
    back = lax.all_to_all(picked.reshape(devices, members // 2, rows, T), "mem", 0, 0)
    resampled, log_weights = pl.pallas_call(
        functools.partial(finish_kernel, members),
        out_shape=(sds(members // 2, devices, rows, T), sds(1, 1, members)),
        in_specs=[VM, VM],
        out_specs=[HB, HB],
        scratch_shapes=[pltpu.VMEM((1, 1, members), F32), pltpu.SemaphoreType.DMA((members // 2 + 1,))],
        compiler_params=PARAMS,
        name="finish",
    )(back, held)
    return (resampled.reshape(fields.shape), log_weights)


def solution(mesh):
    return jax.shard_map(
        shards,
        mesh=mesh,
        in_specs=(
            P("mem", None, "gx", "gy"),
            P("mem", "gx", "gy"),
            P("gx", "gy", None),
            P("gx", "gy", None),
            P("gx", "gy", None),
        ),
        out_specs=(P("mem", None, "gx", "gy"), P("gx", "gy", "mem")),
        check_vma=False,
    )
```

```python
import functools

import jax
import jax.numpy as jnp
from jax import lax
from jax.experimental import pallas as pl
from jax.experimental.pallas import tpu as pltpu
from jax.sharding import PartitionSpec as P

COURANT = 0.3
NOISE_AMP = 0.1
OBS_VAR = 0.25
T = 128
F32 = jnp.float32
CHUNK = 128


def lanes(shape):
    return lax.broadcasted_iota(jnp.int32, shape, len(shape) - 1)


def subl(shape):
    return lax.broadcasted_iota(jnp.int32, shape, len(shape) - 2)


def lroll(a, shift):
    return pltpu.roll(a, shift % T, 1)


def rows_at(ref, lead, start, off, count, total):
    first = start + off
    if first < 0:
        return pltpu.roll(ref[(*lead, pl.ds(0, count))], -first, 0)
    if first + count > total:
        over = first + count - total
        return pltpu.roll(ref[(*lead, pl.ds(total - count, count))], count - over, 0)
    return ref[(*lead, pl.ds(first, count))]


def one_step(ref, lead, start, count, total, force, cor):
    get = lambda f, off: rows_at(ref, (*lead, f), start, off, count, total)
    cen, low, high = [], [], []
    dx, dy, loc, q = [], [], [], []
    for f in range(3):
        a, am, ap = get(f, 0), get(f, -1), get(f, 1)
        far = get(f, -2) + get(f, 2)
        cross = am + ap
        yp, ym = lroll(a, -1), lroll(a, 1)
        cen.append(a)
        low.append(am)
        high.append(ap)
        dx.append(ap - am)
        dy.append(yp - ym)
        loc.append(0.71 * a + (0.09 * cross - 0.005 * far))
        q.append(0.09 * a - (0.01 * cross + 0.005 * (yp + ym)))
    eta, u, v = cen
    half = 0.5 * COURANT
    hv = half * ((1.0 + eta) * v)
    hu = (1.0 + high[0]) * high[1] - (1.0 + low[0]) * low[1]
    new_eta = loc[0] + lroll(q[0] - hv, -1) + lroll(q[0] + hv, 1) - half * hu + NOISE_AMP * force
    tend_u = u * dx[1] + v * dy[1] + dx[0]
    tend_v = u * dx[2] + v * dy[2] + dy[0]
    new_u = loc[1] + (lroll(q[1], -1) + lroll(q[1], 1)) - half * tend_u + (COURANT * cor) * v
    new_v = loc[2] + (lroll(q[2], -1) + lroll(q[2], 1)) - half * tend_v - (COURANT * cor) * u
    return new_eta, new_u, new_v


def coriolis(cols, total_y):
    y = lax.rem(lax.axis_index("gy") * T + cols + total_y, total_y)
    return 0.1 + 0.2 * ((y.astype(F32) + 0.5) / total_y - 0.5)


def pack_kernel(fields_hbm, noise_hbm, fields, noise, rowpack, colpack, ownrow, owncol, sems):
    members = fields.shape[0]
    half = members // 2
    copies = [pltpu.make_async_copy(noise_hbm, noise, sems.at[2])]
    for i in range(2):
        part = slice(i * half, (i + 1) * half)
        copies.append(pltpu.make_async_copy(fields_hbm.at[part], fields.at[part], sems.at[i]))
    for copy in copies:
        copy.start()
    copies[0].wait()
    top = subl((8, T)) < 4
    ln = lanes((T, T)) // 8
    for p in range(members // 2):
        rowpack[3 * members + p] = jnp.where(top, noise[p, 0:8], noise[p, T - 8 : T])
    acc = jnp.zeros((T, T), F32)
    for m in range(members):
        acc = jnp.where(ln == 4 * m + 3, lroll(noise[m // 2], 32 * m + 28), acc)
    for m in range(members):
        if m % half == 0:
            copies[1 + m // half].wait()
        for f in range(3):
            rowpack[3 * m + f] = jnp.where(top, fields[m, f, 0:8], fields[m, f, T - 8 : T])
            acc = jnp.where(ln == 4 * m + f, lroll(fields[m, f], 32 * m + 8 * f + 4), acc)
    colpack[...] = acc

    @pl.when(strips_first())
    def _():
        own_strips(fields, noise, ownrow, owncol)


def strips_first():
    return (lax.axis_index("gx") != 0) & (lax.axis_index("gy") == 0)


def own_columns(tiles, every=1):
    shape = tiles[0].shape
    ln = lanes(shape) // 8
    acc = jnp.zeros(shape, F32)
    for m in range(0, len(tiles), every):
        a = tiles[m]
        acc = jnp.where(ln == 4 * m, lroll(a, 32 * m + 8), acc)
        acc = jnp.where(ln == 4 * m + 3, lroll(a, 32 * m + 24), acc)
    return acc


def own_strips(fields, noise, ownrow, owncol):
    members = fields.shape[0]
    for f in range(4):
        tiles = [fields[m, f] if f < 3 else noise[m // 2] for m in range(members)]
        for m, a in enumerate(tiles):
            ownrow[f, 2 * m] = a[0:8]
            ownrow[f, 2 * m + 1] = a[T - 8 : T]
        if f < 3:
            owncol[f] = own_columns(tiles)
        else:
            even = own_columns(tiles, 2)
            owncol[f] = even + lroll(even, 32)


def interior(total_y, fields, noise, inner, tmp):
    cor = coriolis(lanes((1, T)), total_y)
    for src, dst in ((fields, tmp), (tmp, inner)):
        for m in range(fields.shape[0]):
            for r in range(0, T, CHUNK):
                new = one_step(src, (m,), r, CHUNK, T, noise[m // 2, r : r + CHUNK], cor)
                for f in range(3):
                    dst[m, f, r : r + CHUNK] = new[f]


def interior_kernel(total_y, fields, noise, ownrow_in, owncol_in, cells_hbm, values_hbm, lineage_hbm,
                    ownrow, owncol, inner, pick_y, cell_x, values, lineage, tmp, cells, sems):
    members = fields.shape[0]
    copies = [
        pltpu.make_async_copy(cells_hbm, cells, sems.at[0]),
        pltpu.make_async_copy(values_hbm, values, sems.at[1]),
        pltpu.make_async_copy(lineage_hbm, lineage, sems.at[2]),
    ]
    for copy in copies:
        copy.start()

    @pl.when(jnp.logical_not(strips_first()))
    def _():
        own_strips(fields, noise, ownrow, owncol)

    interior(total_y, fields, noise, inner, tmp)
    for copy in copies:
        copy.wait()
    cell = cells[...]
    line_y = lax.broadcasted_iota(jnp.int32, pick_y.shape, 0)
    pick_y[...] = jnp.where(line_y == lax.rem(cell, T), 1.0, 0.0).astype(pick_y.dtype)
    cell_x[...] = cell // T


def twice(a, a1, total, cor):
    for src, dst in ((a, a1), (a1, a)):
        new = one_step(src, (), 0, total, total, a[3], cor)
        for f in range(3):
            dst[f, 0:total] = new[f]


def column_masks():
    l32 = lax.rem(lanes((1, T)), 32)
    cols = jnp.where(l32 < 16, l32 + 120, l32 - 24)
    return cols, (l32 >= 20) & (l32 < 24), (l32 >= 8) & (l32 < 12)


def with_halo(own, recv, f, is_low, is_high):
    return jnp.where(is_low, lroll(recv, 20 - 8 * f), jnp.where(is_high, lroll(recv, 4 - 8 * f), own))


def some_rows(src, dst, first, count, cor, force):
    new = one_step(src, (), first, count, T + 16, force[3, first : first + count], cor)
    for f in range(3):
        dst[f, first : first + count] = new[f]


def strips_kernel(total_y, ownrow, rowrecv, owncol, colrecv, edge, cs, cs1, rs, rs1):
    members = ownrow.shape[1] // 2
    cols, is_low, is_high = column_masks()
    halo = lambda m, f: rowrecv[3 * m + f] if f < 3 else rowrecv[3 * members + m // 2]
    for f in range(4):
        for m in range(members):
            rs[f, 32 * m : 32 * m + 8] = halo(m, f)
            rs[f, 32 * m + 8 : 32 * m + 16] = ownrow[f, 2 * m]
            rs[f, 32 * m + 16 : 32 * m + 24] = ownrow[f, 2 * m + 1]
            rs[f, 32 * m + 24 : 32 * m + 32] = halo(m, f)
        cs[f, 0:8] = own_columns([halo(m, f) for m in range(members)])
        cs[f, 8 : T + 8] = with_halo(owncol[f], colrecv[...], f, is_low, is_high)
    cor_col = coriolis(cols, total_y)
    some_rows(cs, cs1, 16, T - 16, cor_col, cs)
    twice(rs, rs1, T, coriolis(lanes((1, T)), total_y))
    some_rows(cs1, cs, 24, T - 32, cor_col, cs)
    for f in range(3):
        for m in range(members):
            edge[f, 2 * m] = rs[f, 32 * m + 8 : 32 * m + 16]
            edge[f, 2 * m + 1] = rs[f, 32 * m + 16 : 32 * m + 24]


def merge_kernel(total_y, devices, inner, edge, cs_in, cs1_in, cornrecv, pick_y, cell_x, values, cs, cs1, out, eta_s):
    members = inner.shape[0]
    cols, is_low, is_high = column_masks()
    cor_col = coriolis(cols, total_y)
    corn = jnp.where(subl((8, T)) < 4, cornrecv[0:8], cornrecv[T - 8 : T])
    for f in range(4):
        ends = with_halo(cs[f, 0:8], corn, f, is_low, is_high)
        cs[f, 0:8] = ends
        cs[f, T + 8 : T + 16] = ends
    some_rows(cs, cs1, 0, 16, cor_col, cs)
    some_rows(cs, cs1, T, 16, cor_col, cs)
    some_rows(cs1, cs, 8, 16, cor_col, cs)
    some_rows(cs1, cs, T - 8, 16, cor_col, cs)

    per = 96 // devices
    stride = members // 2 * 8 * per + 1
    top = subl((8, T)) < 4
    left = lanes((8, T)) < 4
    right = lanes((8, T)) >= T - 4
    for m in range(members):
        p, mm = m // 2, m % 2
        for f in range(3):
            for t in range(T // 8):
                a = inner[m, f, 8 * t : 8 * t + 8]
                if t == 0:
                    a = jnp.where(top, edge[f, 2 * m], a)
                if t == T // 8 - 1:
                    a = jnp.where(top, a, edge[f, 2 * m + 1])
                col = cs[f, 8 * t + 8 : 8 * t + 16]
                a = jnp.where(left, lroll(col, 104 - 32 * m), a)
                a = jnp.where(right, lroll(col, 120 - 32 * m), a)
                k = mm * 48 + f * 16 + t
                first = (k // per) * stride + p * 8 * per + 8 * (k % per)
                out[first : first + 8] = a
                if f == 0:
                    eta_s[m * T + 8 * t : m * T + 8 * t + 8] = a

    eta = eta_s[...]
    hi = eta.astype(jnp.bfloat16)
    rest = eta - hi.astype(F32)
    mid = rest.astype(jnp.bfloat16)
    low = (rest - mid.astype(F32)).astype(jnp.bfloat16)
    dot = lambda part: jnp.dot(part, pick_y[...], preferred_element_type=F32)
    seen = dot(hi) + (dot(mid) + dot(low))
    pick_x = lax.broadcasted_iota(jnp.int32, pick_y.shape, 0) == cell_x[...]
    logw = jnp.zeros((1, T), F32)
    for m in range(members):
        at = jnp.sum(jnp.where(pick_x, seen[m * T : (m + 1) * T], 0.0), axis=0, keepdims=True)
        miss = at - values[...]
        total = jnp.sum(miss * miss, axis=1, keepdims=True)
        logw = jnp.where(lanes((1, T)) == m, -0.5 * total / OBS_VAR, logw)
    for j in range(devices):
        out[(j + 1) * stride - 1 : (j + 1) * stride] = logw


def select_kernel(members, lineage, recv, out):
    pairs, rows = out.shape[0], out.shape[1]
    per = members // 2
    for k in range(pairs):
        pair = lineage[0, k]
        out[k] = recv[pl.ds(lax.div(pair, per) * (per * rows + 1) + lax.rem(pair, per) * rows, rows)]


def finish_kernel(members, back, recv, out, log_weights, result, sems):
    devices = back.shape[0]
    copies = [pltpu.make_async_copy(back.at[:, p], out.at[p], sems.at[p]) for p in range(members // 2)]
    for copy in copies:
        copy.start()
    stride = recv.shape[0] // devices
    logw = recv[pl.ds(stride - 1, devices, stride)]
    logw = jnp.where(lanes(logw.shape) < members, logw, -jnp.inf)
    peak = jnp.max(jnp.max(logw, axis=1, keepdims=True), axis=0, keepdims=True)
    total = jnp.sum(jnp.sum(jnp.exp(logw - peak), axis=1, keepdims=True), axis=0, keepdims=True)
    own = recv[pl.ds(lax.axis_index("mem") * stride + stride - 1, 1)]
    result[0] = (own - peak - jnp.log(total))[:, :members]
    last = pltpu.make_async_copy(result, log_weights, sems.at[members // 2])
    last.start()
    for copy in copies:
        copy.wait()
    last.wait()


VM = pl.BlockSpec(memory_space=pltpu.VMEM)
HB = pl.BlockSpec(memory_space=pltpu.MemorySpace.HBM)
PARAMS = pltpu.CompilerParams(vmem_limit_bytes=24 << 20)


def in_hbm(a):
    return pltpu.with_memory_space_constraint(a, pltpu.MemorySpace.HBM)


def sds(*shape):
    return jax.ShapeDtypeStruct(shape, F32)


def shards(fields, noise, ancestors, obs_cells, obs_values):
    members = fields.shape[0]
    devices = lax.axis_size("mem")
    total_y = T * lax.axis_size("gy")
    fields_vm, noise_vm, rowpack, colpack, ownrow, owncol = pl.pallas_call(
        pack_kernel,
        out_shape=(
            sds(*fields.shape),
            sds(*noise.shape),
            sds(3 * members + members // 2, 8, T),
            sds(T, T),
            sds(4, 2 * members, 8, T),
            sds(4, T, T),
        ),
        in_specs=[HB] * 2,
        out_specs=[VM] * 6,
        scratch_shapes=[pltpu.SemaphoreType.DMA((3,))],
        compiler_params=PARAMS,
        name="pack",
    )(in_hbm(fields), in_hbm(noise))
    swap = [(0, 1), (1, 0)]
    colrecv = lax.ppermute(colpack, "gy", swap)
    rowrecv = lax.ppermute(rowpack, "gx", swap)
    count, pairs = obs_cells.shape[-1], ancestors.shape[-1]
    ownrow, owncol, inner, pick_y, cell_x, values, lineage = pl.pallas_call(
        functools.partial(interior_kernel, total_y),
        out_shape=(
            sds(4, 2 * members, 8, T),
            sds(4, T, T),
            sds(members, 3, T, T),
            jax.ShapeDtypeStruct((T, count), jnp.bfloat16),
            jax.ShapeDtypeStruct((1, count), jnp.int32),
            sds(1, count),
            jax.ShapeDtypeStruct((1, pairs), jnp.int32),
        ),
        in_specs=[VM] * 4 + [HB] * 3,
        out_specs=[VM] * 7,
        input_output_aliases={2: 0, 3: 1},
        scratch_shapes=[
            pltpu.VMEM((members, 3, T, T), F32),
            pltpu.VMEM((1, count), jnp.int32),
            pltpu.SemaphoreType.DMA((3,)),
        ],
        compiler_params=PARAMS,
        cost_estimate=pl.CostEstimate(flops=50_000_000, bytes_accessed=2_500_000, transcendentals=0),
        name="interior",
    )(
        fields_vm,
        noise_vm,
        ownrow,
        owncol,
        in_hbm(obs_cells.reshape(1, -1)),
        in_hbm(obs_values.reshape(1, -1)),
        in_hbm(ancestors.reshape(1, -1)),
    )
    colrecv, rowrecv, inner = lax.optimization_barrier((colrecv, rowrecv, inner))
    cornrecv = lax.ppermute(colrecv, "gx", swap)
    edge, cs, cs1 = pl.pallas_call(
        functools.partial(strips_kernel, total_y),
        out_shape=(sds(3, 2 * members, 8, T), sds(4, T + 16, T), sds(3, T + 16, T)),
        in_specs=[VM] * 4,
        out_specs=[VM] * 3,
        scratch_shapes=[pltpu.VMEM((4, T, T), F32), pltpu.VMEM((3, T, T), F32)],
        compiler_params=PARAMS,
        cost_estimate=pl.CostEstimate(flops=18_000_000, bytes_accessed=700_000, transcendentals=0),
        name="strips",
    )(ownrow, rowrecv, owncol, colrecv)
    rows = 768 // devices
    stride = members // 2 * rows + 1
    _, _, pieces = pl.pallas_call(
        functools.partial(merge_kernel, total_y, devices),
        out_shape=(sds(4, T + 16, T), sds(3, T + 16, T), sds(devices * stride, T)),
        in_specs=[VM] * 8,
        out_specs=[VM] * 3,
        input_output_aliases={2: 0, 3: 1},
        scratch_shapes=[pltpu.VMEM((members * T, T), F32)],
        compiler_params=PARAMS,
        name="merge",
    )(inner, edge, cs, cs1, cornrecv, pick_y, cell_x, values)
    held = lax.all_to_all(pieces.reshape(devices, stride, 1, T), "mem", 0, 0).reshape(devices * stride, T)
    picked = pl.pallas_call(
        functools.partial(select_kernel, members),
        out_shape=sds(pairs, rows, T),
        in_specs=[VM, VM],
        out_specs=VM,
        compiler_params=PARAMS,
        name="select",
    )(lineage, held)
    back = lax.all_to_all(picked.reshape(devices, members // 2, rows, T), "mem", 0, 0)
    resampled, log_weights = pl.pallas_call(
        functools.partial(finish_kernel, members),
        out_shape=(sds(members // 2, devices, rows, T), sds(1, 1, members)),
        in_specs=[VM, VM],
        out_specs=[HB, HB],
        scratch_shapes=[pltpu.VMEM((1, 1, members), F32), pltpu.SemaphoreType.DMA((members // 2 + 1,))],
        compiler_params=PARAMS,
        name="finish",
    )(back, held)
    return (resampled.reshape(fields.shape), log_weights)


def solution(mesh):
    return jax.shard_map(
        shards,
        mesh=mesh,
        in_specs=(
            P("mem", None, "gx", "gy"),
            P("mem", "gx", "gy"),
            P("gx", "gy", None),
            P("gx", "gy", None),
            P("gx", "gy", None),
        ),
        out_specs=(P("mem", None, "gx", "gy"), P("gx", "gy", "mem")),
        check_vma=False,
    )
```

```python
import functools

import jax
import jax.numpy as jnp
from jax import lax
from jax.experimental import pallas as pl
from jax.experimental.pallas import tpu as pltpu
from jax.sharding import PartitionSpec as P

COURANT = 0.3
NOISE_AMP = 0.1
OBS_VAR = 0.25
T = 128
F32 = jnp.float32
CHUNK = 128


def lanes(shape):
    return lax.broadcasted_iota(jnp.int32, shape, len(shape) - 1)


def subl(shape):
    return lax.broadcasted_iota(jnp.int32, shape, len(shape) - 2)


def lroll(a, shift):
    return pltpu.roll(a, shift % T, 1)


def rows_at(ref, lead, start, off, count, total):
    first = start + off
    if first < 0:
        return pltpu.roll(ref[(*lead, pl.ds(0, count))], -first, 0)
    if first + count > total:
        over = first + count - total
        return pltpu.roll(ref[(*lead, pl.ds(total - count, count))], count - over, 0)
    return ref[(*lead, pl.ds(first, count))]


def one_step(ref, lead, start, count, total, force, cor):
    get = lambda f, off: rows_at(ref, (*lead, f), start, off, count, total)
    cen, low, high = [], [], []
    dx, dy, loc, q = [], [], [], []
    for f in range(3):
        a, am, ap = get(f, 0), get(f, -1), get(f, 1)
        far = get(f, -2) + get(f, 2)
        cross = am + ap
        yp, ym = lroll(a, -1), lroll(a, 1)
        cen.append(a)
        low.append(am)
        high.append(ap)
        dx.append(ap - am)
        dy.append(yp - ym)
        loc.append(0.71 * a + (0.09 * cross - 0.005 * far))
        q.append(0.09 * a - (0.01 * cross + 0.005 * (yp + ym)))
    eta, u, v = cen
    half = 0.5 * COURANT
    hv = half * ((1.0 + eta) * v)
    hu = (1.0 + high[0]) * high[1] - (1.0 + low[0]) * low[1]
    new_eta = loc[0] + lroll(q[0] - hv, -1) + lroll(q[0] + hv, 1) - half * hu + NOISE_AMP * force
    tend_u = u * dx[1] + v * dy[1] + dx[0]
    tend_v = u * dx[2] + v * dy[2] + dy[0]
    new_u = loc[1] + (lroll(q[1], -1) + lroll(q[1], 1)) - half * tend_u + (COURANT * cor) * v
    new_v = loc[2] + (lroll(q[2], -1) + lroll(q[2], 1)) - half * tend_v - (COURANT * cor) * u
    return new_eta, new_u, new_v


def coriolis(cols, total_y):
    y = lax.rem(lax.axis_index("gy") * T + cols + total_y, total_y)
    return 0.1 + 0.2 * ((y.astype(F32) + 0.5) / total_y - 0.5)


def pack_kernel(fields_hbm, noise_hbm, fields, noise, rowpack, colpack, ownrow, owncol, sems):
    members = fields.shape[0]
    half = members // 2
    copies = [pltpu.make_async_copy(noise_hbm, noise, sems.at[2])]
    for i in range(2):
        part = slice(i * half, (i + 1) * half)
        copies.append(pltpu.make_async_copy(fields_hbm.at[part], fields.at[part], sems.at[i]))
    for copy in copies:
        copy.start()
    copies[0].wait()
    top = subl((8, T)) < 4
    ln = lanes((T, T)) // 8
    for p in range(members // 2):
        rowpack[3 * members + p] = jnp.where(top, noise[p, 0:8], noise[p, T - 8 : T])
    acc = jnp.zeros((T, T), F32)
    for m in range(members):
        acc = jnp.where(ln == 4 * m + 3, lroll(noise[m // 2], 32 * m + 28), acc)
    for m in range(members):
        if m % half == 0:
            copies[1 + m // half].wait()
        for f in range(3):
            rowpack[3 * m + f] = jnp.where(top, fields[m, f, 0:8], fields[m, f, T - 8 : T])
            acc = jnp.where(ln == 4 * m + f, lroll(fields[m, f], 32 * m + 8 * f + 4), acc)
    colpack[...] = acc

    @pl.when(strips_first())
    def _():
        own_strips(fields, noise, ownrow, owncol)


def strips_first():
    first = (lax.axis_index("gx") != 0) | (lax.axis_index("mem") < lax.axis_size("mem") // 2)
    return first & (lax.axis_index("gy") == 0)


def own_columns(tiles, every=1):
    shape = tiles[0].shape
    ln = lanes(shape) // 8
    acc = jnp.zeros(shape, F32)
    for m in range(0, len(tiles), every):
        a = tiles[m]
        acc = jnp.where(ln == 4 * m, lroll(a, 32 * m + 8), acc)
        acc = jnp.where(ln == 4 * m + 3, lroll(a, 32 * m + 24), acc)
    return acc


def own_strips(fields, noise, ownrow, owncol):
    members = fields.shape[0]
    for f in range(4):
        tiles = [fields[m, f] if f < 3 else noise[m // 2] for m in range(members)]
        for m, a in enumerate(tiles):
            ownrow[f, 2 * m] = a[0:8]
            ownrow[f, 2 * m + 1] = a[T - 8 : T]
        if f < 3:
            owncol[f] = own_columns(tiles)
        else:
            even = own_columns(tiles, 2)
            owncol[f] = even + lroll(even, 32)


def interior(total_y, fields, noise, inner, tmp):
    cor = coriolis(lanes((1, T)), total_y)
    for src, dst in ((fields, tmp), (tmp, inner)):
        for m in range(fields.shape[0]):
            for r in range(0, T, CHUNK):
                new = one_step(src, (m,), r, CHUNK, T, noise[m // 2, r : r + CHUNK], cor)
                for f in range(3):
                    dst[m, f, r : r + CHUNK] = new[f]


def interior_kernel(total_y, fields, noise, ownrow_in, owncol_in, cells_hbm, values_hbm, lineage_hbm,
                    ownrow, owncol, inner, pick_y, cell_x, values, lineage, tmp, cells, sems):
    members = fields.shape[0]
    copies = [
        pltpu.make_async_copy(cells_hbm, cells, sems.at[0]),
        pltpu.make_async_copy(values_hbm, values, sems.at[1]),
        pltpu.make_async_copy(lineage_hbm, lineage, sems.at[2]),
    ]
    for copy in copies:
        copy.start()

    @pl.when(jnp.logical_not(strips_first()))
    def _():
        own_strips(fields, noise, ownrow, owncol)

    interior(total_y, fields, noise, inner, tmp)
    for copy in copies:
        copy.wait()
    cell = cells[...]
    line_y = lax.broadcasted_iota(jnp.int32, pick_y.shape, 0)
    pick_y[...] = jnp.where(line_y == lax.rem(cell, T), 1.0, 0.0).astype(pick_y.dtype)
    cell_x[...] = cell // T


def twice(a, a1, total, cor):
    for src, dst in ((a, a1), (a1, a)):
        new = one_step(src, (), 0, total, total, a[3], cor)
        for f in range(3):
            dst[f, 0:total] = new[f]


def column_masks():
    l32 = lax.rem(lanes((1, T)), 32)
    cols = jnp.where(l32 < 16, l32 + 120, l32 - 24)
    return cols, (l32 >= 20) & (l32 < 24), (l32 >= 8) & (l32 < 12)


def with_halo(own, recv, f, is_low, is_high):
    return jnp.where(is_low, lroll(recv, 20 - 8 * f), jnp.where(is_high, lroll(recv, 4 - 8 * f), own))


def some_rows(src, dst, first, count, cor, force):
    new = one_step(src, (), first, count, T + 16, force[3, first : first + count], cor)
    for f in range(3):
        dst[f, first : first + count] = new[f]


def strips_kernel(total_y, ownrow, rowrecv, owncol, colrecv, edge, cs, cs1, rs, rs1):
    members = ownrow.shape[1] // 2
    cols, is_low, is_high = column_masks()
    halo = lambda m, f: rowrecv[3 * m + f] if f < 3 else rowrecv[3 * members + m // 2]
    for f in range(4):
        for m in range(members):
            rs[f, 32 * m : 32 * m + 8] = halo(m, f)
            rs[f, 32 * m + 8 : 32 * m + 16] = ownrow[f, 2 * m]
            rs[f, 32 * m + 16 : 32 * m + 24] = ownrow[f, 2 * m + 1]
            rs[f, 32 * m + 24 : 32 * m + 32] = halo(m, f)
        cs[f, 0:8] = own_columns([halo(m, f) for m in range(members)])
        cs[f, 8 : T + 8] = with_halo(owncol[f], colrecv[...], f, is_low, is_high)
    some_rows(cs, cs1, 16, T - 16, coriolis(cols, total_y), cs)
    twice(rs, rs1, T, coriolis(lanes((1, T)), total_y))
    for f in range(3):
        for m in range(members):
            edge[f, 2 * m] = rs[f, 32 * m + 8 : 32 * m + 16]
            edge[f, 2 * m + 1] = rs[f, 32 * m + 16 : 32 * m + 24]


def merge_kernel(total_y, devices, inner, edge, cs_in, cs1_in, cornrecv, pick_y, cell_x, values, cs, cs1, out, eta_s):
    members = inner.shape[0]
    cols, is_low, is_high = column_masks()
    cor_col = coriolis(cols, total_y)
    corn = jnp.where(subl((8, T)) < 4, cornrecv[0:8], cornrecv[T - 8 : T])
    for f in range(4):
        ends = with_halo(cs[f, 0:8], corn, f, is_low, is_high)
        cs[f, 0:8] = ends
        cs[f, T + 8 : T + 16] = ends
    some_rows(cs, cs1, 0, 16, cor_col, cs)
    some_rows(cs, cs1, T, 16, cor_col, cs)
    some_rows(cs1, cs, 8, T, cor_col, cs)

    per = 96 // devices
    stride = members // 2 * 8 * per + 1
    top = subl((8, T)) < 4
    left = lanes((8, T)) < 4
    right = lanes((8, T)) >= T - 4
    for m in range(members):
        p, mm = m // 2, m % 2
        for f in range(3):
            for t in range(T // 8):
                a = inner[m, f, 8 * t : 8 * t + 8]
                if t == 0:
                    a = jnp.where(top, edge[f, 2 * m], a)
                if t == T // 8 - 1:
                    a = jnp.where(top, a, edge[f, 2 * m + 1])
                col = cs[f, 8 * t + 8 : 8 * t + 16]
                a = jnp.where(left, lroll(col, 104 - 32 * m), a)
                a = jnp.where(right, lroll(col, 120 - 32 * m), a)
                k = mm * 48 + f * 16 + t
                first = (k // per) * stride + p * 8 * per + 8 * (k % per)
                out[first : first + 8] = a
                if f == 0:
                    eta_s[m * T + 8 * t : m * T + 8 * t + 8] = a

    eta = eta_s[...]
    hi = eta.astype(jnp.bfloat16)
    rest = eta - hi.astype(F32)
    mid = rest.astype(jnp.bfloat16)
    low = (rest - mid.astype(F32)).astype(jnp.bfloat16)
    dot = lambda part: jnp.dot(part, pick_y[...], preferred_element_type=F32)
    seen = dot(hi) + (dot(mid) + dot(low))
    pick_x = lax.broadcasted_iota(jnp.int32, pick_y.shape, 0) == cell_x[...]
    logw = jnp.zeros((1, T), F32)
    for m in range(members):
        at = jnp.sum(jnp.where(pick_x, seen[m * T : (m + 1) * T], 0.0), axis=0, keepdims=True)
        miss = at - values[...]
        total = jnp.sum(miss * miss, axis=1, keepdims=True)
        logw = jnp.where(lanes((1, T)) == m, -0.5 * total / OBS_VAR, logw)
    for j in range(devices):
        out[(j + 1) * stride - 1 : (j + 1) * stride] = logw


def select_kernel(members, lineage, recv, out):
    pairs, rows = out.shape[0], out.shape[1]
    per = members // 2
    for k in range(pairs):
        pair = lineage[0, k]
        out[k] = recv[pl.ds(lax.div(pair, per) * (per * rows + 1) + lax.rem(pair, per) * rows, rows)]


def finish_kernel(members, back, recv, out, log_weights, result, sems):
    devices = back.shape[0]
    copies = [pltpu.make_async_copy(back.at[:, p], out.at[p], sems.at[p]) for p in range(members // 2)]
    for copy in copies:
        copy.start()
    stride = recv.shape[0] // devices
    logw = recv[pl.ds(stride - 1, devices, stride)]
    logw = jnp.where(lanes(logw.shape) < members, logw, -jnp.inf)
    peak = jnp.max(jnp.max(logw, axis=1, keepdims=True), axis=0, keepdims=True)
    total = jnp.sum(jnp.sum(jnp.exp(logw - peak), axis=1, keepdims=True), axis=0, keepdims=True)
    own = recv[pl.ds(lax.axis_index("mem") * stride + stride - 1, 1)]
    result[0] = (own - peak - jnp.log(total))[:, :members]
    last = pltpu.make_async_copy(result, log_weights, sems.at[members // 2])
    last.start()
    for copy in copies:
        copy.wait()
    last.wait()


VM = pl.BlockSpec(memory_space=pltpu.VMEM)
HB = pl.BlockSpec(memory_space=pltpu.MemorySpace.HBM)
PARAMS = pltpu.CompilerParams(vmem_limit_bytes=24 << 20)


def in_hbm(a):
    return pltpu.with_memory_space_constraint(a, pltpu.MemorySpace.HBM)


def sds(*shape):
    return jax.ShapeDtypeStruct(shape, F32)


def shards(fields, noise, ancestors, obs_cells, obs_values):
    members = fields.shape[0]
    devices = lax.axis_size("mem")
    total_y = T * lax.axis_size("gy")
    fields_vm, noise_vm, rowpack, colpack, ownrow, owncol = pl.pallas_call(
        pack_kernel,
        out_shape=(
            sds(*fields.shape),
            sds(*noise.shape),
            sds(3 * members + members // 2, 8, T),
            sds(T, T),
            sds(4, 2 * members, 8, T),
            sds(4, T, T),
        ),
        in_specs=[HB] * 2,
        out_specs=[VM] * 6,
        scratch_shapes=[pltpu.SemaphoreType.DMA((3,))],
        compiler_params=PARAMS,
        name="pack",
    )(in_hbm(fields), in_hbm(noise))
    swap = [(0, 1), (1, 0)]
    colrecv = lax.ppermute(colpack, "gy", swap)
    rowrecv = lax.ppermute(rowpack, "gx", swap)
    count, pairs = obs_cells.shape[-1], ancestors.shape[-1]
    ownrow, owncol, inner, pick_y, cell_x, values, lineage = pl.pallas_call(
        functools.partial(interior_kernel, total_y),
        out_shape=(
            sds(4, 2 * members, 8, T),
            sds(4, T, T),
            sds(members, 3, T, T),
            jax.ShapeDtypeStruct((T, count), jnp.bfloat16),
            jax.ShapeDtypeStruct((1, count), jnp.int32),
            sds(1, count),
            jax.ShapeDtypeStruct((1, pairs), jnp.int32),
        ),
        in_specs=[VM] * 4 + [HB] * 3,
        out_specs=[VM] * 7,
        input_output_aliases={2: 0, 3: 1},
        scratch_shapes=[
            pltpu.VMEM((members, 3, T, T), F32),
            pltpu.VMEM((1, count), jnp.int32),
            pltpu.SemaphoreType.DMA((3,)),
        ],
        compiler_params=PARAMS,
        cost_estimate=pl.CostEstimate(flops=50_000_000, bytes_accessed=2_500_000, transcendentals=0),
        name="interior",
    )(
        fields_vm,
        noise_vm,
        ownrow,
        owncol,
        in_hbm(obs_cells.reshape(1, -1)),
        in_hbm(obs_values.reshape(1, -1)),
        in_hbm(ancestors.reshape(1, -1)),
    )
    colrecv, rowrecv, inner = lax.optimization_barrier((colrecv, rowrecv, inner))
    cornrecv = lax.ppermute(colrecv, "gx", swap)
    edge, cs, cs1 = pl.pallas_call(
        functools.partial(strips_kernel, total_y),
        out_shape=(sds(3, 2 * members, 8, T), sds(4, T + 16, T), sds(3, T + 16, T)),
        in_specs=[VM] * 4,
        out_specs=[VM] * 3,
        scratch_shapes=[pltpu.VMEM((4, T, T), F32), pltpu.VMEM((3, T, T), F32)],
        compiler_params=PARAMS,
        cost_estimate=pl.CostEstimate(flops=18_000_000, bytes_accessed=700_000, transcendentals=0),
        name="strips",
    )(ownrow, rowrecv, owncol, colrecv)
    rows = 768 // devices
    stride = members // 2 * rows + 1
    _, _, pieces = pl.pallas_call(
        functools.partial(merge_kernel, total_y, devices),
        out_shape=(sds(4, T + 16, T), sds(3, T + 16, T), sds(devices * stride, T)),
        in_specs=[VM] * 8,
        out_specs=[VM] * 3,
        input_output_aliases={2: 0, 3: 1},
        scratch_shapes=[pltpu.VMEM((members * T, T), F32)],
        compiler_params=PARAMS,
        name="merge",
    )(inner, edge, cs, cs1, cornrecv, pick_y, cell_x, values)
    held = lax.all_to_all(pieces.reshape(devices, stride, 1, T), "mem", 0, 0).reshape(devices * stride, T)
    picked = pl.pallas_call(
        functools.partial(select_kernel, members),
        out_shape=sds(pairs, rows, T),
        in_specs=[VM, VM],
        out_specs=VM,
        compiler_params=PARAMS,
        name="select",
    )(lineage, held)
    back = lax.all_to_all(picked.reshape(devices, members // 2, rows, T), "mem", 0, 0)
    resampled, log_weights = pl.pallas_call(
        functools.partial(finish_kernel, members),
        out_shape=(sds(members // 2, devices, rows, T), sds(1, 1, members)),
        in_specs=[VM, VM],
        out_specs=[HB, HB],
        scratch_shapes=[pltpu.VMEM((1, 1, members), F32), pltpu.SemaphoreType.DMA((members // 2 + 1,))],
        compiler_params=PARAMS,
        name="finish",
    )(back, held)
    return (resampled.reshape(fields.shape), log_weights)


def solution(mesh):
    return jax.shard_map(
        shards,
        mesh=mesh,
        in_specs=(
            P("mem", None, "gx", "gy"),
            P("mem", "gx", "gy"),
            P("gx", "gy", None),
            P("gx", "gy", None),
            P("gx", "gy", None),
        ),
        out_specs=(P("mem", None, "gx", "gy"), P("gx", "gy", "mem")),
        check_vma=False,
    )
```

```python
import functools

import jax
import jax.numpy as jnp
from jax import lax
from jax.experimental import pallas as pl
from jax.experimental.pallas import tpu as pltpu
from jax.sharding import PartitionSpec as P

COURANT = 0.3
NOISE_AMP = 0.1
OBS_VAR = 0.25
T = 128
F32 = jnp.float32
CHUNK = 128


def lanes(shape):
    return lax.broadcasted_iota(jnp.int32, shape, len(shape) - 1)


def subl(shape):
    return lax.broadcasted_iota(jnp.int32, shape, len(shape) - 2)


def lroll(a, shift):
    return pltpu.roll(a, shift % T, 1)


def rows_at(ref, lead, start, off, count, total):
    first = start + off
    if first < 0:
        return pltpu.roll(ref[(*lead, pl.ds(0, count))], -first, 0)
    if first + count > total:
        over = first + count - total
        return pltpu.roll(ref[(*lead, pl.ds(total - count, count))], count - over, 0)
    return ref[(*lead, pl.ds(first, count))]


def one_step(ref, lead, start, count, total, force, cor):
    get = lambda f, off: rows_at(ref, (*lead, f), start, off, count, total)
    cen, low, high = [], [], []
    dx, dy, loc, q = [], [], [], []
    for f in range(3):
        a, am, ap = get(f, 0), get(f, -1), get(f, 1)
        far = get(f, -2) + get(f, 2)
        cross = am + ap
        yp, ym = lroll(a, -1), lroll(a, 1)
        cen.append(a)
        low.append(am)
        high.append(ap)
        dx.append(ap - am)
        dy.append(yp - ym)
        loc.append(0.71 * a + (0.09 * cross - 0.005 * far))
        q.append(0.09 * a - (0.01 * cross + 0.005 * (yp + ym)))
    eta, u, v = cen
    half = 0.5 * COURANT
    hv = half * ((1.0 + eta) * v)
    hu = (1.0 + high[0]) * high[1] - (1.0 + low[0]) * low[1]
    new_eta = loc[0] + lroll(q[0] - hv, -1) + lroll(q[0] + hv, 1) - half * hu + NOISE_AMP * force
    tend_u = u * dx[1] + v * dy[1] + dx[0]
    tend_v = u * dx[2] + v * dy[2] + dy[0]
    new_u = loc[1] + (lroll(q[1], -1) + lroll(q[1], 1)) - half * tend_u + (COURANT * cor) * v
    new_v = loc[2] + (lroll(q[2], -1) + lroll(q[2], 1)) - half * tend_v - (COURANT * cor) * u
    return new_eta, new_u, new_v


def coriolis(cols, total_y):
    y = lax.rem(lax.axis_index("gy") * T + cols + total_y, total_y)
    return 0.1 + 0.2 * ((y.astype(F32) + 0.5) / total_y - 0.5)


def pack_kernel(fields_hbm, noise_hbm, fields, noise, rowpack, colpack, ownrow, owncol, sems):
    members = fields.shape[0]
    half = members // 2
    copies = [pltpu.make_async_copy(noise_hbm, noise, sems.at[2])]
    for i in range(2):
        part = slice(i * half, (i + 1) * half)
        copies.append(pltpu.make_async_copy(fields_hbm.at[part], fields.at[part], sems.at[i]))
    for copy in copies:
        copy.start()
    copies[0].wait()
    top = subl((8, T)) < 4
    ln = lanes((T, T)) // 8
    for p in range(members // 2):
        rowpack[3 * members + p] = jnp.where(top, noise[p, 0:8], noise[p, T - 8 : T])
    acc = jnp.zeros((T, T), F32)
    for m in range(members):
        acc = jnp.where(ln == 4 * m + 3, lroll(noise[m // 2], 32 * m + 28), acc)
    for m in range(members):
        if m % half == 0:
            copies[1 + m // half].wait()
        for f in range(3):
            rowpack[3 * m + f] = jnp.where(top, fields[m, f, 0:8], fields[m, f, T - 8 : T])
            acc = jnp.where(ln == 4 * m + f, lroll(fields[m, f], 32 * m + 8 * f + 4), acc)
    colpack[...] = acc

    @pl.when(strips_first())
    def _():
        own_strips(fields, noise, ownrow, owncol)


def strips_first():
    first = (lax.axis_index("gx") != 0) | (lax.axis_index("mem") < lax.axis_size("mem") // 2)
    return first & (lax.axis_index("gy") == 0)


def own_columns(tiles, every=1):
    shape = tiles[0].shape
    ln = lanes(shape) // 8
    acc = jnp.zeros(shape, F32)
    for m in range(0, len(tiles), every):
        a = tiles[m]
        acc = jnp.where(ln == 4 * m, lroll(a, 32 * m + 8), acc)
        acc = jnp.where(ln == 4 * m + 3, lroll(a, 32 * m + 24), acc)
    return acc


def own_tall(tiles, every=1):
    lane = lanes((T, T))
    acc = jnp.zeros((T, T), F32)
    for m in range(0, len(tiles), every):
        acc = jnp.where(lane // 32 == m, lroll(tiles[m], 32 * m + 24), acc)
    return jnp.where(lane % 32 < 8, lroll(acc, -16), acc)


def own_strips(fields, noise, ownrow, owncol):
    members = fields.shape[0]
    for f in range(4):
        tiles = [fields[m, f] if f < 3 else noise[m // 2] for m in range(members)]
        for m, a in enumerate(tiles):
            ownrow[f, 2 * m] = a[0:8]
            ownrow[f, 2 * m + 1] = a[T - 8 : T]
        if f < 3:
            owncol[f] = own_tall(tiles)
        else:
            even = own_tall(tiles, 2)
            owncol[f] = even + lroll(even, 32)


def interior(total_y, fields, noise, inner, tmp):
    cor = coriolis(lanes((1, T)), total_y)
    for src, dst in ((fields, tmp), (tmp, inner)):
        for m in range(fields.shape[0]):
            for r in range(0, T, CHUNK):
                new = one_step(src, (m,), r, CHUNK, T, noise[m // 2, r : r + CHUNK], cor)
                for f in range(3):
                    dst[m, f, r : r + CHUNK] = new[f]


def interior_kernel(total_y, fields, noise, ownrow_in, owncol_in, cells_hbm, values_hbm, lineage_hbm,
                    ownrow, owncol, inner, pick_y, cell_x, values, lineage, tmp, cells, sems):
    members = fields.shape[0]
    copies = [
        pltpu.make_async_copy(cells_hbm, cells, sems.at[0]),
        pltpu.make_async_copy(values_hbm, values, sems.at[1]),
        pltpu.make_async_copy(lineage_hbm, lineage, sems.at[2]),
    ]
    for copy in copies:
        copy.start()

    @pl.when(jnp.logical_not(strips_first()))
    def _():
        own_strips(fields, noise, ownrow, owncol)

    interior(total_y, fields, noise, inner, tmp)
    for copy in copies:
        copy.wait()
    cell = cells[...]
    line_y = lax.broadcasted_iota(jnp.int32, pick_y.shape, 0)
    pick_y[...] = jnp.where(line_y == lax.rem(cell, T), 1.0, 0.0).astype(pick_y.dtype)
    cell_x[...] = cell // T


def twice(a, a1, total, cor):
    for src, dst in ((a, a1), (a1, a)):
        new = one_step(src, (), 0, total, total, a[3], cor)
        for f in range(3):
            dst[f, 0:total] = new[f]


def column_masks():
    l32 = lax.rem(lanes((1, T)), 32)
    cols = jnp.where(l32 < 16, l32 + 120, l32 - 24)
    return cols, (l32 >= 20) & (l32 < 24), (l32 >= 8) & (l32 < 12)


def with_halo(own, recv, f, is_low, is_high):
    return jnp.where(is_low, lroll(recv, 20 - 8 * f), jnp.where(is_high, lroll(recv, 4 - 8 * f), own))


def some_rows(src, dst, first, count, cor, force):
    new = one_step(src, (), first, count, T + 16, force[3, first : first + count], cor)
    for f in range(3):
        dst[f, first : first + count] = new[f]


def strips_kernel(total_y, ownrow, rowrecv, owncol, colrecv, edge, cs, cs1, rs, rs1):
    members = ownrow.shape[1] // 2
    cols, is_low, is_high = column_masks()
    halo = lambda m, f: rowrecv[3 * m + f] if f < 3 else rowrecv[3 * members + m // 2]
    for f in range(4):
        for m in range(members):
            rs[f, 32 * m : 32 * m + 8] = halo(m, f)
            rs[f, 32 * m + 8 : 32 * m + 16] = ownrow[f, 2 * m]
            rs[f, 32 * m + 16 : 32 * m + 24] = ownrow[f, 2 * m + 1]
            rs[f, 32 * m + 24 : 32 * m + 32] = halo(m, f)
        cs[f, 0:8] = own_columns([halo(m, f) for m in range(members)])
        cs[f, 8 : T + 8] = with_halo(owncol[f], colrecv[...], f, is_low, is_high)
    some_rows(cs, cs1, 16, T - 16, coriolis(cols, total_y), cs)
    twice(rs, rs1, T, coriolis(lanes((1, T)), total_y))
    for f in range(3):
        for m in range(members):
            edge[f, 2 * m] = rs[f, 32 * m + 8 : 32 * m + 16]
            edge[f, 2 * m + 1] = rs[f, 32 * m + 16 : 32 * m + 24]


def merge_kernel(total_y, devices, inner, edge, cs_in, cs1_in, cornrecv, pick_y, cell_x, values, cs, cs1, out, eta_s):
    members = inner.shape[0]
    cols, is_low, is_high = column_masks()
    cor_col = coriolis(cols, total_y)
    corn = jnp.where(subl((8, T)) < 4, cornrecv[0:8], cornrecv[T - 8 : T])
    for f in range(4):
        ends = with_halo(cs[f, 0:8], corn, f, is_low, is_high)
        cs[f, 0:8] = ends
        cs[f, T + 8 : T + 16] = ends
    some_rows(cs, cs1, 0, 16, cor_col, cs)
    some_rows(cs, cs1, T, 16, cor_col, cs)
    some_rows(cs1, cs, 8, T, cor_col, cs)

    per = 96 // devices
    stride = members // 2 * 8 * per + 1
    top = subl((8, T)) < 4
    left = lanes((8, T)) < 4
    right = lanes((8, T)) >= T - 4
    for m in range(members):
        p, mm = m // 2, m % 2
        for f in range(3):
            for t in range(T // 8):
                a = inner[m, f, 8 * t : 8 * t + 8]
                if t == 0:
                    a = jnp.where(top, edge[f, 2 * m], a)
                if t == T // 8 - 1:
                    a = jnp.where(top, a, edge[f, 2 * m + 1])
                col = cs[f, 8 * t + 8 : 8 * t + 16]
                a = jnp.where(left, lroll(col, 104 - 32 * m), a)
                a = jnp.where(right, lroll(col, 120 - 32 * m), a)
                k = mm * 48 + f * 16 + t
                first = (k // per) * stride + p * 8 * per + 8 * (k % per)
                out[first : first + 8] = a
                if f == 0:
                    eta_s[m * T + 8 * t : m * T + 8 * t + 8] = a

    eta = eta_s[...]
    hi = eta.astype(jnp.bfloat16)
    rest = eta - hi.astype(F32)
    mid = rest.astype(jnp.bfloat16)
    low = (rest - mid.astype(F32)).astype(jnp.bfloat16)
    dot = lambda part: jnp.dot(part, pick_y[...], preferred_element_type=F32)
    seen = dot(hi) + (dot(mid) + dot(low))
    pick_x = lax.broadcasted_iota(jnp.int32, pick_y.shape, 0) == cell_x[...]
    logw = jnp.zeros((1, T), F32)
    for m in range(members):
        at = jnp.sum(jnp.where(pick_x, seen[m * T : (m + 1) * T], 0.0), axis=0, keepdims=True)
        miss = at - values[...]
        total = jnp.sum(miss * miss, axis=1, keepdims=True)
        logw = jnp.where(lanes((1, T)) == m, -0.5 * total / OBS_VAR, logw)
    for j in range(devices):
        out[(j + 1) * stride - 1 : (j + 1) * stride] = logw


def select_kernel(members, lineage, recv, out):
    pairs, rows = out.shape[0], out.shape[1]
    per = members // 2
    for k in range(pairs):
        pair = lineage[0, k]
        out[k] = recv[pl.ds(lax.div(pair, per) * (per * rows + 1) + lax.rem(pair, per) * rows, rows)]


def finish_kernel(members, back, recv, out, log_weights, result, sems):
    devices = back.shape[0]
    copies = [pltpu.make_async_copy(back.at[:, p], out.at[p], sems.at[p]) for p in range(members // 2)]
    for copy in copies:
        copy.start()
    stride = recv.shape[0] // devices
    logw = recv[pl.ds(stride - 1, devices, stride)]
    logw = jnp.where(lanes(logw.shape) < members, logw, -jnp.inf)
    peak = jnp.max(jnp.max(logw, axis=1, keepdims=True), axis=0, keepdims=True)
    total = jnp.sum(jnp.sum(jnp.exp(logw - peak), axis=1, keepdims=True), axis=0, keepdims=True)
    own = recv[pl.ds(lax.axis_index("mem") * stride + stride - 1, 1)]
    result[0] = (own - peak - jnp.log(total))[:, :members]
    last = pltpu.make_async_copy(result, log_weights, sems.at[members // 2])
    last.start()
    for copy in copies:
        copy.wait()
    last.wait()


VM = pl.BlockSpec(memory_space=pltpu.VMEM)
HB = pl.BlockSpec(memory_space=pltpu.MemorySpace.HBM)
PARAMS = pltpu.CompilerParams(vmem_limit_bytes=24 << 20)


def in_hbm(a):
    return pltpu.with_memory_space_constraint(a, pltpu.MemorySpace.HBM)


def sds(*shape):
    return jax.ShapeDtypeStruct(shape, F32)


def shards(fields, noise, ancestors, obs_cells, obs_values):
    members = fields.shape[0]
    devices = lax.axis_size("mem")
    total_y = T * lax.axis_size("gy")
    fields_vm, noise_vm, rowpack, colpack, ownrow, owncol = pl.pallas_call(
        pack_kernel,
        out_shape=(
            sds(*fields.shape),
            sds(*noise.shape),
            sds(3 * members + members // 2, 8, T),
            sds(T, T),
            sds(4, 2 * members, 8, T),
            sds(4, T, T),
        ),
        in_specs=[HB] * 2,
        out_specs=[VM] * 6,
        scratch_shapes=[pltpu.SemaphoreType.DMA((3,))],
        compiler_params=PARAMS,
        name="pack",
    )(in_hbm(fields), in_hbm(noise))
    swap = [(0, 1), (1, 0)]
    colrecv = lax.ppermute(colpack, "gy", swap)
    rowrecv = lax.ppermute(rowpack, "gx", swap)
    count, pairs = obs_cells.shape[-1], ancestors.shape[-1]
    ownrow, owncol, inner, pick_y, cell_x, values, lineage = pl.pallas_call(
        functools.partial(interior_kernel, total_y),
        out_shape=(
            sds(4, 2 * members, 8, T),
            sds(4, T, T),
            sds(members, 3, T, T),
            jax.ShapeDtypeStruct((T, count), jnp.bfloat16),
            jax.ShapeDtypeStruct((1, count), jnp.int32),
            sds(1, count),
            jax.ShapeDtypeStruct((1, pairs), jnp.int32),
        ),
        in_specs=[VM] * 4 + [HB] * 3,
        out_specs=[VM] * 7,
        input_output_aliases={2: 0, 3: 1},
        scratch_shapes=[
            pltpu.VMEM((members, 3, T, T), F32),
            pltpu.VMEM((1, count), jnp.int32),
            pltpu.SemaphoreType.DMA((3,)),
        ],
        compiler_params=PARAMS,
        cost_estimate=pl.CostEstimate(flops=50_000_000, bytes_accessed=2_500_000, transcendentals=0),
        name="interior",
    )(
        fields_vm,
        noise_vm,
        ownrow,
        owncol,
        in_hbm(obs_cells.reshape(1, -1)),
        in_hbm(obs_values.reshape(1, -1)),
        in_hbm(ancestors.reshape(1, -1)),
    )
    colrecv, rowrecv, inner = lax.optimization_barrier((colrecv, rowrecv, inner))
    cornrecv = lax.ppermute(colrecv, "gx", swap)
    edge, cs, cs1 = pl.pallas_call(
        functools.partial(strips_kernel, total_y),
        out_shape=(sds(3, 2 * members, 8, T), sds(4, T + 16, T), sds(3, T + 16, T)),
        in_specs=[VM] * 4,
        out_specs=[VM] * 3,
        scratch_shapes=[pltpu.VMEM((4, T, T), F32), pltpu.VMEM((3, T, T), F32)],
        compiler_params=PARAMS,
        cost_estimate=pl.CostEstimate(flops=18_000_000, bytes_accessed=700_000, transcendentals=0),
        name="strips",
    )(ownrow, rowrecv, owncol, colrecv)
    rows = 768 // devices
    stride = members // 2 * rows + 1
    _, _, pieces = pl.pallas_call(
        functools.partial(merge_kernel, total_y, devices),
        out_shape=(sds(4, T + 16, T), sds(3, T + 16, T), sds(devices * stride, T)),
        in_specs=[VM] * 8,
        out_specs=[VM] * 3,
        input_output_aliases={2: 0, 3: 1},
        scratch_shapes=[pltpu.VMEM((members * T, T), F32)],
        compiler_params=PARAMS,
        name="merge",
    )(inner, edge, cs, cs1, cornrecv, pick_y, cell_x, values)
    held = lax.all_to_all(pieces.reshape(devices, stride, 1, T), "mem", 0, 0).reshape(devices * stride, T)
    picked = pl.pallas_call(
        functools.partial(select_kernel, members),
        out_shape=sds(pairs, rows, T),
        in_specs=[VM, VM],
        out_specs=VM,
        compiler_params=PARAMS,
        name="select",
    )(lineage, held)
    back = lax.all_to_all(picked.reshape(devices, members // 2, rows, T), "mem", 0, 0)
    resampled, log_weights = pl.pallas_call(
        functools.partial(finish_kernel, members),
        out_shape=(sds(members // 2, devices, rows, T), sds(1, 1, members)),
        in_specs=[VM, VM],
        out_specs=[HB, HB],
        scratch_shapes=[pltpu.VMEM((1, 1, members), F32), pltpu.SemaphoreType.DMA((members // 2 + 1,))],
        compiler_params=PARAMS,
        name="finish",
    )(back, held)
    return (resampled.reshape(fields.shape), log_weights)


def solution(mesh):
    return jax.shard_map(
        shards,
        mesh=mesh,
        in_specs=(
            P("mem", None, "gx", "gy"),
            P("mem", "gx", "gy"),
            P("gx", "gy", None),
            P("gx", "gy", None),
            P("gx", "gy", None),
        ),
        out_specs=(P("mem", None, "gx", "gy"), P("gx", "gy", "mem")),
        check_vma=False,
    )
```
